256 devices in a mesh: gx: 8 (over y, core), gy: 32 (over z, x).
Axes of the slice: x: 4, y: 4, z: 8, core: 2. Of those that a mesh axis runs over, the one named last changes fastest.
Arguments:
- volume: bfloat16 [64, 512, 2048], P('gx', 'gy'), may hold values from -6 to 6
- cotangent: bfloat16 [64, 512, 2048], P('gx', 'gy'), may hold values from -6 to 6
- weight: bfloat16 [3, 3, 3, 32, 32], replicated, may hold values from -0.21875 to 0.21875
- bias: float32 [32], replicated, may hold values from -4 to 4
Outputs:
- data_grad: bfloat16 [64, 512, 2048], P('gx', 'gy')
- filter_grad: float32 [3, 3, 3, 32, 32], replicated
- bias_grad: float32 [32], replicated
The draws below stay inside these ranges and needn't reach their ends.
All inputs are finite; a program needn't handle non-finite values.
Results may differ from the reference program's by a relative error of at most 0.008.
Values may be sent and summed in bfloat16 or wider, within the bound.
A program may use at most 128 MiB of HBM per device.

```python
import math
import jax
import jax.numpy as jnp
from jax import lax

C = 32
CX = 8
NZ = 64
NX = 64
NY = 512


def levels(key, shape, split, smallest, high):
    factor_of = 1.0
    for axis_at, shards_of in split:
        draws = jax.random.uniform(jax.random.fold_in(jax.random.fold_in(key, 6), axis_at), (shards_of,), jnp.float32, smallest / len(split), high / len(split))
        factor_of = factor_of * jnp.repeat(jnp.exp(draws), shape[axis_at] // shards_of).reshape((-1,) + (1,) * (len(shape) - 1 - axis_at))
    return factor_of


def scatter_about(key, extent, spread, most, shards=(), kind=jnp.bfloat16):
    result = jax.random.normal(key, extent, jnp.float32) * spread
    if len(shards) > 0:
        result = levels(key, extent, shards, -0.22, 0.18) * result
    return jnp.clip(result, min=-most, max=most).astype(kind)


def setup_inputs(seed: int = 0) -> dict:
    key_list = jax.random.split(jax.random.key(seed), 5)
    return {
        "volume": scatter_about(key_list[0], (NX, NY, C * NZ), 1.0, 6.0, ((0, 8), (1, 32))),
        "cotangent": scatter_about(key_list[1], (NX, NY, C * NZ), 1.0, 6.0, ((0, 8), (1, 32))),
        "weight": scatter_about(key_list[2], (3, 3, 3, C, C), (27 * C) ** -0.5, 0.21875),
        "bias": scatter_about(key_list[3], (C,), 1.0, 4.0, (), jnp.float32),
    }


def forward_pre(block, weight, bias):
    out = lax.conv_general_dilated(block[None], weight, (1, 1, 1), ((0, 0), (0, 0), (1, 1)), dimension_numbers=('NDHCW', 'DHWIO', 'NDHCW'), preferred_element_type=jnp.float32)[0]
    return out + bias[:, None]

def activation_grad(pre, grad_out):
    sig = jax.nn.sigmoid(pre)
    return (grad_out.astype(jnp.float32) * sig * (1.0 + pre * (1.0 - sig))).astype(jnp.bfloat16)

def input_grad(grad_pre, weight):
    flipped = weight[::-1, ::-1, ::-1]
    out = lax.conv_general_dilated(grad_pre[None], flipped, (1, 1, 1), ((0, 0), (0, 0), (1, 1)), dimension_numbers=('NDHCW', 'DHWOI', 'NDHCW'), preferred_element_type=jnp.float32)[0]
    return out.astype(jnp.bfloat16)

def weight_grad(inputs, grad_pre):
    padded = jnp.pad(inputs, ((0, 0), (0, 0), (0, 0), (1, 1)))
    return lax.conv_general_dilated(padded[None], grad_pre[None], (1, 1, 1), ((0, 0), (0, 0), (0, 0)), dimension_numbers=('CDHNW', 'IDHOW', 'DHWNC'), preferred_element_type=jnp.float32)

def reference(volume, cotangent, weight, bias):
    field = volume.reshape(NX, NY, C, NZ)
    grads = cotangent.reshape(NX, NY, C, NZ)
    field_pad = jnp.pad(field, ((2, 2), (2, 2), (0, 0), (0, 0)))
    grads_pad = jnp.pad(grads, ((1, 1), (1, 1), (0, 0), (0, 0)))

    def one_block(index):
        start = (index * CX).astype(jnp.int32)
        xblock = lax.dynamic_slice_in_dim(field_pad, start, CX + 4, 0)
        gblock = lax.dynamic_slice_in_dim(grads_pad, start, CX + 2, 0)
        pre = forward_pre(xblock, weight, bias)
        grad_pre = activation_grad(pre, gblock)
        dx = input_grad(grad_pre, weight)
        own = grad_pre[1:-1, 1:-1]
        dw = weight_grad(xblock[1:-1, 1:-1], own)
        db = lax.optimization_barrier(jnp.sum(own.astype(jnp.float32), axis=(0, 1, 3)))
        return (dx, dw, db)
    dxs, dws, dbs = lax.map(one_block, jnp.arange(NX // CX, dtype=jnp.int32))
    scale = 1.0 / math.sqrt(NX * NY * NZ)
    data_grad = dxs.reshape(NX, NY, C * NZ)
    return (data_grad, lax.optimization_barrier(jnp.sum(dws, axis=0)) * scale, lax.optimization_barrier(jnp.sum(dbs, axis=0)) * scale)
```

```python
import functools
import math

import jax
import jax.numpy as jnp
from jax import lax
from jax.experimental import pallas as pl
from jax.experimental.pallas import tpu as pltpu
from jax.sharding import PartitionSpec as P

C = 32
MESH = pl.DeviceIdType.MESH
BF = jnp.bfloat16
F32 = jnp.float32
X_CHIPS = 4
Z_CHIPS = 8
NT = (((1,), (1,)), ((), ()))


def halves(low, high, mask):
    return jnp.where(mask, low, high)


def shifted(block, amount, keep):
    return jnp.where(keep, pltpu.roll(block, amount, axis=1), jnp.zeros_like(block))


def kernel(scale, comm, vol, cot, wc, bias, dx, df, db, nv, nc, s, c, gp, t1, t2, dq,
           part, part16, rs, xs, zs, fin, ssem, rsem):
    if comm:
        gx = lax.axis_index("gx")
        gy = lax.axis_index("gy")
        ngx = lax.axis_size("gx")
        ngy = lax.axis_size("gy")
        xi = lax.rem(gy, X_CHIPS)
        zi = lax.div(gy, X_CHIPS)

        def at(ax, ay):
            return {"gx": lax.rem(ax + ngx, ngx), "gy": lax.rem(ay + ngy, ngy)}

        diag = [(dx_, dy_) for dx_ in (-1, 1) for dy_ in (-1, 1)]
        gx_peers = [at(gx + k, gy) for k in range(1, 8)]
        x_peers = [at(gx, zi * X_CHIPS + lax.rem(xi + k, X_CHIPS)) for k in range(1, X_CHIPS)]
        z_peers = [at(gx, lax.rem(zi + k, Z_CHIPS) * X_CHIPS + xi) for k in range(1, Z_CHIPS)]
        peers = gx_peers + x_peers + z_peers + [at(gx, gy - 1), at(gx, gy + 1)]
        peers += [at(gx + a, gy + b) for a, b in diag]
        barrier = pltpu.get_barrier_semaphore()
        for peer in peers:
            pl.semaphore_signal(barrier, inc=1, device_id=peer, device_id_type=MESH)

    lane = lax.broadcasted_iota(jnp.int32, (1, 128), 1)
    low = lane < 64
    z_first = (lane % 64) != 0
    z_last = (lane % 64) != 63
    row = lax.broadcasted_iota(jnp.int32, (256, 256), 0)
    col = lax.broadcasted_iota(jnp.int32, (256, 256), 1)
    perm = jnp.where(col == (row % 16) * 16 + row // 16, 1.0, 0.0).astype(BF)

    def turn(src, dst, first, offset):
        for x in range(0, 8, 2):
            parts = [
                jnp.concatenate([src[x + e, :, g * 128:(g + 1) * 128] for g in range(16)], axis=0)
                for e in range(2)
            ]
            out = jnp.dot(perm, jnp.concatenate(parts, axis=1), preferred_element_type=F32).astype(BF)
            dst[first + x, offset:offset + 256] = out[:, :128]
            dst[first + x + 1, offset:offset + 256] = out[:, 128:]

    turn(vol, nv, 2, 32)
    turn(cot, nc, 1, 16)

    copies = []

    def send(index, src, dst, peer):
        copy = pltpu.make_async_remote_copy(
            src_ref=src, dst_ref=dst, send_sem=ssem.at[index], recv_sem=rsem.at[index],
            device_id=peer, device_id_type=MESH)
        copy.start()
        return copy

    if comm:
        pl.semaphore_wait(barrier, len(peers))
        index = 0
        for buf, w, nx, rows in ((nv, 2, 8, 16), (nc, 1, 8, 16)):
            top = w + nx
            r0, r1, r2, r3 = 0, w * 16, (w + rows) * 16, (2 * w + rows) * 16
            xr = {-1: (slice(w, 2 * w), slice(top, top + w)),
                  0: (slice(w, top), slice(w, top)),
                  1: (slice(top - w, top), slice(0, w))}
            yr = {-1: (slice(r1, 2 * r1), slice(r2, r3)),
                  0: (slice(r1, r2), slice(r1, r2)),
                  1: (slice(r2 - r1, r2), slice(r0, r1))}
            for a in (-1, 0, 1):
                for b in (-1, 0, 1):
                    if a == 0 and b == 0:
                        continue
                    copies.append(send(index, buf.at[xr[a][0], yr[b][0]],
                                       buf.at[xr[a][1], yr[b][1]], at(gx + a, gy + b)))
                    index += 1
    else:
        nv[0:2] = jnp.zeros((2, 320, 128), BF)
        nv[10:12] = jnp.zeros((2, 320, 128), BF)
        nv[:, 0:32] = jnp.zeros((12, 32, 128), BF)
        nv[:, 288:320] = jnp.zeros((12, 32, 128), BF)
        nc[0:1] = jnp.zeros((1, 288, 128), BF)
        nc[9:10] = jnp.zeros((1, 288, 128), BF)
        nc[:, 0:16] = jnp.zeros((10, 16, 128), BF)
        nc[:, 272:288] = jnp.zeros((10, 16, 128), BF)

    for kk in range(9):
        for t, base in ((t1, 0), (t2, 9)):
            w = wc[base + kk].astype(F32)
            for yo in range(6):
                t[yo * 32:(yo + 1) * 32, kk * 256:(kk + 1) * 256] = (
                    w if yo == 0 else pltpu.roll(w, 32 * yo, axis=1)).astype(BF)
    for kz in range(3):
        gp[kz, 576:640] = jnp.zeros((64, 768), BF)

    if comm:
        for copy in copies:
            copy.wait()

        @pl.when(gx == 0)
        def _():
            nv[0:2] = jnp.zeros((2, 320, 128), BF)
            nc[0:1] = jnp.zeros((1, 288, 128), BF)

        @pl.when(gx == ngx - 1)
        def _():
            nv[10:12] = jnp.zeros((2, 320, 128), BF)
            nc[9:10] = jnp.zeros((1, 288, 128), BF)

        @pl.when(gy == 0)
        def _():
            nv[:, 0:32] = jnp.zeros((12, 32, 128), BF)
            nc[:, 0:16] = jnp.zeros((10, 16, 128), BF)

        @pl.when(gy == ngy - 1)
        def _():
            nv[:, 288:320] = jnp.zeros((12, 32, 128), BF)
            nc[:, 272:288] = jnp.zeros((10, 16, 128), BF)

    def paired(buf, j, rows):
        a = buf[j]
        b = buf[j + 4]
        even = jnp.where(low, a, pltpu.roll(b, 64, axis=1))
        odd = jnp.where(low, pltpu.roll(a, 64, axis=1), b)
        both = jnp.concatenate(
            [even.reshape(rows, 1, 16, 128), odd.reshape(rows, 1, 16, 128)], axis=1)
        return both.reshape(rows * 32, 128)

    def fill_s(j, carry):
        block = paired(nv, j, 20)
        lanes = pl.ds(pl.multiple_of(j * 128, 128), 128)
        s[1, :, lanes] = block
        s[0, :, lanes] = shifted(block, 1, z_first)
        s[2, :, lanes] = shifted(block, 127, z_last)
        return carry

    lax.fori_loop(0, 8, fill_s, 0)

    def fill_c(j, carry):
        lanes = pl.ds(pl.multiple_of(j * 128, 128), 128)
        c[:, lanes] = paired(nc, j, 18)
        return carry

    lax.fori_loop(0, 6, fill_c, 0)

    def forward(step, carry):
        b = lax.div(step, 3)
        n = lax.rem(step, 3)
        rows = pl.ds(pl.multiple_of(b * 192, 64), 256)
        out_rows = pl.ds(pl.multiple_of(b * 192, 64), 192)
        out_lanes = pl.ds(pl.multiple_of(n * 256, 128), 256)
        rhs = jnp.concatenate(
            [s[kz, rows, pl.ds(pl.multiple_of(n * 256 + kx * 128, 128), 256)]
             for kx in range(3) for kz in range(3)], axis=0)
        pre = jnp.dot(t1[...], rhs, preferred_element_type=F32) + bias[...]
        sig = 0.5 * jnp.tanh(0.5 * pre) + 0.5
        own = (c[out_rows, out_lanes].astype(F32) * sig * (1.0 + pre * (1.0 - sig))).astype(BF)
        gp[1, out_rows, out_lanes] = own
        for e in range(2):
            piece = own[:, e * 128:(e + 1) * 128]
            lanes = pl.ds(pl.multiple_of(n * 256 + e * 128, 128), 128)
            gp[0, out_rows, lanes] = shifted(piece, 127, z_last)
            gp[2, out_rows, lanes] = shifted(piece, 1, z_first)
        return carry

    lax.fori_loop(0, 9, forward, 0)

    group = lane // 32

    def gathered(wide, tail, rows):
        cells = []
        for q in range(4):
            step = 32 if rows == 96 else 0
            cell = wide[step * q:step * q + rows, :128] + tail[step * q:step * q + rows, :128]
            if q < 2:
                cell = cell + wide[step * (q + 4):step * (q + 4) + rows, 128:]
            cells.append(cell)
        total = jnp.where(group == 0, cells[0], jnp.where(group == 1, cells[1],
                          jnp.where(group == 2, cells[2], cells[3])))
        total = total + pltpu.roll(total, 64, axis=1)
        return total + pltpu.roll(total, 32, axis=1)

    part[...] = jnp.zeros((8, 32, 128), F32)

    def grads(n, count, height):
        return jnp.concatenate([gp[1, 192 * b + 32:192 * b + 32 + height, 128:640]
                                for b in range(n, n + count)], axis=1)

    def filters(kk, carry):
        kx = lax.div(kk, 3)
        kz = lax.rem(kk, 3)
        lanes = pl.ds(pl.multiple_of(kx * 128 + 128, 128), 512)
        left = jnp.concatenate([s[kz, 32:288, lanes], s[kz, 224:480, lanes]], axis=1)
        wide = lax.dot_general(left, grads(0, 2, 256), NT, preferred_element_type=F32)
        tail = lax.dot_general(s[kz, 416:608, lanes], grads(2, 1, 128), NT,
                               preferred_element_type=F32)
        total = gathered(wide, tail, 96)
        for ky in range(3):
            t = kk * 3 + ky
            which = lax.div(t, 4)
            part[which] = jnp.where(group == lax.rem(t, 4), total[ky * 32:(ky + 1) * 32], part[which])
        return carry

    lax.fori_loop(0, 9, filters, 0)
    ones = jnp.ones((16, 1024), BF)
    wide = lax.dot_general(ones, grads(0, 2, 256), NT, preferred_element_type=F32)
    tail = lax.dot_general(ones[:, :512], grads(2, 1, 128), NT, preferred_element_type=F32)
    total = gathered(wide, tail, 16)
    part[6] = jnp.where(group == 3, jnp.concatenate([total, total], axis=0), part[6])

    def backward(b):
        for n in range(2):
            rhs = jnp.concatenate(
                [gp[kz, b * 192:b * 192 + 256, 128 * (2 * n + 2 - kx):128 * (2 * n + 4 - kx)]
                 for kx in range(3) for kz in range(3)], axis=0)
            dq[b * 192:b * 192 + 192, n * 256:n * 256 + 256] = jnp.dot(
                t2[...], rhs, preferred_element_type=F32).astype(BF)

    def emit():
        for j in range(4):
            block = dq[0:512, j * 128:j * 128 + 128].reshape(16, 2, 16, 128)
            even = block[:, 0].reshape(256, 128)
            odd = block[:, 1].reshape(256, 128)
            first = jnp.where(low, even, pltpu.roll(odd, 64, axis=1))
            second = jnp.where(low, pltpu.roll(even, 64, axis=1), odd)
            out = jnp.dot(perm, jnp.concatenate([first, second], axis=1),
                          preferred_element_type=F32).astype(BF)
            for g in range(16):
                dx[j, :, g * 128:(g + 1) * 128] = out[g * 16:(g + 1) * 16, :128]
                dx[j + 4, :, g * 128:(g + 1) * 128] = out[g * 16:(g + 1) * 16, 128:]

    if comm:
        for i in range(8):
            part16[i] = part[i].astype(BF)
        base = 16
        round1 = [send(base + k, part16.at[lax.rem(gx + k + 1, 8)], rs.at[k], gx_peers[k])
                  for k in range(7)]
        backward(0)
        for copy in round1:
            copy.wait()
        mine = part[gx]
        for k in range(7):
            mine = mine + rs[k].astype(F32)
        xs[xi] = mine.astype(BF)
        base += 7
        round2 = [send(base + k, xs.at[xi], xs.at[xi], x_peers[k]) for k in range(X_CHIPS - 1)]
        backward(1)
        for copy in round2:
            copy.wait()
        mine = xs[0].astype(F32)
        for k in range(1, X_CHIPS):
            mine = mine + xs[k].astype(F32)
        zs[zi] = mine.astype(BF)
        base += X_CHIPS - 1
        round3 = [send(base + k, zs.at[zi], zs.at[zi], z_peers[k]) for k in range(Z_CHIPS - 1)]
        backward(2)
        emit()
        for copy in round3:
            copy.wait()
        mine = zs[0].astype(F32)
        for k in range(1, Z_CHIPS):
            mine = mine + zs[k].astype(F32)
        fin[gx] = mine.astype(BF)
        base += Z_CHIPS - 1
        round4 = [send(base + k, fin.at[gx], fin.at[gx], gx_peers[k]) for k in range(7)]
        for copy in round4:
            copy.wait()
    else:
        backward(0)
        backward(1)
        backward(2)
        emit()
        for i in range(8):
            fin[i] = part[i].astype(BF)

    row = lax.broadcasted_iota(jnp.int32, (128, 128), 0)
    col = lax.broadcasted_iota(jnp.int32, (128, 128), 1)
    source = (col // 32) * 32 + (col % 2) * 16 + (col % 32) // 2
    swap = jnp.where(row == source, 1.0, 0.0).astype(BF)
    final = jnp.dot(fin[...].reshape(256, 128), swap, preferred_element_type=F32) * scale
    for t in range(27):
        block = final[(t // 4) * 32:(t // 4) * 32 + 32]
        if t % 4:
            block = pltpu.roll(block, 128 - 32 * (t % 4), axis=1)
        k = (t // 9) * 9 + (t % 3) * 3 + (t // 3) % 3
        df[k, pl.ds(0, 16, stride=2), :] = block[0:16, 0:32]
        df[k, pl.ds(1, 16, stride=2), :] = block[16:32, 0:32]
    db[...] = pltpu.roll(final[192:200], 32, axis=1)[0:1, 0:32]


def shards(comm, cells, volume, cotangent, weight, bias):
    order = jnp.array([2 * (i % 16) + i // 16 for i in range(C)])
    w = weight.reshape(3, 3, 3, 16, 2, 16, 2).transpose(0, 2, 1, 4, 3, 6, 5).reshape(9, 3, C, C)
    fwd = w.transpose(0, 3, 1, 2).reshape(9, C, 3 * C)
    bwd = w[:, ::-1].transpose(0, 2, 1, 3).reshape(9, C, 3 * C)
    wc = jnp.pad(jnp.concatenate([fwd, bwd], axis=0), ((0, 0), (0, 0), (0, 256 - 3 * C)))
    bias_rows = jnp.tile(bias.reshape(16, 2).T.reshape(C), 6).reshape(192, 1)
    vm = pl.BlockSpec(memory_space=pltpu.VMEM)
    dg, df, db = pl.pallas_call(
        functools.partial(kernel, 1.0 / math.sqrt(cells), comm),
        out_shape=(jax.ShapeDtypeStruct(volume.shape, BF),
                   jax.ShapeDtypeStruct((27, C, C), F32),
                   jax.ShapeDtypeStruct((1, C), F32)),
        in_specs=[vm] * 4,
        out_specs=(vm, vm, vm),
        scratch_shapes=[
            pltpu.VMEM((12, 320, 128), BF),
            pltpu.VMEM((10, 288, 128), BF),
            pltpu.VMEM((3, 640, 1024), BF),
            pltpu.VMEM((576, 768), BF),
            pltpu.VMEM((3, 640, 768), BF),
            pltpu.VMEM((192, 2304), BF),
            pltpu.VMEM((192, 2304), BF),
            pltpu.VMEM((576, 512), BF),
            pltpu.VMEM((8, 32, 128), F32),
            pltpu.VMEM((8, 32, 128), BF),
            pltpu.VMEM((7, 32, 128), BF),
            pltpu.VMEM((X_CHIPS, 32, 128), BF),
            pltpu.VMEM((Z_CHIPS, 32, 128), BF),
            pltpu.VMEM((8, 32, 128), BF),
            pltpu.SemaphoreType.DMA((40,)),
            pltpu.SemaphoreType.DMA((40,)),
        ],
        compiler_params=pltpu.CompilerParams(
            collective_id=0 if comm else None, has_side_effects=comm, vmem_limit_bytes=48 << 20),
    )(volume, cotangent, wc, bias_rows)
    return dg, df.reshape(3, 3, 3, C, C), db.reshape(C)


def solution(mesh):
    cells = 8 * mesh.shape["gx"] * 16 * mesh.shape["gy"] * 64
    in_specs = (P("gx", "gy", None), P("gx", "gy", None), P(), P())
    out_specs = (P("gx", "gy", None), P(), P())
    return jax.shard_map(functools.partial(shards, True, cells), mesh=mesh, in_specs=in_specs,
                         out_specs=out_specs, check_vma=False)
```

```python
import functools
import math

import jax
import jax.numpy as jnp
from jax import lax
from jax.experimental import pallas as pl
from jax.experimental.pallas import tpu as pltpu
from jax.sharding import PartitionSpec as P

C = 32
MESH = pl.DeviceIdType.MESH
BF = jnp.bfloat16
F32 = jnp.float32
X_CHIPS = 4
Z_CHIPS = 8
NT = (((1,), (1,)), ((), ()))


def shifted(block, amount, keep):
    return jnp.where(keep, pltpu.roll(block, amount, axis=1), jnp.zeros_like(block))


def natural(index):
    return 2 * (index % 16) + (index % 32) // 16


def one_hot(rows, cols, test):
    row = lax.broadcasted_iota(jnp.int32, (rows, cols), 0)
    col = lax.broadcasted_iota(jnp.int32, (rows, cols), 1)
    return jnp.where(test(row, col), 1.0, 0.0)


def kernel(scale, comm, vol_hbm, cot_hbm, w_hbm, b_hbm, dx, df, db, vol, cot, wbuf, bbuf, nv, nc,
           s, c, gp, t1, t2, tb, dq, part, part16, rs, xs, zs, fin, ssem, rsem, lsem):
    if comm:
        gx = lax.axis_index("gx")
        gy = lax.axis_index("gy")
        ngx = lax.axis_size("gx")
        ngy = lax.axis_size("gy")
        xi = lax.rem(gy, X_CHIPS)
        zi = lax.div(gy, X_CHIPS)

        def at(ax, ay):
            return {"gx": lax.rem(ax + ngx, ngx), "gy": lax.rem(ay + ngy, ngy)}

        around = [(a, b) for a in (-1, 0, 1) for b in (-1, 0, 1) if a or b]
        gx_peers = [at(gx + k, gy) for k in range(1, 8)]
        x_peers = [at(gx, zi * X_CHIPS + lax.rem(xi + k, X_CHIPS)) for k in range(1, X_CHIPS)]
        z_peers = [at(gx, lax.rem(zi + k, Z_CHIPS) * X_CHIPS + xi) for k in range(1, Z_CHIPS)]
        peers = gx_peers + x_peers + z_peers + [at(gx + a, gy + b) for a, b in around if b]
        barrier = pltpu.get_barrier_semaphore()
        for peer in peers:
            pl.semaphore_signal(barrier, inc=1, device_id=peer, device_id_type=MESH)

    loads = [pltpu.make_async_copy(a, b, lsem.at[i]) for i, (a, b) in enumerate(
        ((vol_hbm, vol), (cot_hbm, cot), (w_hbm, wbuf), (b_hbm, bbuf)))]
    for load in loads:
        load.start()

    lane = lax.broadcasted_iota(jnp.int32, (1, 128), 1)
    low = lane < 64
    z_first = (lane % 64) != 0
    z_last = (lane % 64) != 63
    perm = one_hot(256, 256, lambda r, q: q == (r % 16) * 16 + r // 16).astype(BF)

    def turn(src, dst, first, offset):
        for x in range(0, 8, 2):
            parts = [
                jnp.concatenate([src[x + e, :, g * 128:(g + 1) * 128] for g in range(16)], axis=0)
                for e in range(2)
            ]
            out = jnp.dot(perm, jnp.concatenate(parts, axis=1), preferred_element_type=F32).astype(BF)
            dst[first + x, offset:offset + 256] = out[:, :128]
            dst[first + x + 1, offset:offset + 256] = out[:, 128:]

    used = []

    def send(src, dst, peer):
        index = len(used)
        used.append(index)
        copy = pltpu.make_async_remote_copy(
            src_ref=src, dst_ref=dst, send_sem=ssem.at[index], recv_sem=rsem.at[index],
            device_id=peer, device_id_type=MESH)
        copy.start()
        return copy

    def wipe(ref, *shape):
        ref[...] = jnp.zeros(shape, BF)

    loads[0].wait()
    turn(vol, nv, 2, 32)
    if comm:
        pl.semaphore_wait(barrier, len(peers))
        wave1 = [
            send(nv.at[2, 32:288], nv.at[10, 32:288], at(gx - 1, gy)),
            send(nv.at[9, 32:288], nv.at[1, 32:288], at(gx + 1, gy)),
            send(nv.at[2:10, 32:48], nv.at[2:10, 288:304], at(gx, gy - 1)),
            send(nv.at[2:10, 272:288], nv.at[2:10, 16:32], at(gx, gy + 1)),
        ]
        corner_x = {-1: (slice(2, 4), slice(10, 12)), 1: (slice(8, 10), slice(0, 2))}
        corner_y = {-1: (slice(32, 64), slice(288, 320)), 1: (slice(256, 288), slice(0, 32))}
        for a in (-1, 1):
            for b in (-1, 1):
                wave1.append(send(nv.at[corner_x[a][0], corner_y[b][0]],
                                  nv.at[corner_x[a][1], corner_y[b][1]], at(gx + a, gy + b)))
    loads[1].wait()
    turn(cot, nc, 1, 16)
    if comm:
        wave2 = [
            send(nv.at[3, 32:288], nv.at[11, 32:288], at(gx - 1, gy)),
            send(nv.at[8, 32:288], nv.at[0, 32:288], at(gx + 1, gy)),
            send(nv.at[2:10, 48:64], nv.at[2:10, 304:320], at(gx, gy - 1)),
            send(nv.at[2:10, 256:272], nv.at[2:10, 0:16], at(gx, gy + 1)),
        ]
        side_x = {-1: (slice(1, 2), slice(9, 10)), 0: (slice(1, 9), slice(1, 9)),
                  1: (slice(8, 9), slice(0, 1))}
        side_y = {-1: (slice(16, 32), slice(272, 288)), 0: (slice(16, 272), slice(16, 272)),
                  1: (slice(256, 272), slice(0, 16))}
        for a, b in around:
            wave2.append(send(nc.at[side_x[a][0], side_y[b][0]],
                              nc.at[side_x[a][1], side_y[b][1]], at(gx + a, gy + b)))

    def paired(buf, j, r0, r1):
        rows = (r1 - r0) // 16
        a = buf[j, r0:r1]
        b = buf[j + 4, r0:r1]
        even = jnp.where(low, a, pltpu.roll(b, 64, axis=1))
        odd = jnp.where(low, pltpu.roll(a, 64, axis=1), b)
        both = jnp.concatenate(
            [even.reshape(rows, 1, 16, 128), odd.reshape(rows, 1, 16, 128)], axis=1)
        return both.reshape(rows * 32, 128)

    def fill_s(j, y0, y1):
        block = paired(nv, j, y0 * 16, y1 * 16)
        s[1, j, y0 * 32:y1 * 32] = block
        s[0, j, y0 * 32:y1 * 32] = shifted(block, 1, z_first)
        s[2, j, y0 * 32:y1 * 32] = shifted(block, 127, z_last)

    def fill_c(j, y0, y1):
        c[j, y0 * 32:y1 * 32] = paired(nc, j, y0 * 16, y1 * 16)

    @pl.loop(2, 6)
    def _(j):
        fill_s(j, 2, 18)

    @pl.loop(1, 5)
    def _(j):
        fill_c(j, 1, 17)

    def spread(t, kk, base):
        turned = [base] + [pltpu.roll(base, 32 * i, axis=1) for i in (1, 2, 3)]
        zero = jnp.zeros_like(base)
        rows = [(base, zero), (turned[1], zero),
                (jnp.where(lane >= 64, turned[2], zero), jnp.where(lane < 64, turned[2], zero)),
                (jnp.where(lane >= 96, turned[3], zero), jnp.where(lane < 96, turned[3], zero)),
                (zero, base), (zero, turned[1])]
        for yo in range(6):
            for half in range(2):
                t[2 * kk + half, yo * 32:(yo + 1) * 32] = rows[yo][half]

    loads[2].wait()
    loads[3].wait()
    rows4 = one_hot(128, 128, lambda r, q: (r // 32 == q // 32) & (q % 32 == natural(r))).astype(BF)
    lanes1 = one_hot(32, 32, lambda r, q: q == natural(r)).astype(BF)
    stacked = []
    for kk in range(9):
        raw = jnp.concatenate([wbuf[(kk // 3) * 9 + ky * 3 + kk % 3] for ky in range(3)]
                              + [jnp.zeros((32, 32), BF)], axis=0)
        stacked.append(jnp.dot(rows4, raw, preferred_element_type=F32).astype(BF))
        spread(t1, kk, lax.dot_general(lanes1, stacked[kk], NT, preferred_element_type=F32).astype(BF))
    tb[...] = lax.dot_general(
        one_hot(192, 32, lambda r, q: q == natural(r)),
        jnp.broadcast_to(bbuf[...], (128, 32)), NT,
        preferred_element_type=F32, precision=lax.Precision.HIGHEST)

    if comm:
        for copy in wave1:
            copy.wait()

        @pl.when(gx == 0)
        def _():
            wipe(nv.at[1], 320, 128)
            wipe(nv.at[0, 0:32], 32, 128)
            wipe(nv.at[0, 288:320], 32, 128)

        @pl.when(gx == ngx - 1)
        def _():
            wipe(nv.at[10], 320, 128)
            wipe(nv.at[11, 0:32], 32, 128)
            wipe(nv.at[11, 288:320], 32, 128)

        @pl.when(gy == 0)
        def _():
            wipe(nv.at[2:10, 16:32], 8, 16, 128)
            wipe(nv.at[0:2, 0:32], 2, 32, 128)
            wipe(nv.at[10:12, 0:32], 2, 32, 128)

        @pl.when(gy == ngy - 1)
        def _():
            wipe(nv.at[2:10, 288:304], 8, 16, 128)
            wipe(nv.at[0:2, 288:320], 2, 32, 128)
            wipe(nv.at[10:12, 288:320], 2, 32, 128)
    else:
        wipe(nv.at[0:2], 2, 320, 128)
        wipe(nv.at[10:12], 2, 320, 128)
        wipe(nv.at[:, 0:32], 12, 32, 128)
        wipe(nv.at[:, 288:320], 12, 32, 128)
        wipe(nc.at[0], 288, 128)
        wipe(nc.at[9], 288, 128)
        wipe(nc.at[:, 0:16], 10, 16, 128)
        wipe(nc.at[:, 272:288], 10, 16, 128)

    fill_s(1, 1, 19)
    fill_s(6, 1, 19)
    for j in range(2, 6):
        fill_s(j, 1, 2)
        fill_s(j, 18, 19)

    def tiles(buf, kz, cells, r0, r1):
        return jnp.concatenate([buf[kz, cell, r0:r1] for cell in cells], axis=1)

    def filter_rows(t, r0, r1, halves=(0, 1)):
        return jnp.concatenate([t[2 * kk + h, r0:r1] for kk in range(9) for h in halves], axis=1)

    def activate(acc, r0, r1, cells, y):
        for e, cell in enumerate(cells):
            pre = acc[:, e * 128:(e + 1) * 128] + tb[r0:r1]
            sig = 0.5 * jnp.tanh(0.5 * pre) + 0.5
            grad = c[cell, y:y + r1 - r0].astype(F32)
            gp[1, cell, y:y + r1 - r0] = (grad * sig * (1.0 + pre * (1.0 - sig))).astype(BF)

    def forward(r0, r1, y_in, y_out, cells):
        rhs = jnp.concatenate(
            [tiles(s, kz, [cell + kx for cell in cells], y_in * 32, y_in * 32 + 256)
             for kx in range(3) for kz in range(3)], axis=0)
        acc = jnp.dot(filter_rows(t1, r0, r1), rhs, preferred_element_type=F32)
        activate(acc, r0, r1, cells, y_out * 32)

    @pl.loop(0, 2)
    def _(n):
        cells = (2 * n + 1, 2 * n + 2)
        forward(0, 192, 1, 1, cells)
        forward(0, 192, 7, 7, cells)
        forward(64, 192, 11, 13, cells)

    group = lane // 32

    def gathered(wide, tail, rows):
        cells = []
        for q in range(4):
            step = 32 if rows == 96 else 0
            cell = wide[step * q:step * q + rows, :128] + tail[step * q:step * q + rows, :128]
            if q < 2:
                cell = cell + wide[step * (q + 4):step * (q + 4) + rows, 128:]
            cells.append(cell)
        total = jnp.where(group == 0, cells[0], jnp.where(group == 1, cells[1],
                          jnp.where(group == 2, cells[2], cells[3])))
        total = total + pltpu.roll(total, 64, axis=1)
        return total + pltpu.roll(total, 32, axis=1)

    part[...] = jnp.zeros((8, 32, 128), F32)
    own = range(1, 5)

    def grads():
        wide = jnp.concatenate([tiles(gp, 1, own, 32, 288), tiles(gp, 1, own, 224, 480)], axis=1)
        return wide, tiles(gp, 1, own, 416, 544)

    @pl.loop(0, 3)
    def _(kx):
        right, right_tail = grads()
        for kz in range(3):
            cells = [kx + cell for cell in own]
            left = jnp.concatenate([tiles(s, kz, cells, 32, 288), tiles(s, kz, cells, 224, 480)], axis=1)
            wide = lax.dot_general(left, right, NT, preferred_element_type=F32)
            tail = lax.dot_general(tiles(s, kz, cells, 416, 608), right_tail, NT,
                                   preferred_element_type=F32)
            total = gathered(wide, tail, 96)
            for ky in range(3):
                t = kx * 9 + kz * 3 + ky
                which = lax.div(t, 4)
                part[which] = jnp.where(group == lax.rem(t, 4), total[ky * 32:(ky + 1) * 32],
                                        part[which])

    right, right_tail = grads()
    ones = jnp.ones((16, 1024), BF)
    wide = lax.dot_general(ones, right, NT, preferred_element_type=F32)
    tail = lax.dot_general(ones[:, :512], right_tail, NT, preferred_element_type=F32)
    total = gathered(wide, tail, 16)
    part[6] = jnp.where(group == 3, jnp.concatenate([total, total], axis=0), part[6])

    lower = lax.broadcasted_iota(jnp.int32, (32, 128), 0) >= 16

    def split(value, index):
        rounded = value.astype(BF)
        rest = (value - rounded.astype(F32)).astype(BF)
        return jnp.where((index == 6) & (group == 3) & lower, rest, rounded)

    def joined(value, index):
        both = value + jnp.concatenate([value[16:], value[:16]], axis=0)
        return jnp.where((index == 6) & (group == 3), both, value)

    def later_halo():
        base = sum(jnp.dot(jnp.concatenate([stacked_rows(kk, 2 - d) for kk in range(9)], axis=0),
                           one_hot(32, 128, lambda r, q: (q // 32 == d) & (r == natural(q))).astype(BF),
                           preferred_element_type=F32) for d in range(3)).astype(BF)
        for kk in range(9):
            spread(t2, kk, base[kk * 32:(kk + 1) * 32])

        @pl.loop(1, 5)
        def _(j):
            turn_gp(j, 1, 17)

        if comm:
            for copy in wave2:
                copy.wait()

            @pl.when(gx == 0)
            def _():
                wipe(nv.at[0, 32:288], 256, 128)
                wipe(nc.at[0], 288, 128)

            @pl.when(gx == ngx - 1)
            def _():
                wipe(nv.at[11, 32:288], 256, 128)
                wipe(nc.at[9], 288, 128)

            @pl.when(gy == 0)
            def _():
                wipe(nv.at[2:10, 0:16], 8, 16, 128)
                wipe(nc.at[:, 0:16], 10, 16, 128)

            @pl.when(gy == ngy - 1)
            def _():
                wipe(nv.at[2:10, 304:320], 8, 16, 128)
                wipe(nc.at[:, 272:288], 10, 16, 128)

        for j in (0, 7):
            fill_s(j, 0, 20)
        for j in range(1, 7):
            fill_s(j, 0, 1)
            fill_s(j, 19, 20)
        for j in (0, 5):
            fill_c(j, 0, 18)
        for j in own:
            fill_c(j, 0, 1)
            fill_c(j, 17, 18)
        for b in range(3):
            forward(0, 192, 6 * b, 6 * b, (0, 5))
        for cells in ((1, 2), (3, 4)):
            for half, y_in, r0, y_out in ((0, 0, 0, 0), (1, 16, 160, 17)):
                rhs = jnp.concatenate(
                    [tiles(s, kz, [cell + kx for cell in cells], y_in * 32, y_in * 32 + 128)
                     for kx in range(3) for kz in range(3)], axis=0)
                acc = jnp.dot(filter_rows(t1, r0, r0 + 32, (half,)), rhs, preferred_element_type=F32)
                activate(acc, r0, r0 + 32, cells, y_out * 32)
        for j in (0, 5):
            turn_gp(j, 0, 18)
        for j in own:
            turn_gp(j, 0, 1)
            turn_gp(j, 17, 18)

    def stacked_rows(kk, ky):
        return stacked[kk][ky * 32:(ky + 1) * 32]

    def turn_gp(j, y0, y1):
        block = gp[1, j, y0 * 32:y1 * 32]
        gp[0, j, y0 * 32:y1 * 32] = shifted(block, 127, z_last)
        gp[2, j, y0 * 32:y1 * 32] = shifted(block, 1, z_first)

    def backward(b):
        start, r0 = ((0, 0), (6, 0), (10, 64))[b]
        left = filter_rows(t2, r0, 192)
        out = start * 32 + r0
        for n in range(2):
            rhs = jnp.concatenate(
                [tiles(gp, kz, (2 * n + 2 - kx, 2 * n + 3 - kx), start * 32, start * 32 + 256)
                 for kx in range(3) for kz in range(3)], axis=0)
            acc = jnp.dot(left, rhs, preferred_element_type=F32).astype(BF)
            dq[2 * n, out:out + 192 - r0] = acc[:, :128]
            dq[2 * n + 1, out:out + 192 - r0] = acc[:, 128:]

    def emit():
        for j in range(4):
            block = dq[j].reshape(16, 2, 16, 128)
            even = block[:, 0].reshape(256, 128)
            odd = block[:, 1].reshape(256, 128)
            first = jnp.where(low, even, pltpu.roll(odd, 64, axis=1))
            second = jnp.where(low, pltpu.roll(even, 64, axis=1), odd)
            out = jnp.dot(perm, jnp.concatenate([first, second], axis=1),
                          preferred_element_type=F32).astype(BF)
            for g in range(16):
                dx[j, :, g * 128:(g + 1) * 128] = out[g * 16:(g + 1) * 16, :128]
                dx[j + 4, :, g * 128:(g + 1) * 128] = out[g * 16:(g + 1) * 16, 128:]

    def summed(buf, count, index):
        total = buf[0].astype(F32)
        for k in range(1, count):
            total = total + buf[k].astype(F32)
        return joined(total, index)

    for i in range(8):
        part16[i] = split(part[i], i) if i == 6 else part[i].astype(BF)
    if comm:
        round1 = [send(part16.at[lax.rem(gx + k + 1, 8)], rs.at[k], gx_peers[k]) for k in range(7)]
        rs[7] = part16[gx]
        later_halo()
        for copy in round1:
            copy.wait()
        xs[xi] = split(summed(rs, 8, gx), gx)
        round2 = [send(xs.at[xi], xs.at[xi], x_peers[k]) for k in range(X_CHIPS - 1)]
        backward(0)
        backward(1)
        for copy in round2:
            copy.wait()
        zs[zi] = split(summed(xs, X_CHIPS, gx), gx)
        round3 = [send(zs.at[zi], zs.at[zi], z_peers[k]) for k in range(Z_CHIPS - 1)]
        backward(2)
        emit()
        for copy in round3:
            copy.wait()
        fin[gx] = split(summed(zs, Z_CHIPS, gx), gx)
        round4 = [send(fin.at[gx], fin.at[gx], gx_peers[k]) for k in range(7)]
        for copy in round4:
            copy.wait()
    else:
        later_halo()
        backward(0)
        backward(1)
        backward(2)
        emit()
        for i in range(8):
            fin[i] = part16[i]

    swap = one_hot(128, 128, lambda r, q: r == (q // 32) * 32 + (q % 2) * 16 + (q % 32) // 2).astype(BF)
    final = jnp.dot(fin[...].reshape(256, 128), swap, preferred_element_type=F32) * scale
    for t in range(27):
        block = final[(t // 4) * 32:(t // 4) * 32 + 32]
        if t % 4:
            block = pltpu.roll(block, 128 - 32 * (t % 4), axis=1)
        k = (t // 9) * 9 + (t % 3) * 3 + (t // 3) % 3
        df[k, pl.ds(0, 16, stride=2), :] = block[0:16, 0:32]
        df[k, pl.ds(1, 16, stride=2), :] = block[16:32, 0:32]
    db[...] = pltpu.roll(final[192:200] + final[208:216], 32, axis=1)[0:1, 0:32]


def shards(comm, cells, volume, cotangent, weight, bias):
    vm = pl.BlockSpec(memory_space=pltpu.VMEM)
    hbm = pl.BlockSpec(memory_space=pltpu.MemorySpace.HBM)
    dg, df, db = pl.pallas_call(
        functools.partial(kernel, 1.0 / math.sqrt(cells), comm),
        out_shape=(jax.ShapeDtypeStruct(volume.shape, BF),
                   jax.ShapeDtypeStruct((27, C, C), F32),
                   jax.ShapeDtypeStruct((1, C), F32)),
        in_specs=[hbm] * 4,
        out_specs=(vm, vm, vm),
        scratch_shapes=[
            pltpu.VMEM((8, 16, 2048), BF),
            pltpu.VMEM((8, 16, 2048), BF),
            pltpu.VMEM((27, C, C), BF),
            pltpu.VMEM((1, C), F32),
            pltpu.VMEM((12, 320, 128), BF),
            pltpu.VMEM((10, 288, 128), BF),
            pltpu.VMEM((3, 8, 640, 128), BF),
            pltpu.VMEM((6, 576, 128), BF),
            pltpu.VMEM((3, 6, 576, 128), BF),
            pltpu.VMEM((18, 192, 128), BF),
            pltpu.VMEM((18, 192, 128), BF),
            pltpu.VMEM((192, 128), F32),
            pltpu.VMEM((4, 512, 128), BF),
            pltpu.VMEM((8, 32, 128), F32),
            pltpu.VMEM((8, 32, 128), BF),
            pltpu.VMEM((8, 32, 128), BF),
            pltpu.VMEM((X_CHIPS, 32, 128), BF),
            pltpu.VMEM((Z_CHIPS, 32, 128), BF),
            pltpu.VMEM((8, 32, 128), BF),
            pltpu.SemaphoreType.DMA((44,)),
            pltpu.SemaphoreType.DMA((44,)),
            pltpu.SemaphoreType.DMA((4,)),
        ],
        compiler_params=pltpu.CompilerParams(
            collective_id=0 if comm else None, has_side_effects=comm, vmem_limit_bytes=48 << 20),
    )(volume, cotangent, weight.reshape(27, C, C), bias.reshape(1, C))
    return dg, df.reshape(3, 3, 3, C, C), db.reshape(C)


def solution(mesh):
    cells = 8 * mesh.shape["gx"] * 16 * mesh.shape["gy"] * 64
    in_specs = (P("gx", "gy", None), P("gx", "gy", None), P(), P())
    out_specs = (P("gx", "gy", None), P(), P())
    return jax.shard_map(functools.partial(shards, True, cells), mesh=mesh, in_specs=in_specs,
                         out_specs=out_specs, check_vma=False)
```

```python
import functools
import math

import jax
import jax.numpy as jnp
from jax import lax
from jax.experimental import pallas as pl
from jax.experimental.pallas import tpu as pltpu
from jax.sharding import PartitionSpec as P

C = 32
MESH = pl.DeviceIdType.MESH
BF = jnp.bfloat16
F32 = jnp.float32
X_CHIPS = 4
Z_CHIPS = 8
NT = (((1,), (1,)), ((), ()))


def shifted(block, amount, keep):
    return jnp.where(keep, pltpu.roll(block, amount, axis=1), jnp.zeros_like(block))


def natural(index):
    return 2 * (index % 16) + (index % 32) // 16


def one_hot(rows, cols, test):
    row = lax.broadcasted_iota(jnp.int32, (rows, cols), 0)
    col = lax.broadcasted_iota(jnp.int32, (rows, cols), 1)
    return jnp.where(test(row, col), 1.0, 0.0)


def kernel(comm, vol_hbm, cot_hbm, w_hbm, b_hbm, dx, fin, vol, cot, wbuf, bbuf, nv, nc,
           s, c, gp, t1, t2, tb, dq, part, part16, rs, xs, zs, ssem, rsem, lsem):
    if comm:
        gx = lax.axis_index("gx")
        gy = lax.axis_index("gy")
        ngx = lax.axis_size("gx")
        ngy = lax.axis_size("gy")
        xi = lax.rem(gy, X_CHIPS)
        zi = lax.div(gy, X_CHIPS)

        def at(ax, ay):
            return {"gx": lax.rem(ax + ngx, ngx), "gy": lax.rem(ay + ngy, ngy)}

        around = [(a, b) for a in (-1, 0, 1) for b in (-1, 0, 1) if a or b]
        gx_peers = [at(gx + k, gy) for k in range(1, 8)]
        x_peers = [at(gx, zi * X_CHIPS + lax.rem(xi + k, X_CHIPS)) for k in range(1, X_CHIPS)]
        z_peers = [at(gx, lax.rem(zi + k, Z_CHIPS) * X_CHIPS + xi) for k in range(1, Z_CHIPS)]
        peers = gx_peers + x_peers + z_peers + [at(gx + a, gy + b) for a, b in around if b]
        barrier = pltpu.get_barrier_semaphore()
        for peer in peers:
            pl.semaphore_signal(barrier, inc=1, device_id=peer, device_id_type=MESH)

    loads = [pltpu.make_async_copy(a, b, lsem.at[i]) for i, (a, b) in enumerate(
        ((vol_hbm, vol), (cot_hbm, cot), (w_hbm, wbuf), (b_hbm, bbuf)))]
    for load in loads:
        load.start()

    lane = lax.broadcasted_iota(jnp.int32, (1, 128), 1)
    low = lane < 64
    z_first = (lane % 64) != 0
    z_last = (lane % 64) != 63
    perm = one_hot(256, 256, lambda r, q: q == (r % 16) * 16 + r // 16).astype(BF)

    def turn(src, dst, first, offset):
        for x in range(0, 8, 2):
            parts = [
                jnp.concatenate([src[x + e, :, g * 128:(g + 1) * 128] for g in range(16)], axis=0)
                for e in range(2)
            ]
            out = jnp.dot(perm, jnp.concatenate(parts, axis=1), preferred_element_type=F32).astype(BF)
            dst[first + x, offset:offset + 256] = out[:, :128]
            dst[first + x + 1, offset:offset + 256] = out[:, 128:]

    used = []

    def send(src, dst, peer):
        index = len(used)
        used.append(index)
        copy = pltpu.make_async_remote_copy(
            src_ref=src, dst_ref=dst, send_sem=ssem.at[index], recv_sem=rsem.at[index],
            device_id=peer, device_id_type=MESH)
        copy.start()
        return copy

    def wipe(ref, *shape):
        ref[...] = jnp.zeros(shape, BF)

    loads[0].wait()
    turn(vol, nv, 2, 32)
    if comm:
        pl.semaphore_wait(barrier, len(peers))
        wave1 = [
            send(nv.at[2, 32:288], nv.at[10, 32:288], at(gx - 1, gy)),
            send(nv.at[9, 32:288], nv.at[1, 32:288], at(gx + 1, gy)),
            send(nv.at[2:10, 32:48], nv.at[2:10, 288:304], at(gx, gy - 1)),
            send(nv.at[2:10, 272:288], nv.at[2:10, 16:32], at(gx, gy + 1)),
        ]
        inner_x = {-1: (2, 10), 1: (9, 1)}
        inner_y = {-1: (slice(32, 48), slice(288, 304)), 1: (slice(272, 288), slice(16, 32))}
        for a in (-1, 1):
            for b in (-1, 1):
                wave1.append(send(nv.at[inner_x[a][0], inner_y[b][0]],
                                  nv.at[inner_x[a][1], inner_y[b][1]], at(gx + a, gy + b)))
    loads[1].wait()
    turn(cot, nc, 1, 16)

    def paired(buf, j, r0, r1):
        rows = (r1 - r0) // 16
        a = buf[j, r0:r1]
        b = buf[j + 4, r0:r1]
        even = jnp.where(low, a, pltpu.roll(b, 64, axis=1))
        odd = jnp.where(low, pltpu.roll(a, 64, axis=1), b)
        both = jnp.concatenate(
            [even.reshape(rows, 1, 16, 128), odd.reshape(rows, 1, 16, 128)], axis=1)
        return both.reshape(rows * 32, 128)

    def fill_s(j, y0, y1):
        block = paired(nv, j, y0 * 16, y1 * 16)
        s[1, j, y0 * 32:y1 * 32] = block
        s[0, j, y0 * 32:y1 * 32] = shifted(block, 1, z_first)
        s[2, j, y0 * 32:y1 * 32] = shifted(block, 127, z_last)

    def fill_c(j, y0, y1):
        c[j, y0 * 32:y1 * 32] = paired(nc, j, y0 * 16, y1 * 16)

    @pl.loop(2, 6)
    def _(j):
        fill_s(j, 2, 18)

    @pl.loop(1, 5)
    def _(j):
        fill_c(j, 1, 17)

    def spread(t, kk, base):
        turned = [base] + [pltpu.roll(base, 32 * i, axis=1) for i in (1, 2, 3)]
        zero = jnp.zeros_like(base)
        rows = [(base, zero), (turned[1], zero),
                (jnp.where(lane >= 64, turned[2], zero), jnp.where(lane < 64, turned[2], zero)),
                (jnp.where(lane >= 96, turned[3], zero), jnp.where(lane < 96, turned[3], zero)),
                (zero, base), (zero, turned[1])]
        for yo in range(6):
            for half in range(2):
                t[2 * kk + half, yo * 32:(yo + 1) * 32] = rows[yo][half]

    loads[2].wait()
    loads[3].wait()
    rows4 = one_hot(128, 128, lambda r, q: (r // 32 == q // 32) & (q % 32 == natural(r))).astype(BF)
    lanes1 = one_hot(32, 32, lambda r, q: q == natural(r)).astype(BF)
    stacked = []
    for kk in range(9):
        raw = jnp.concatenate([wbuf[(kk // 3) * 9 + ky * 3 + kk % 3] for ky in range(3)]
                              + [jnp.zeros((32, 32), BF)], axis=0)
        stacked.append(jnp.dot(rows4, raw, preferred_element_type=F32).astype(BF))
        spread(t1, kk, lax.dot_general(lanes1, stacked[kk], NT, preferred_element_type=F32).astype(BF))
    tb[...] = lax.dot_general(
        one_hot(192, 32, lambda r, q: q == natural(r)),
        jnp.broadcast_to(bbuf[...], (128, 32)), NT,
        preferred_element_type=F32, precision=lax.Precision.HIGHEST)

    if comm:
        for copy in wave1:
            copy.wait()

        wave2 = [
            send(nv.at[3, 32:288], nv.at[11, 32:288], at(gx - 1, gy)),
            send(nv.at[8, 32:288], nv.at[0, 32:288], at(gx + 1, gy)),
            send(nv.at[2:10, 48:64], nv.at[2:10, 304:320], at(gx, gy - 1)),
            send(nv.at[2:10, 256:272], nv.at[2:10, 0:16], at(gx, gy + 1)),
        ]
        outer_x = {-1: (3, 11), 1: (8, 0)}
        outer_y = {-1: (slice(48, 64), slice(304, 320)), 1: (slice(256, 272), slice(0, 16))}
        both_y = {-1: (slice(32, 64), slice(288, 320)), 1: (slice(256, 288), slice(0, 32))}
        for a in (-1, 1):
            for b in (-1, 1):
                peer = at(gx + a, gy + b)
                wave2.append(send(nv.at[outer_x[a][0], both_y[b][0]],
                                  nv.at[outer_x[a][1], both_y[b][1]], peer))
                wave2.append(send(nv.at[inner_x[a][0], outer_y[b][0]],
                                  nv.at[inner_x[a][1], outer_y[b][1]], peer))
        side_x = {-1: (slice(1, 2), slice(9, 10)), 0: (slice(1, 9), slice(1, 9)),
                  1: (slice(8, 9), slice(0, 1))}
        side_y = {-1: (slice(16, 32), slice(272, 288)), 0: (slice(16, 272), slice(16, 272)),
                  1: (slice(256, 272), slice(0, 16))}
        for a, b in around:
            wave2.append(send(nc.at[side_x[a][0], side_y[b][0]],
                              nc.at[side_x[a][1], side_y[b][1]], at(gx + a, gy + b)))

        @pl.when(gx == 0)
        def _():
            wipe(nv.at[1, 16:304], 288, 128)

        @pl.when(gx == ngx - 1)
        def _():
            wipe(nv.at[10, 16:304], 288, 128)

        @pl.when(gy == 0)
        def _():
            wipe(nv.at[1:11, 16:32], 10, 16, 128)

        @pl.when(gy == ngy - 1)
        def _():
            wipe(nv.at[1:11, 288:304], 10, 16, 128)
    else:
        wipe(nv.at[0:2], 2, 320, 128)
        wipe(nv.at[10:12], 2, 320, 128)
        wipe(nv.at[:, 0:32], 12, 32, 128)
        wipe(nv.at[:, 288:320], 12, 32, 128)
        wipe(nc.at[0], 288, 128)
        wipe(nc.at[9], 288, 128)
        wipe(nc.at[:, 0:16], 10, 16, 128)
        wipe(nc.at[:, 272:288], 10, 16, 128)

    fill_s(1, 1, 19)
    fill_s(6, 1, 19)
    for j in range(2, 6):
        fill_s(j, 1, 2)
        fill_s(j, 18, 19)

    def tiles(buf, kz, cells, r0, r1):
        return jnp.concatenate([buf[kz, cell, r0:r1] for cell in cells], axis=1)

    def filter_rows(t, r0, r1, halves=(0, 1)):
        return jnp.concatenate([t[2 * kk + h, r0:r1] for kk in range(9) for h in halves], axis=1)

    def activate(acc, r0, r1, cells, y):
        for e, cell in enumerate(cells):
            pre = acc[:, e * 128:(e + 1) * 128] + tb[r0:r1]
            sig = 0.5 * jnp.tanh(0.5 * pre) + 0.5
            grad = c[cell, y:y + r1 - r0].astype(F32)
            gp[1, cell, y:y + r1 - r0] = (grad * sig * (1.0 + pre * (1.0 - sig))).astype(BF)

    def forward(r0, r1, y_in, y_out, cells):
        rhs = jnp.concatenate(
            [tiles(s, kz, [cell + kx for cell in cells], y_in * 32, y_in * 32 + 256)
             for kx in range(3) for kz in range(3)], axis=0)
        acc = jnp.dot(filter_rows(t1, r0, r1), rhs, preferred_element_type=F32)
        activate(acc, r0, r1, cells, y_out * 32)

    @pl.loop(0, 2)
    def _(n):
        cells = (2 * n + 1, 2 * n + 2)
        forward(0, 192, 1, 1, cells)
        forward(0, 192, 7, 7, cells)
        forward(64, 192, 11, 13, cells)

    group = lane // 32

    def gathered(wide, tail, rows):
        cells = []
        for q in range(4):
            step = 32 if rows == 96 else 0
            cell = wide[step * q:step * q + rows, :128] + tail[step * q:step * q + rows, :128]
            if q < 2:
                cell = cell + wide[step * (q + 4):step * (q + 4) + rows, 128:]
            cells.append(cell)
        total = jnp.where(group == 0, cells[0], jnp.where(group == 1, cells[1],
                          jnp.where(group == 2, cells[2], cells[3])))
        total = total + pltpu.roll(total, 64, axis=1)
        return total + pltpu.roll(total, 32, axis=1)

    part[...] = jnp.zeros((8, 32, 128), F32)
    own = range(1, 5)

    def grads():
        wide = jnp.concatenate([tiles(gp, 1, own, 32, 288), tiles(gp, 1, own, 224, 480)], axis=1)
        return wide, tiles(gp, 1, own, 416, 544)

    @pl.loop(0, 3)
    def _(kx):
        right, right_tail = grads()
        for kz in range(3):
            cells = [kx + cell for cell in own]
            left = jnp.concatenate([tiles(s, kz, cells, 32, 288), tiles(s, kz, cells, 224, 480)], axis=1)
            wide = lax.dot_general(left, right, NT, preferred_element_type=F32)
            tail = lax.dot_general(tiles(s, kz, cells, 416, 608), right_tail, NT,
                                   preferred_element_type=F32)
            total = gathered(wide, tail, 96)
            for ky in range(3):
                t = kx * 9 + kz * 3 + ky
                which = lax.div(t, 4)
                part[which] = jnp.where(group == lax.rem(t, 4), total[ky * 32:(ky + 1) * 32],
                                        part[which])

    right, right_tail = grads()
    ones = jnp.ones((16, 1024), BF)
    wide = lax.dot_general(ones, right, NT, preferred_element_type=F32)
    tail = lax.dot_general(ones[:, :512], right_tail, NT, preferred_element_type=F32)
    total = gathered(wide, tail, 16)
    part[6] = jnp.where(group == 3, jnp.concatenate([total, total], axis=0), part[6])

    lower = lax.broadcasted_iota(jnp.int32, (32, 128), 0) >= 16

    def split(value, index):
        rounded = value.astype(BF)
        rest = (value - rounded.astype(F32)).astype(BF)
        return jnp.where((index == 6) & (group == 3) & lower, rest, rounded)

    def joined(value, index):
        both = value + jnp.concatenate([value[16:], value[:16]], axis=0)
        return jnp.where((index == 6) & (group == 3), both, value)

    def later_halo():
        base = sum(jnp.dot(jnp.concatenate([stacked_rows(kk, 2 - d) for kk in range(9)], axis=0),
                           one_hot(32, 128, lambda r, q: (q // 32 == d) & (r == natural(q))).astype(BF),
                           preferred_element_type=F32) for d in range(3)).astype(BF)
        for kk in range(9):
            spread(t2, kk, base[kk * 32:(kk + 1) * 32])

        @pl.loop(1, 5)
        def _(j):
            turn_gp(j, 1, 17)

        if comm:
            for copy in wave2:
                copy.wait()

            @pl.when(gx == 0)
            def _():
                wipe(nv.at[0], 320, 128)
                wipe(nv.at[1, 0:16], 16, 128)
                wipe(nv.at[1, 304:320], 16, 128)
                wipe(nc.at[0], 288, 128)

            @pl.when(gx == ngx - 1)
            def _():
                wipe(nv.at[11], 320, 128)
                wipe(nv.at[10, 0:16], 16, 128)
                wipe(nv.at[10, 304:320], 16, 128)
                wipe(nc.at[9], 288, 128)

            @pl.when(gy == 0)
            def _():
                wipe(nv.at[:, 0:16], 12, 16, 128)
                wipe(nv.at[0, 16:32], 16, 128)
                wipe(nv.at[11, 16:32], 16, 128)
                wipe(nc.at[:, 0:16], 10, 16, 128)

            @pl.when(gy == ngy - 1)
            def _():
                wipe(nv.at[:, 304:320], 12, 16, 128)
                wipe(nv.at[0, 288:304], 16, 128)
                wipe(nv.at[11, 288:304], 16, 128)
                wipe(nc.at[:, 272:288], 10, 16, 128)

        for j in (0, 7):
            fill_s(j, 0, 20)
        for j in range(1, 7):
            fill_s(j, 0, 1)
            fill_s(j, 19, 20)
        for j in (0, 5):
            fill_c(j, 0, 18)
        for j in own:
            fill_c(j, 0, 1)
            fill_c(j, 17, 18)
        for b in range(3):
            forward(0, 192, 6 * b, 6 * b, (0, 5))
        for cells in ((1, 2), (3, 4)):
            for half, y_in, r0, y_out in ((0, 0, 0, 0), (1, 16, 160, 17)):
                rhs = jnp.concatenate(
                    [tiles(s, kz, [cell + kx for cell in cells], y_in * 32, y_in * 32 + 128)
                     for kx in range(3) for kz in range(3)], axis=0)
                acc = jnp.dot(filter_rows(t1, r0, r0 + 32, (half,)), rhs, preferred_element_type=F32)
                activate(acc, r0, r0 + 32, cells, y_out * 32)
        for j in (0, 5):
            turn_gp(j, 0, 18)
        for j in own:
            turn_gp(j, 0, 1)
            turn_gp(j, 17, 18)

    def stacked_rows(kk, ky):
        return stacked[kk][ky * 32:(ky + 1) * 32]

    def turn_gp(j, y0, y1):
        block = gp[1, j, y0 * 32:y1 * 32]
        gp[0, j, y0 * 32:y1 * 32] = shifted(block, 127, z_last)
        gp[2, j, y0 * 32:y1 * 32] = shifted(block, 1, z_first)

    def backward(b):
        start, r0 = ((0, 0), (6, 0), (10, 64))[b]
        left = filter_rows(t2, r0, 192)
        out = start * 32 + r0
        for n in range(2):
            rhs = jnp.concatenate(
                [tiles(gp, kz, (2 * n + 2 - kx, 2 * n + 3 - kx), start * 32, start * 32 + 256)
                 for kx in range(3) for kz in range(3)], axis=0)
            acc = jnp.dot(left, rhs, preferred_element_type=F32).astype(BF)
            dq[2 * n, out:out + 192 - r0] = acc[:, :128]
            dq[2 * n + 1, out:out + 192 - r0] = acc[:, 128:]

    def emit():
        for j in range(4):
            block = dq[j].reshape(16, 2, 16, 128)
            even = block[:, 0].reshape(256, 128)
            odd = block[:, 1].reshape(256, 128)
            first = jnp.where(low, even, pltpu.roll(odd, 64, axis=1))
            second = jnp.where(low, pltpu.roll(even, 64, axis=1), odd)
            out = jnp.dot(perm, jnp.concatenate([first, second], axis=1),
                          preferred_element_type=F32).astype(BF)
            for g in range(16):
                dx[j, :, g * 128:(g + 1) * 128] = out[g * 16:(g + 1) * 16, :128]
                dx[j + 4, :, g * 128:(g + 1) * 128] = out[g * 16:(g + 1) * 16, 128:]

    def summed(buf, count, index):
        total = buf[0].astype(F32)
        for k in range(1, count):
            total = total + buf[k].astype(F32)
        return joined(total, index)

    for i in range(8):
        part16[i] = split(part[i], i) if i == 6 else part[i].astype(BF)
    if comm:
        round1 = [send(part16.at[lax.rem(gx + k + 1, 8)], rs.at[k], gx_peers[k]) for k in range(7)]
        rs[7] = part16[gx]
        later_halo()
        for copy in round1:
            copy.wait()
        xs[xi] = split(summed(rs, 8, gx), gx)
        round2 = [send(xs.at[xi], xs.at[xi], x_peers[k]) for k in range(X_CHIPS - 1)]
        backward(0)
        backward(1)
        for copy in round2:
            copy.wait()
        zs[zi] = split(summed(xs, X_CHIPS, gx), gx)
        round3 = [send(zs.at[zi], zs.at[zi], z_peers[k]) for k in range(Z_CHIPS - 1)]
        backward(2)
        emit()
        for copy in round3:
            copy.wait()
        fin[gx] = split(summed(zs, Z_CHIPS, gx), gx)
        round4 = [send(fin.at[gx], fin.at[gx], gx_peers[k]) for k in range(7)]
        for copy in round4:
            copy.wait()
    else:
        later_halo()
        backward(0)
        backward(1)
        backward(2)
        emit()
        for i in range(8):
            fin[i] = part16[i]


def finish(scale, dx, fin, dx_hbm, df_hbm, db_hbm, df, db, sem):
    out = pltpu.make_async_copy(dx, dx_hbm, sem.at[0])
    out.start()
    swap = one_hot(128, 128, lambda r, q: r == (q // 32) * 32 + (q % 2) * 16 + (q % 32) // 2).astype(BF)
    final = jnp.dot(fin[...].reshape(256, 128), swap, preferred_element_type=F32) * scale
    for t in range(27):
        block = final[(t // 4) * 32:(t // 4) * 32 + 32]
        if t % 4:
            block = pltpu.roll(block, 128 - 32 * (t % 4), axis=1)
        k = (t // 9) * 9 + (t % 3) * 3 + (t // 3) % 3
        df[k, pl.ds(0, 16, stride=2), :] = block[0:16, 0:32]
        df[k, pl.ds(1, 16, stride=2), :] = block[16:32, 0:32]
    db[...] = pltpu.roll(final[192:200] + final[208:216], 32, axis=1)[0:1, 0:32]
    others = [pltpu.make_async_copy(df, df_hbm, sem.at[1]), pltpu.make_async_copy(db, db_hbm, sem.at[2])]
    for copy in others:
        copy.start()
    for copy in [out] + others:
        copy.wait()


def shards(comm, cells, volume, cotangent, weight, bias):
    vm = pl.BlockSpec(memory_space=pltpu.VMEM)
    hbm = pl.BlockSpec(memory_space=pltpu.MemorySpace.HBM)
    inputs = (volume, cotangent, weight.reshape(27, C, C), bias.reshape(1, C))
    if comm:
        inputs = [pltpu.with_memory_space_constraint(a, pltpu.MemorySpace.HBM) for a in inputs]
    dx, fin = pl.pallas_call(
        functools.partial(kernel, comm),
        out_shape=(jax.ShapeDtypeStruct(volume.shape, BF), jax.ShapeDtypeStruct((8, 32, 128), BF)),
        in_specs=[hbm] * 4,
        out_specs=(vm, vm),
        scratch_shapes=[
            pltpu.VMEM((8, 16, 2048), BF),
            pltpu.VMEM((8, 16, 2048), BF),
            pltpu.VMEM((27, C, C), BF),
            pltpu.VMEM((1, C), F32),
            pltpu.VMEM((12, 320, 128), BF),
            pltpu.VMEM((10, 288, 128), BF),
            pltpu.VMEM((3, 8, 640, 128), BF),
            pltpu.VMEM((6, 576, 128), BF),
            pltpu.VMEM((3, 6, 576, 128), BF),
            pltpu.VMEM((18, 192, 128), BF),
            pltpu.VMEM((18, 192, 128), BF),
            pltpu.VMEM((192, 128), F32),
            pltpu.VMEM((4, 512, 128), BF),
            pltpu.VMEM((8, 32, 128), F32),
            pltpu.VMEM((8, 32, 128), BF),
            pltpu.VMEM((8, 32, 128), BF),
            pltpu.VMEM((X_CHIPS, 32, 128), BF),
            pltpu.VMEM((Z_CHIPS, 32, 128), BF),
            pltpu.SemaphoreType.DMA((52,)),
            pltpu.SemaphoreType.DMA((52,)),
            pltpu.SemaphoreType.DMA((4,)),
        ],
        compiler_params=pltpu.CompilerParams(
            collective_id=0 if comm else None, has_side_effects=comm, vmem_limit_bytes=48 << 20),
    )(*inputs)
    dg, df, db = pl.pallas_call(
        functools.partial(finish, 1.0 / math.sqrt(cells)),
        out_shape=(jax.ShapeDtypeStruct(volume.shape, BF),
                   jax.ShapeDtypeStruct((27, C, C), F32),
                   jax.ShapeDtypeStruct((1, C), F32)),
        in_specs=[vm, vm],
        out_specs=[pl.BlockSpec(memory_space=pl.ANY)] * 3,
        scratch_shapes=[pltpu.VMEM((27, C, C), F32), pltpu.VMEM((1, C), F32),
                        pltpu.SemaphoreType.DMA((3,))],
        compiler_params=pltpu.CompilerParams(vmem_limit_bytes=4 << 20),
    )(dx, fin)
    return dg, df.reshape(3, 3, 3, C, C), db.reshape(C)


def solution(mesh):
    cells = 8 * mesh.shape["gx"] * 16 * mesh.shape["gy"] * 64
    in_specs = (P("gx", "gy", None), P("gx", "gy", None), P(), P())
    out_specs = (P("gx", "gy", None), P(), P())
    return jax.shard_map(functools.partial(shards, True, cells), mesh=mesh, in_specs=in_specs,
                         out_specs=out_specs, check_vma=False)
```

```python
import functools
import math

import jax
import jax.numpy as jnp
from jax import lax
from jax.experimental import pallas as pl
from jax.experimental.pallas import tpu as pltpu
from jax.sharding import PartitionSpec as P

C = 32
MESH = pl.DeviceIdType.MESH
BF = jnp.bfloat16
F32 = jnp.float32
X_CHIPS = 4
Z_CHIPS = 8
NT = (((1,), (1,)), ((), ()))


def shifted(block, amount, keep):
    return jnp.where(keep, pltpu.roll(block, amount, axis=1), jnp.zeros_like(block))


def natural(index):
    return 2 * (index % 16) + (index % 32) // 16


def one_hot(rows, cols, test):
    row = lax.broadcasted_iota(jnp.int32, (rows, cols), 0)
    col = lax.broadcasted_iota(jnp.int32, (rows, cols), 1)
    return jnp.where(test(row, col), 1.0, 0.0)


def kernel(comm, vol_hbm, cot_hbm, w_hbm, b_hbm, dx, fin, vol, cot, wbuf, bbuf, nv, nc,
           s, c, gp, t1, t2, tb, dq, part16, rs, xs, zs, ssem, rsem, lsem):
    loads = [pltpu.make_async_copy(a, b, lsem.at[i]) for i, (a, b) in enumerate(
        ((vol_hbm, vol), (cot_hbm, cot), (w_hbm, wbuf), (b_hbm, bbuf)))]
    for load in loads:
        load.start()

    if comm:
        gx = lax.axis_index("gx")
        gy = lax.axis_index("gy")
        ngx = lax.axis_size("gx")
        ngy = lax.axis_size("gy")
        xi = lax.rem(gy, X_CHIPS)
        zi = lax.div(gy, X_CHIPS)

        def at(ax, ay):
            return {"gx": lax.rem(ax + ngx, ngx), "gy": lax.rem(ay + ngy, ngy)}

        around = [(a, b) for a in (-1, 0, 1) for b in (-1, 0, 1) if a or b]
        gx_peers = [at(gx + k, gy) for k in range(1, 8)]
        x_peers = [at(gx, zi * X_CHIPS + lax.rem(xi + k, X_CHIPS)) for k in range(1, X_CHIPS)]
        z_peers = [at(gx, lax.rem(zi + k, Z_CHIPS) * X_CHIPS + xi) for k in range(1, Z_CHIPS)]
        peers = z_peers + [at(gx + a, gy + b) for a, b in around if b] + gx_peers + x_peers
        barrier = pltpu.get_barrier_semaphore()
        for peer in peers:
            pl.semaphore_signal(barrier, inc=1, device_id=peer, device_id_type=MESH)


    lane = lax.broadcasted_iota(jnp.int32, (1, 128), 1)
    low = lane < 64
    z_first = (lane % 64) != 0
    z_last = (lane % 64) != 63
    perm = one_hot(256, 256, lambda r, q: q == (r % 16) * 16 + r // 16).astype(BF)

    def turn(src, dst, first, offset):
        for x in range(0, 8, 2):
            parts = [
                jnp.concatenate([src[x + e, :, g * 128:(g + 1) * 128] for g in range(16)], axis=0)
                for e in range(2)
            ]
            out = jnp.dot(perm, jnp.concatenate(parts, axis=1), preferred_element_type=F32).astype(BF)
            dst[first + x, offset:offset + 256] = out[:, :128]
            dst[first + x + 1, offset:offset + 256] = out[:, 128:]

    used = []

    def send(src, dst, peer):
        index = len(used)
        used.append(index)
        copy = pltpu.make_async_remote_copy(
            src_ref=src, dst_ref=dst, send_sem=ssem.at[index], recv_sem=rsem.at[index],
            device_id=peer, device_id_type=MESH)
        copy.start()
        return copy

    def wipe(ref, *shape):
        ref[...] = jnp.zeros(shape, BF)

    loads[0].wait()
    turn(vol, nv, 2, 32)
    if comm:
        pl.semaphore_wait(barrier, len(peers))
        wave1 = [
            send(nv.at[2, 32:288], nv.at[10, 32:288], at(gx - 1, gy)),
            send(nv.at[9, 32:288], nv.at[1, 32:288], at(gx + 1, gy)),
            send(nv.at[2:10, 32:48], nv.at[2:10, 288:304], at(gx, gy - 1)),
            send(nv.at[2:10, 272:288], nv.at[2:10, 16:32], at(gx, gy + 1)),
        ]
        inner_x = {-1: (2, 10), 1: (9, 1)}
        inner_y = {-1: (slice(32, 48), slice(288, 304)), 1: (slice(272, 288), slice(16, 32))}
        for a in (-1, 1):
            for b in (-1, 1):
                wave1.append(send(nv.at[inner_x[a][0], inner_y[b][0]],
                                  nv.at[inner_x[a][1], inner_y[b][1]], at(gx + a, gy + b)))
    loads[1].wait()
    turn(cot, nc, 1, 16)

    def paired(buf, j, r0, r1):
        rows = (r1 - r0) // 16
        a = buf[j, r0:r1]
        b = buf[j + 4, r0:r1]
        even = jnp.where(low, a, pltpu.roll(b, 64, axis=1))
        odd = jnp.where(low, pltpu.roll(a, 64, axis=1), b)
        both = jnp.concatenate(
            [even.reshape(rows, 1, 16, 128), odd.reshape(rows, 1, 16, 128)], axis=1)
        return both.reshape(rows * 32, 128)

    def fill_s(j, y0, y1):
        block = paired(nv, j, y0 * 16, y1 * 16)
        s[1, j, y0 * 32:y1 * 32] = block
        s[0, j, y0 * 32:y1 * 32] = shifted(block, 1, z_first)
        s[2, j, y0 * 32:y1 * 32] = shifted(block, 127, z_last)

    def fill_c(j, y0, y1):
        c[j, y0 * 32:y1 * 32] = paired(nc, j, y0 * 16, y1 * 16)

    @pl.loop(2, 6)
    def _(j):
        fill_s(j, 2, 18)

    @pl.loop(1, 5)
    def _(j):
        fill_c(j, 1, 17)

    def spread(t, kk, base):
        turned = [base] + [pltpu.roll(base, 32 * i, axis=1) for i in (1, 2, 3)]
        zero = jnp.zeros_like(base)
        rows = [(base, zero), (turned[1], zero),
                (jnp.where(lane >= 64, turned[2], zero), jnp.where(lane < 64, turned[2], zero)),
                (jnp.where(lane >= 96, turned[3], zero), jnp.where(lane < 96, turned[3], zero)),
                (zero, base), (zero, turned[1])]
        for yo in range(6):
            for half in range(2):
                t[2 * kk + half, yo * 32:(yo + 1) * 32] = rows[yo][half]

    loads[2].wait()
    loads[3].wait()
    rows4 = one_hot(128, 128, lambda r, q: (r // 32 == q // 32) & (q % 32 == natural(r))).astype(BF)
    lanes1 = one_hot(32, 32, lambda r, q: q == natural(r)).astype(BF)
    stacked = []
    for kk in range(9):
        raw = jnp.concatenate([wbuf[(kk // 3) * 9 + ky * 3 + kk % 3] for ky in range(3)]
                              + [jnp.zeros((32, 32), BF)], axis=0)
        stacked.append(jnp.dot(rows4, raw, preferred_element_type=F32).astype(BF))
        spread(t1, kk, lax.dot_general(lanes1, stacked[kk], NT, preferred_element_type=F32).astype(BF))
    tb[...] = lax.dot_general(
        one_hot(192, 32, lambda r, q: q == natural(r)),
        jnp.broadcast_to(bbuf[...], (128, 32)), NT,
        preferred_element_type=F32, precision=lax.Precision.HIGHEST)

    if comm:
        for copy in wave1:
            copy.wait()

        wave2 = [
            send(nv.at[3, 32:288], nv.at[11, 32:288], at(gx - 1, gy)),
            send(nv.at[8, 32:288], nv.at[0, 32:288], at(gx + 1, gy)),
            send(nv.at[2:10, 48:64], nv.at[2:10, 304:320], at(gx, gy - 1)),
            send(nv.at[2:10, 256:272], nv.at[2:10, 0:16], at(gx, gy + 1)),
        ]
        outer_x = {-1: (3, 11), 1: (8, 0)}
        outer_y = {-1: (slice(48, 64), slice(304, 320)), 1: (slice(256, 272), slice(0, 16))}
        both_y = {-1: (slice(32, 64), slice(288, 320)), 1: (slice(256, 288), slice(0, 32))}
        for a in (-1, 1):
            for b in (-1, 1):
                peer = at(gx + a, gy + b)
                wave2.append(send(nv.at[outer_x[a][0], both_y[b][0]],
                                  nv.at[outer_x[a][1], both_y[b][1]], peer))
                wave2.append(send(nv.at[inner_x[a][0], outer_y[b][0]],
                                  nv.at[inner_x[a][1], outer_y[b][1]], peer))
        side_x = {-1: (slice(1, 2), slice(9, 10)), 0: (slice(1, 9), slice(1, 9)),
                  1: (slice(8, 9), slice(0, 1))}
        side_y = {-1: (slice(16, 32), slice(272, 288)), 0: (slice(16, 272), slice(16, 272)),
                  1: (slice(256, 272), slice(0, 16))}
        for a, b in around:
            wave2.append(send(nc.at[side_x[a][0], side_y[b][0]],
                              nc.at[side_x[a][1], side_y[b][1]], at(gx + a, gy + b)))

        @pl.when(gx == 0)
        def _():
            wipe(nv.at[1, 16:304], 288, 128)

        @pl.when(gx == ngx - 1)
        def _():
            wipe(nv.at[10, 16:304], 288, 128)

        @pl.when(gy == 0)
        def _():
            wipe(nv.at[1:11, 16:32], 10, 16, 128)

        @pl.when(gy == ngy - 1)
        def _():
            wipe(nv.at[1:11, 288:304], 10, 16, 128)
    else:
        wipe(nv.at[0:2], 2, 320, 128)
        wipe(nv.at[10:12], 2, 320, 128)
        wipe(nv.at[:, 0:32], 12, 32, 128)
        wipe(nv.at[:, 288:320], 12, 32, 128)
        wipe(nc.at[0], 288, 128)
        wipe(nc.at[9], 288, 128)
        wipe(nc.at[:, 0:16], 10, 16, 128)
        wipe(nc.at[:, 272:288], 10, 16, 128)

    fill_s(1, 1, 19)
    fill_s(6, 1, 19)
    for j in range(2, 6):
        fill_s(j, 1, 2)
        fill_s(j, 18, 19)

    def tiles(buf, kz, cells, r0, r1):
        return jnp.concatenate([buf[kz, cell, r0:r1] for cell in cells], axis=1)

    def filter_rows(t, r0, r1, halves=(0, 1)):
        return jnp.concatenate([t[2 * kk + h, r0:r1] for kk in range(9) for h in halves], axis=1)

    def activate(acc, r0, r1, cells, y):
        for e, cell in enumerate(cells):
            pre = acc[:, e * 128:(e + 1) * 128] + tb[r0:r1]
            sig = 0.5 * jnp.tanh(0.5 * pre) + 0.5
            grad = c[cell, y:y + r1 - r0].astype(F32)
            gp[1, cell, y:y + r1 - r0] = (grad * sig * (1.0 + pre * (1.0 - sig))).astype(BF)

    def forward(r0, r1, y_in, y_out, cells):
        rhs = jnp.concatenate(
            [tiles(s, kz, [cell + kx for cell in cells], y_in * 32, y_in * 32 + 256)
             for kx in range(3) for kz in range(3)], axis=0)
        acc = jnp.dot(filter_rows(t1, r0, r1), rhs, preferred_element_type=F32)
        activate(acc, r0, r1, cells, y_out * 32)

    for n in range(2):
        cells = (2 * n + 1, 2 * n + 2)
        forward(0, 192, 1, 1, cells)
        forward(0, 192, 7, 7, cells)
        forward(64, 192, 11, 13, cells)

    group = lane // 32

    def gathered(wide, rows, step):
        cells = [wide[step * q:step * q + rows, :128] + wide[step * (q + 4):step * (q + 4) + rows, 128:]
                 for q in range(4)]
        total = jnp.where(group == 0, cells[0], jnp.where(group == 1, cells[1],
                          jnp.where(group == 2, cells[2], cells[3])))
        total = total + pltpu.roll(total, 64, axis=1)
        return total + pltpu.roll(total, 32, axis=1)

    lower = lax.broadcasted_iota(jnp.int32, (32, 128), 0) >= 16

    def split(value, index):
        rounded = value.astype(BF)
        rest = (value - rounded.astype(F32)).astype(BF)
        return jnp.where((index == 6) & (group == 3) & lower, rest, rounded)

    def joined(value, index):
        both = value + jnp.concatenate([value[16:], value[:16]], axis=0)
        return jnp.where((index == 6) & (group == 3), both, value)

    done = []

    def put(four):
        value = jnp.where(group == 0, four[0], jnp.where(group == 1, four[1],
                          jnp.where(group == 2, four[2], four[3])))
        part16[len(done)] = split(value, len(done)) if len(done) == 6 else value.astype(BF)
        done.append(0)

    own = range(1, 5)
    right = jnp.concatenate([tiles(gp, 1, own, 32, 288), tiles(gp, 1, own, 288, 544)], axis=1)
    blocks = []
    for kx in range(3):
        for kz in range(3):
            cells = [kx + cell for cell in own]
            left = jnp.concatenate([tiles(s, kz, cells, 32, 352), tiles(s, kz, cells, 288, 608)], axis=1)
            wide = lax.dot_general(left, right, NT, preferred_element_type=F32)
            total = gathered(wide, 96, 32)
            blocks += [total[ky * 32:(ky + 1) * 32] for ky in range(3)]
            while len(blocks) >= 4:
                put(blocks[:4])
                blocks = blocks[4:]
    wide = lax.dot_general(jnp.ones((16, 1024), BF), right, NT, preferred_element_type=F32)
    total = gathered(wide, 16, 0)
    put(blocks + [jnp.concatenate([total, total], axis=0)])
    part16[7] = jnp.zeros((32, 128), BF)

    def later_halo():
        base = sum(jnp.dot(jnp.concatenate([stacked_rows(kk, 2 - d) for kk in range(9)], axis=0),
                           one_hot(32, 128, lambda r, q: (q // 32 == d) & (r == natural(q))).astype(BF),
                           preferred_element_type=F32) for d in range(3)).astype(BF)
        for kk in range(9):
            spread(t2, kk, base[kk * 32:(kk + 1) * 32])

        @pl.loop(1, 5)
        def _(j):
            turn_gp(j, 1, 17)

        if comm:
            for copy in wave2:
                copy.wait()

            @pl.when(gx == 0)
            def _():
                wipe(nv.at[0], 320, 128)
                wipe(nv.at[1, 0:16], 16, 128)
                wipe(nv.at[1, 304:320], 16, 128)
                wipe(nc.at[0], 288, 128)

            @pl.when(gx == ngx - 1)
            def _():
                wipe(nv.at[11], 320, 128)
                wipe(nv.at[10, 0:16], 16, 128)
                wipe(nv.at[10, 304:320], 16, 128)
                wipe(nc.at[9], 288, 128)

            @pl.when(gy == 0)
            def _():
                wipe(nv.at[:, 0:16], 12, 16, 128)
                wipe(nv.at[0, 16:32], 16, 128)
                wipe(nv.at[11, 16:32], 16, 128)
                wipe(nc.at[:, 0:16], 10, 16, 128)

            @pl.when(gy == ngy - 1)
            def _():
                wipe(nv.at[:, 304:320], 12, 16, 128)
                wipe(nv.at[0, 288:304], 16, 128)
                wipe(nv.at[11, 288:304], 16, 128)
                wipe(nc.at[:, 272:288], 10, 16, 128)

        for j in (0, 7):
            fill_s(j, 0, 20)
        for j in range(1, 7):
            fill_s(j, 0, 1)
            fill_s(j, 19, 20)
        for j in (0, 5):
            fill_c(j, 0, 18)
        for j in own:
            fill_c(j, 0, 1)
            fill_c(j, 17, 18)
        for b in range(3):
            forward(0, 192, 6 * b, 6 * b, (0, 5))
        for cells in ((1, 2), (3, 4)):
            for half, y_in, r0, y_out in ((0, 0, 0, 0), (1, 16, 160, 17)):
                rhs = jnp.concatenate(
                    [tiles(s, kz, [cell + kx for cell in cells], y_in * 32, y_in * 32 + 128)
                     for kx in range(3) for kz in range(3)], axis=0)
                acc = jnp.dot(filter_rows(t1, r0, r0 + 32, (half,)), rhs, preferred_element_type=F32)
                activate(acc, r0, r0 + 32, cells, y_out * 32)
        for j in (0, 5):
            turn_gp(j, 0, 18)
        for j in own:
            turn_gp(j, 0, 1)
            turn_gp(j, 17, 18)

    def stacked_rows(kk, ky):
        return stacked[kk][ky * 32:(ky + 1) * 32]

    def turn_gp(j, y0, y1):
        block = gp[1, j, y0 * 32:y1 * 32]
        gp[0, j, y0 * 32:y1 * 32] = shifted(block, 127, z_last)
        gp[2, j, y0 * 32:y1 * 32] = shifted(block, 1, z_first)

    def backward(b):
        start, r0 = ((0, 0), (6, 0), (10, 64))[b]
        left = filter_rows(t2, r0, 192)
        out = start * 32 + r0
        for n in range(2):
            rhs = jnp.concatenate(
                [tiles(gp, kz, (2 * n + 2 - kx, 2 * n + 3 - kx), start * 32, start * 32 + 256)
                 for kx in range(3) for kz in range(3)], axis=0)
            acc = jnp.dot(left, rhs, preferred_element_type=F32).astype(BF)
            dq[2 * n, out:out + 192 - r0] = acc[:, :128]
            dq[2 * n + 1, out:out + 192 - r0] = acc[:, 128:]

    def emit():
        for j in range(4):
            block = dq[j].reshape(16, 2, 16, 128)
            even = block[:, 0].reshape(256, 128)
            odd = block[:, 1].reshape(256, 128)
            first = jnp.where(low, even, pltpu.roll(odd, 64, axis=1))
            second = jnp.where(low, pltpu.roll(even, 64, axis=1), odd)
            out = jnp.dot(perm, jnp.concatenate([first, second], axis=1),
                          preferred_element_type=F32).astype(BF)
            for g in range(16):
                dx[j, :, g * 128:(g + 1) * 128] = out[g * 16:(g + 1) * 16, :128]
                dx[j + 4, :, g * 128:(g + 1) * 128] = out[g * 16:(g + 1) * 16, 128:]

    def summed(buf, count, index):
        total = buf[0].astype(F32)
        for k in range(1, count):
            total = total + buf[k].astype(F32)
        return joined(total, index)

    if comm:
        round1 = [send(part16.at[lax.rem(gx + k + 1, 8)], rs.at[k], gx_peers[k]) for k in range(7)]
        rs[7] = part16[gx]
        later_halo()
        for copy in round1:
            copy.wait()
        xs[xi] = split(summed(rs, 8, gx), gx)
        round2 = [send(xs.at[xi], xs.at[xi], x_peers[k]) for k in range(X_CHIPS - 1)]
        backward(0)
        backward(1)
        for copy in round2:
            copy.wait()
        zs[zi] = split(summed(xs, X_CHIPS, gx), gx)
        round3 = [send(zs.at[zi], zs.at[zi], z_peers[k]) for k in range(Z_CHIPS - 1)]
        backward(2)
        emit()
        for copy in round3:
            copy.wait()
        fin[gx] = split(summed(zs, Z_CHIPS, gx), gx)
        round4 = [send(fin.at[gx], fin.at[gx], gx_peers[k]) for k in range(7)]
        for copy in round4:
            copy.wait()
    else:
        later_halo()
        backward(0)
        backward(1)
        backward(2)
        emit()
        for i in range(8):
            fin[i] = part16[i]


def finish(scale, dx, fin, dx_hbm, df_hbm, db_hbm, df, db, sem):
    out = pltpu.make_async_copy(dx, dx_hbm, sem.at[0])
    out.start()
    swap = one_hot(128, 128, lambda r, q: r == (q // 32) * 32 + (q % 2) * 16 + (q % 32) // 2).astype(BF)
    final = jnp.dot(fin[...].reshape(256, 128), swap, preferred_element_type=F32) * scale
    for t in range(27):
        block = final[(t // 4) * 32:(t // 4) * 32 + 32]
        if t % 4:
            block = pltpu.roll(block, 128 - 32 * (t % 4), axis=1)
        k = (t // 9) * 9 + (t % 3) * 3 + (t // 3) % 3
        df[k, pl.ds(0, 16, stride=2), :] = block[0:16, 0:32]
        df[k, pl.ds(1, 16, stride=2), :] = block[16:32, 0:32]
    db[...] = pltpu.roll(final[192:200] + final[208:216], 32, axis=1)[0:1, 0:32]
    others = [pltpu.make_async_copy(df, df_hbm, sem.at[1]), pltpu.make_async_copy(db, db_hbm, sem.at[2])]
    for copy in others:
        copy.start()
    for copy in [out] + others:
        copy.wait()


def shards(comm, cells, volume, cotangent, weight, bias):
    vm = pl.BlockSpec(memory_space=pltpu.VMEM)
    hbm = pl.BlockSpec(memory_space=pltpu.MemorySpace.HBM)
    inputs = (volume, cotangent, weight.reshape(27, C, C), bias.reshape(1, C))
    if comm:
        inputs = [pltpu.with_memory_space_constraint(a, pltpu.MemorySpace.HBM) for a in inputs]
    dx, fin = pl.pallas_call(
        functools.partial(kernel, comm),
        out_shape=(jax.ShapeDtypeStruct(volume.shape, BF), jax.ShapeDtypeStruct((8, 32, 128), BF)),
        in_specs=[hbm] * 4,
        out_specs=(vm, vm),
        scratch_shapes=[
            pltpu.VMEM((8, 16, 2048), BF),
            pltpu.VMEM((8, 16, 2048), BF),
            pltpu.VMEM((27, C, C), BF),
            pltpu.VMEM((1, C), F32),
            pltpu.VMEM((12, 320, 128), BF),
            pltpu.VMEM((10, 288, 128), BF),
            pltpu.VMEM((3, 8, 640, 128), BF),
            pltpu.VMEM((6, 576, 128), BF),
            pltpu.VMEM((3, 6, 576, 128), BF),
            pltpu.VMEM((18, 192, 128), BF),
            pltpu.VMEM((18, 192, 128), BF),
            pltpu.VMEM((192, 128), F32),
            pltpu.VMEM((4, 512, 128), BF),
            pltpu.VMEM((8, 32, 128), BF),
            pltpu.VMEM((8, 32, 128), BF),
            pltpu.VMEM((X_CHIPS, 32, 128), BF),
            pltpu.VMEM((Z_CHIPS, 32, 128), BF),
            pltpu.SemaphoreType.DMA((52,)),
            pltpu.SemaphoreType.DMA((52,)),
            pltpu.SemaphoreType.DMA((4,)),
        ],
        compiler_params=pltpu.CompilerParams(
            collective_id=0 if comm else None, has_side_effects=comm, vmem_limit_bytes=48 << 20),
    )(*inputs)
    dg, df, db = pl.pallas_call(
        functools.partial(finish, 1.0 / math.sqrt(cells)),
        out_shape=(jax.ShapeDtypeStruct(volume.shape, BF),
                   jax.ShapeDtypeStruct((27, C, C), F32),
                   jax.ShapeDtypeStruct((1, C), F32)),
        in_specs=[vm, vm],
        out_specs=[pl.BlockSpec(memory_space=pl.ANY)] * 3,
        scratch_shapes=[pltpu.VMEM((27, C, C), F32), pltpu.VMEM((1, C), F32),
                        pltpu.SemaphoreType.DMA((3,))],
        compiler_params=pltpu.CompilerParams(vmem_limit_bytes=4 << 20),
    )(dx, fin)
    return dg, df.reshape(3, 3, 3, C, C), db.reshape(C)


def solution(mesh):
    cells = 8 * mesh.shape["gx"] * 16 * mesh.shape["gy"] * 64
    in_specs = (P("gx", "gy", None), P("gx", "gy", None), P(), P())
    out_specs = (P("gx", "gy", None), P(), P())
    return jax.shard_map(functools.partial(shards, True, cells), mesh=mesh, in_specs=in_specs,
                         out_specs=out_specs, check_vma=False)
```

```python
import functools
import math

import jax
import jax.numpy as jnp
from jax import lax
from jax.experimental import pallas as pl
from jax.experimental.pallas import tpu as pltpu
from jax.sharding import PartitionSpec as P

C = 32
MESH = pl.DeviceIdType.MESH
BF = jnp.bfloat16
F32 = jnp.float32
X_CHIPS = 4
Z_CHIPS = 8
NT = (((1,), (1,)), ((), ()))


def shifted(block, amount, keep):
    return jnp.where(keep, pltpu.roll(block, amount, axis=1), jnp.zeros_like(block))


def natural(index):
    return 2 * (index % 16) + (index % 32) // 16


def one_hot(rows, cols, test):
    row = lax.broadcasted_iota(jnp.int32, (rows, cols), 0)
    col = lax.broadcasted_iota(jnp.int32, (rows, cols), 1)
    return jnp.where(test(row, col), 1.0, 0.0)


def kernel(comm, vol_hbm, cot_hbm, w_hbm, b_hbm, dx, fin, vol, cot, wbuf, bbuf, nv, nc,
           s, c, gp, t1, t2, tb, dq, part, rs, xs, zs, ssem, rsem, lsem):
    loads = [pltpu.make_async_copy(a, b, lsem.at[i]) for i, (a, b) in enumerate(
        ((vol_hbm, vol), (cot_hbm, cot), (w_hbm, wbuf), (b_hbm, bbuf)))]
    for load in loads:
        load.start()

    if comm:
        gx = lax.axis_index("gx")
        gy = lax.axis_index("gy")
        ngx = lax.axis_size("gx")
        ngy = lax.axis_size("gy")
        xi = lax.rem(gy, X_CHIPS)
        zi = lax.div(gy, X_CHIPS)

        def at(ax, ay):
            return {"gx": lax.rem(ax + ngx, ngx), "gy": lax.rem(ay + ngy, ngy)}

        around = [(a, b) for a in (-1, 0, 1) for b in (-1, 0, 1) if a or b]
        gx_peers = [at(gx + k, gy) for k in range(1, 8)]
        x_peers = [at(gx, zi * X_CHIPS + lax.rem(xi + k, X_CHIPS)) for k in range(1, X_CHIPS)]
        z_peers = [at(gx, lax.rem(zi + k, Z_CHIPS) * X_CHIPS + xi) for k in range(1, Z_CHIPS)]
        peers = z_peers + [at(gx + a, gy + b) for a, b in around if b] + gx_peers + x_peers
        barrier = pltpu.get_barrier_semaphore()
        for peer in peers:
            pl.semaphore_signal(barrier, inc=1, device_id=peer, device_id_type=MESH)


    lane = lax.broadcasted_iota(jnp.int32, (1, 128), 1)
    low = lane < 64
    z_first = (lane % 64) != 0
    z_last = (lane % 64) != 63
    perm = one_hot(256, 256, lambda r, q: q == (r % 16) * 16 + r // 16).astype(BF)

    def turn(src, dst, first, offset):
        for x in range(0, 8, 2):
            parts = [
                jnp.concatenate([src[x + e, :, g * 128:(g + 1) * 128] for g in range(16)], axis=0)
                for e in range(2)
            ]
            out = jnp.dot(perm, jnp.concatenate(parts, axis=1), preferred_element_type=F32).astype(BF)
            dst[first + x, offset:offset + 256] = out[:, :128]
            dst[first + x + 1, offset:offset + 256] = out[:, 128:]

    used = []

    def send(src, dst, peer):
        index = len(used)
        used.append(index)
        copy = pltpu.make_async_remote_copy(
            src_ref=src, dst_ref=dst, send_sem=ssem.at[index], recv_sem=rsem.at[index],
            device_id=peer, device_id_type=MESH)
        copy.start()
        return copy

    def wipe(ref, *shape):
        ref[...] = jnp.zeros(shape, BF)

    loads[0].wait()
    turn(vol, nv, 2, 32)
    if comm:
        pl.semaphore_wait(barrier, len(peers))
        wave1 = [
            send(nv.at[2, 32:288], nv.at[10, 32:288], at(gx - 1, gy)),
            send(nv.at[9, 32:288], nv.at[1, 32:288], at(gx + 1, gy)),
            send(nv.at[2:10, 32:48], nv.at[2:10, 288:304], at(gx, gy - 1)),
            send(nv.at[2:10, 272:288], nv.at[2:10, 16:32], at(gx, gy + 1)),
        ]
        inner_x = {-1: (2, 10), 1: (9, 1)}
        inner_y = {-1: (slice(32, 48), slice(288, 304)), 1: (slice(272, 288), slice(16, 32))}
        for a in (-1, 1):
            for b in (-1, 1):
                wave1.append(send(nv.at[inner_x[a][0], inner_y[b][0]],
                                  nv.at[inner_x[a][1], inner_y[b][1]], at(gx + a, gy + b)))
    loads[1].wait()
    turn(cot, nc, 1, 16)

    def paired(buf, j, r0, r1):
        rows = (r1 - r0) // 16
        a = buf[j, r0:r1]
        b = buf[j + 4, r0:r1]
        even = jnp.where(low, a, pltpu.roll(b, 64, axis=1))
        odd = jnp.where(low, pltpu.roll(a, 64, axis=1), b)
        both = jnp.concatenate(
            [even.reshape(rows, 1, 16, 128), odd.reshape(rows, 1, 16, 128)], axis=1)
        return both.reshape(rows * 32, 128)

    def fill_s(j, y0, y1):
        block = paired(nv, j, y0 * 16, y1 * 16)
        s[1, j, y0 * 32:y1 * 32] = block
        s[0, j, y0 * 32:y1 * 32] = shifted(block, 1, z_first)
        s[2, j, y0 * 32:y1 * 32] = shifted(block, 127, z_last)

    def fill_c(j, y0, y1):
        c[j, y0 * 32:y1 * 32] = paired(nc, j, y0 * 16, y1 * 16)

    @pl.loop(2, 6)
    def _(j):
        fill_s(j, 2, 18)

    @pl.loop(1, 5)
    def _(j):
        fill_c(j, 1, 17)

    def spread(t, kk, base):
        turned = [base] + [pltpu.roll(base, 32 * i, axis=1) for i in (1, 2, 3)]
        zero = jnp.zeros_like(base)
        rows = [(base, zero), (turned[1], zero),
                (jnp.where(lane >= 64, turned[2], zero), jnp.where(lane < 64, turned[2], zero)),
                (jnp.where(lane >= 96, turned[3], zero), jnp.where(lane < 96, turned[3], zero)),
                (zero, base), (zero, turned[1])]
        for yo in range(6):
            for half in range(2):
                t[2 * kk + half, yo * 32:(yo + 1) * 32] = rows[yo][half]

    loads[2].wait()
    loads[3].wait()
    rows4 = one_hot(128, 128, lambda r, q: (r // 32 == q // 32) & (q % 32 == natural(r))).astype(BF)
    lanes1 = one_hot(32, 32, lambda r, q: q == natural(r)).astype(BF)
    stacked = []
    for kk in range(9):
        raw = jnp.concatenate([wbuf[(kk // 3) * 9 + ky * 3 + kk % 3] for ky in range(3)]
                              + [jnp.zeros((32, 32), BF)], axis=0)
        stacked.append(jnp.dot(rows4, raw, preferred_element_type=F32).astype(BF))
        spread(t1, kk, lax.dot_general(lanes1, stacked[kk], NT, preferred_element_type=F32).astype(BF))
    tb[...] = lax.dot_general(
        one_hot(192, 32, lambda r, q: q == natural(r)),
        jnp.broadcast_to(bbuf[...], (128, 32)), NT,
        preferred_element_type=F32, precision=lax.Precision.HIGHEST)

    if comm:
        for copy in wave1:
            copy.wait()

        wave2 = [
            send(nv.at[3, 32:288], nv.at[11, 32:288], at(gx - 1, gy)),
            send(nv.at[8, 32:288], nv.at[0, 32:288], at(gx + 1, gy)),
            send(nv.at[2:10, 48:64], nv.at[2:10, 304:320], at(gx, gy - 1)),
            send(nv.at[2:10, 256:272], nv.at[2:10, 0:16], at(gx, gy + 1)),
        ]
        outer_x = {-1: (3, 11), 1: (8, 0)}
        outer_y = {-1: (slice(48, 64), slice(304, 320)), 1: (slice(256, 272), slice(0, 16))}
        both_y = {-1: (slice(32, 64), slice(288, 320)), 1: (slice(256, 288), slice(0, 32))}
        for a in (-1, 1):
            for b in (-1, 1):
                peer = at(gx + a, gy + b)
                wave2.append(send(nv.at[outer_x[a][0], both_y[b][0]],
                                  nv.at[outer_x[a][1], both_y[b][1]], peer))
                wave2.append(send(nv.at[inner_x[a][0], outer_y[b][0]],
                                  nv.at[inner_x[a][1], outer_y[b][1]], peer))
        side_x = {-1: (slice(1, 2), slice(9, 10)), 0: (slice(1, 9), slice(1, 9)),
                  1: (slice(8, 9), slice(0, 1))}
        side_y = {-1: (slice(16, 32), slice(272, 288)), 0: (slice(16, 272), slice(16, 272)),
                  1: (slice(256, 272), slice(0, 16))}
        for a, b in around:
            wave2.append(send(nc.at[side_x[a][0], side_y[b][0]],
                              nc.at[side_x[a][1], side_y[b][1]], at(gx + a, gy + b)))

        @pl.when(gx == 0)
        def _():
            wipe(nv.at[1, 16:304], 288, 128)

        @pl.when(gx == ngx - 1)
        def _():
            wipe(nv.at[10, 16:304], 288, 128)

        @pl.when(gy == 0)
        def _():
            wipe(nv.at[1:11, 16:32], 10, 16, 128)

        @pl.when(gy == ngy - 1)
        def _():
            wipe(nv.at[1:11, 288:304], 10, 16, 128)
    else:
        wipe(nv.at[0:2], 2, 320, 128)
        wipe(nv.at[10:12], 2, 320, 128)
        wipe(nv.at[:, 0:32], 12, 32, 128)
        wipe(nv.at[:, 288:320], 12, 32, 128)
        wipe(nc.at[0], 288, 128)
        wipe(nc.at[9], 288, 128)
        wipe(nc.at[:, 0:16], 10, 16, 128)
        wipe(nc.at[:, 272:288], 10, 16, 128)

    fill_s(1, 1, 19)
    fill_s(6, 1, 19)
    for j in range(2, 6):
        fill_s(j, 1, 2)
        fill_s(j, 18, 19)

    def tiles(buf, kz, cells, r0, r1):
        return jnp.concatenate([buf[kz, cell, r0:r1] for cell in cells], axis=1)

    def filter_rows(t, r0, r1, halves=(0, 1)):
        return jnp.concatenate([t[2 * kk + h, r0:r1] for kk in range(9) for h in halves], axis=1)

    def activate(acc, r0, r1, cells, y):
        for e, cell in enumerate(cells):
            pre = acc[:, e * 128:(e + 1) * 128] + tb[r0:r1]
            sig = 0.5 * jnp.tanh(0.5 * pre) + 0.5
            grad = c[cell, y:y + r1 - r0].astype(F32)
            gp[1, cell, y:y + r1 - r0] = (grad * sig * (1.0 + pre * (1.0 - sig))).astype(BF)

    def forward(r0, r1, y_in, y_out, cells):
        rhs = jnp.concatenate(
            [tiles(s, kz, [cell + kx for cell in cells], y_in * 32, y_in * 32 + 256)
             for kx in range(3) for kz in range(3)], axis=0)
        acc = jnp.dot(filter_rows(t1, r0, r1), rhs, preferred_element_type=F32)
        activate(acc, r0, r1, cells, y_out * 32)

    for n in range(2):
        cells = (2 * n + 1, 2 * n + 2)
        forward(0, 192, 1, 1, cells)
        forward(0, 192, 7, 7, cells)
        forward(64, 192, 11, 13, cells)

    group = lane // 32

    def gathered(wide, rows, step):
        cells = [wide[step * q:step * q + rows, :128] + wide[step * (q + 4):step * (q + 4) + rows, 128:]
                 for q in range(4)]
        total = jnp.where(group == 0, cells[0], jnp.where(group == 1, cells[1],
                          jnp.where(group == 2, cells[2], cells[3])))
        total = total + pltpu.roll(total, 64, axis=1)
        return total + pltpu.roll(total, 32, axis=1)

    lower = lax.broadcasted_iota(jnp.int32, (16, 128), 0) >= 8

    def split(chain, value, index):
        rounded = value.astype(BF)
        if chain == 0:
            return rounded
        rest = (value - rounded.astype(F32)).astype(BF)
        return jnp.where((index == 6) & (group == 3) & lower, rest, rounded)

    def summed(chain, buf, count, index):
        total = buf[chain, 0].astype(F32)
        for k in range(1, count):
            total = total + buf[chain, k].astype(F32)
        if chain == 0:
            return total
        both = total + jnp.concatenate([total[8:], total[:8]], axis=0)
        return jnp.where((index == 6) & (group == 3), both, total)

    def scatter(chain):
        part[chain, 7] = jnp.zeros((16, 128), BF)
        if not comm:
            return []
        copies = [send(part.at[chain, lax.rem(gx + k + 1, 8)], rs.at[chain, k], gx_peers[k])
                  for k in range(7)]
        rs[chain, 7] = part[chain, gx]
        return copies

    def along(buf, chain, slot, peers):
        return [send(buf.at[chain, slot], buf.at[chain, slot], peer) for peer in peers]

    done = []
    round1 = []

    def put(four):
        value = jnp.where(group == 0, four[0], jnp.where(group == 1, four[1],
                          jnp.where(group == 2, four[2], four[3])))
        for piece in (value[:16], value[16:]):
            chain, index = divmod(len(done), 7)
            part[chain, index] = split(chain, piece, index) if index == 6 else piece.astype(BF)
            done.append(0)
            if index == 6:
                round1.append(scatter(chain))

    own = range(1, 5)
    right = jnp.concatenate([tiles(gp, 1, own, 32, 288), tiles(gp, 1, own, 288, 544)], axis=1)
    blocks = []
    for kx in range(3):
        for kz in range(3):
            cells = [kx + cell for cell in own]
            left = jnp.concatenate([tiles(s, kz, cells, 32, 352), tiles(s, kz, cells, 288, 608)], axis=1)
            wide = lax.dot_general(left, right, NT, preferred_element_type=F32)
            total = gathered(wide, 96, 32)
            blocks += [total[ky * 32:(ky + 1) * 32] for ky in range(3)]
            while len(blocks) >= 4:
                put(blocks[:4])
                blocks = blocks[4:]
    wide = lax.dot_general(jnp.ones((16, 1024), BF), right, NT, preferred_element_type=F32)
    total = gathered(wide, 16, 0)
    put(blocks + [jnp.concatenate([total, total], axis=0)])

    def later_halo():
        base = sum(jnp.dot(jnp.concatenate([stacked_rows(kk, 2 - d) for kk in range(9)], axis=0),
                           one_hot(32, 128, lambda r, q: (q // 32 == d) & (r == natural(q))).astype(BF),
                           preferred_element_type=F32) for d in range(3)).astype(BF)
        for kk in range(9):
            spread(t2, kk, base[kk * 32:(kk + 1) * 32])

        @pl.loop(1, 5)
        def _(j):
            turn_gp(j, 1, 17)

        if comm:
            for copy in wave2:
                copy.wait()

            @pl.when(gx == 0)
            def _():
                wipe(nv.at[0], 320, 128)
                wipe(nv.at[1, 0:16], 16, 128)
                wipe(nv.at[1, 304:320], 16, 128)
                wipe(nc.at[0], 288, 128)

            @pl.when(gx == ngx - 1)
            def _():
                wipe(nv.at[11], 320, 128)
                wipe(nv.at[10, 0:16], 16, 128)
                wipe(nv.at[10, 304:320], 16, 128)
                wipe(nc.at[9], 288, 128)

            @pl.when(gy == 0)
            def _():
                wipe(nv.at[:, 0:16], 12, 16, 128)
                wipe(nv.at[0, 16:32], 16, 128)
                wipe(nv.at[11, 16:32], 16, 128)
                wipe(nc.at[:, 0:16], 10, 16, 128)

            @pl.when(gy == ngy - 1)
            def _():
                wipe(nv.at[:, 304:320], 12, 16, 128)
                wipe(nv.at[0, 288:304], 16, 128)
                wipe(nv.at[11, 288:304], 16, 128)
                wipe(nc.at[:, 272:288], 10, 16, 128)

        for j in (0, 7):
            fill_s(j, 0, 20)
        for j in range(1, 7):
            fill_s(j, 0, 1)
            fill_s(j, 19, 20)
        for j in (0, 5):
            fill_c(j, 0, 18)
        for j in own:
            fill_c(j, 0, 1)
            fill_c(j, 17, 18)
        for b in range(3):
            forward(0, 192, 6 * b, 6 * b, (0, 5))
        for cells in ((1, 2), (3, 4)):
            for half, y_in, r0, y_out in ((0, 0, 0, 0), (1, 16, 160, 17)):
                rhs = jnp.concatenate(
                    [tiles(s, kz, [cell + kx for cell in cells], y_in * 32, y_in * 32 + 128)
                     for kx in range(3) for kz in range(3)], axis=0)
                acc = jnp.dot(filter_rows(t1, r0, r0 + 32, (half,)), rhs, preferred_element_type=F32)
                activate(acc, r0, r0 + 32, cells, y_out * 32)
        for j in (0, 5):
            turn_gp(j, 0, 18)
        for j in own:
            turn_gp(j, 0, 1)
            turn_gp(j, 17, 18)

    def stacked_rows(kk, ky):
        return stacked[kk][ky * 32:(ky + 1) * 32]

    def turn_gp(j, y0, y1):
        block = gp[1, j, y0 * 32:y1 * 32]
        gp[0, j, y0 * 32:y1 * 32] = shifted(block, 127, z_last)
        gp[2, j, y0 * 32:y1 * 32] = shifted(block, 1, z_first)

    def backward(b):
        start, r0 = ((0, 0), (6, 0), (10, 64))[b]
        left = filter_rows(t2, r0, 192)
        out = start * 32 + r0
        for n in range(2):
            rhs = jnp.concatenate(
                [tiles(gp, kz, (2 * n + 2 - kx, 2 * n + 3 - kx), start * 32, start * 32 + 256)
                 for kx in range(3) for kz in range(3)], axis=0)
            acc = jnp.dot(left, rhs, preferred_element_type=F32).astype(BF)
            dq[2 * n, out:out + 192 - r0] = acc[:, :128]
            dq[2 * n + 1, out:out + 192 - r0] = acc[:, 128:]

    def emit():
        for j in range(4):
            block = dq[j].reshape(16, 2, 16, 128)
            even = block[:, 0].reshape(256, 128)
            odd = block[:, 1].reshape(256, 128)
            first = jnp.where(low, even, pltpu.roll(odd, 64, axis=1))
            second = jnp.where(low, pltpu.roll(even, 64, axis=1), odd)
            out = jnp.dot(perm, jnp.concatenate([first, second], axis=1),
                          preferred_element_type=F32).astype(BF)
            for g in range(16):
                dx[j, :, g * 128:(g + 1) * 128] = out[g * 16:(g + 1) * 16, :128]
                dx[j + 4, :, g * 128:(g + 1) * 128] = out[g * 16:(g + 1) * 16, 128:]

    later_halo()
    if comm:
        for copy in round1[0]:
            copy.wait()
        xs[0, xi] = split(0, summed(0, rs, 8, gx), gx)
        round2a = along(xs, 0, xi, x_peers)
        for copy in round1[1]:
            copy.wait()
        zs[1, zi] = split(1, summed(1, rs, 8, gx), gx)
        round2b = along(zs, 1, zi, z_peers)
        backward(0)
        for copy in round2a:
            copy.wait()
        zs[0, zi] = split(0, summed(0, xs, X_CHIPS, gx), gx)
        round3a = along(zs, 0, zi, z_peers)
        backward(1)
        backward(2)
        emit()
        for copy in round2b:
            copy.wait()
        xs[1, xi] = split(1, summed(1, zs, Z_CHIPS, gx), gx)
        round3b = along(xs, 1, xi, x_peers)
        for copy in round3a:
            copy.wait()
        fin[0, gx] = split(0, summed(0, zs, Z_CHIPS, gx), gx)
        round4 = along(fin, 0, gx, gx_peers)
        for copy in round3b:
            copy.wait()
        fin[1, gx] = split(1, summed(1, xs, X_CHIPS, gx), gx)
        round4 += along(fin, 1, gx, gx_peers)
        for copy in round4:
            copy.wait()
    else:
        backward(0)
        backward(1)
        backward(2)
        emit()
        for i in range(8):
            fin[0, i] = part[0, i]
            fin[1, i] = part[1, i]


def finish(scale, dx, fin, dx_hbm, df_hbm, db_hbm, df, db, sem):
    out = pltpu.make_async_copy(dx, dx_hbm, sem.at[0])
    out.start()
    swap = one_hot(128, 128, lambda r, q: r == (q // 32) * 32 + (q % 2) * 16 + (q % 32) // 2).astype(BF)
    rows = jnp.concatenate([fin[chain, i] for chain in range(2) for i in range(7)], axis=0)
    final = jnp.dot(rows, swap, preferred_element_type=F32) * scale
    for t in range(27):
        block = final[(t // 4) * 32:(t // 4) * 32 + 32]
        if t % 4:
            block = pltpu.roll(block, 128 - 32 * (t % 4), axis=1)
        k = (t // 9) * 9 + (t % 3) * 3 + (t // 3) % 3
        df[k, pl.ds(0, 16, stride=2), :] = block[0:16, 0:32]
        df[k, pl.ds(1, 16, stride=2), :] = block[16:32, 0:32]
    db[...] = pltpu.roll(final[208:216] + final[216:224], 32, axis=1)[0:1, 0:32]
    others = [pltpu.make_async_copy(df, df_hbm, sem.at[1]), pltpu.make_async_copy(db, db_hbm, sem.at[2])]
    for copy in others:
        copy.start()
    for copy in [out] + others:
        copy.wait()


def shards(comm, cells, volume, cotangent, weight, bias):
    vm = pl.BlockSpec(memory_space=pltpu.VMEM)
    hbm = pl.BlockSpec(memory_space=pltpu.MemorySpace.HBM)
    inputs = (volume, cotangent, weight.reshape(27, C, C), bias.reshape(1, C))
    if comm:
        inputs = [pltpu.with_memory_space_constraint(a, pltpu.MemorySpace.HBM) for a in inputs]
    dx, fin = pl.pallas_call(
        functools.partial(kernel, comm),
        out_shape=(jax.ShapeDtypeStruct(volume.shape, BF), jax.ShapeDtypeStruct((2, 8, 16, 128), BF)),
        in_specs=[hbm] * 4,
        out_specs=(vm, vm),
        scratch_shapes=[
            pltpu.VMEM((8, 16, 2048), BF),
            pltpu.VMEM((8, 16, 2048), BF),
            pltpu.VMEM((27, C, C), BF),
            pltpu.VMEM((1, C), F32),
            pltpu.VMEM((12, 320, 128), BF),
            pltpu.VMEM((10, 288, 128), BF),
            pltpu.VMEM((3, 8, 640, 128), BF),
            pltpu.VMEM((6, 576, 128), BF),
            pltpu.VMEM((3, 6, 576, 128), BF),
            pltpu.VMEM((18, 192, 128), BF),
            pltpu.VMEM((18, 192, 128), BF),
            pltpu.VMEM((192, 128), F32),
            pltpu.VMEM((4, 512, 128), BF),
            pltpu.VMEM((2, 8, 16, 128), BF),
            pltpu.VMEM((2, 8, 16, 128), BF),
            pltpu.VMEM((2, X_CHIPS, 16, 128), BF),
            pltpu.VMEM((2, Z_CHIPS, 16, 128), BF),
            pltpu.SemaphoreType.DMA((76,)),
            pltpu.SemaphoreType.DMA((76,)),
            pltpu.SemaphoreType.DMA((4,)),
        ],
        compiler_params=pltpu.CompilerParams(
            collective_id=0 if comm else None, has_side_effects=comm, vmem_limit_bytes=48 << 20),
    )(*inputs)
    dg, df, db = pl.pallas_call(
        functools.partial(finish, 1.0 / math.sqrt(cells)),
        out_shape=(jax.ShapeDtypeStruct(volume.shape, BF),
                   jax.ShapeDtypeStruct((27, C, C), F32),
                   jax.ShapeDtypeStruct((1, C), F32)),
        in_specs=[vm, vm],
        out_specs=[pl.BlockSpec(memory_space=pl.ANY)] * 3,
        scratch_shapes=[pltpu.VMEM((27, C, C), F32), pltpu.VMEM((1, C), F32),
                        pltpu.SemaphoreType.DMA((3,))],
        compiler_params=pltpu.CompilerParams(vmem_limit_bytes=4 << 20),
    )(dx, fin)
    return dg, df.reshape(3, 3, 3, C, C), db.reshape(C)


def solution(mesh):
    cells = 8 * mesh.shape["gx"] * 16 * mesh.shape["gy"] * 64
    in_specs = (P("gx", "gy", None), P("gx", "gy", None), P(), P())
    out_specs = (P("gx", "gy", None), P(), P())
    return jax.shard_map(functools.partial(shards, True, cells), mesh=mesh, in_specs=in_specs,
                         out_specs=out_specs, check_vma=False)
```

```python
import functools
import math

import jax
import jax.numpy as jnp
from jax import lax
from jax.experimental import pallas as pl
from jax.experimental.pallas import tpu as pltpu
from jax.sharding import PartitionSpec as P

C = 32
MESH = pl.DeviceIdType.MESH
BF = jnp.bfloat16
F32 = jnp.float32
X_CHIPS = 4
Z_CHIPS = 8
NT = (((1,), (1,)), ((), ()))


def shifted(block, amount, keep):
    return jnp.where(keep, pltpu.roll(block, amount, axis=1), jnp.zeros_like(block))


def natural(index):
    return 2 * (index % 16) + (index % 32) // 16


def one_hot(rows, cols, test):
    row = lax.broadcasted_iota(jnp.int32, (rows, cols), 0)
    col = lax.broadcasted_iota(jnp.int32, (rows, cols), 1)
    return jnp.where(test(row, col), 1.0, 0.0)


def kernel(comm, vol_hbm, cot_hbm, w_hbm, b_hbm, dx, fin, vol, cot, wbuf, bbuf, nv, nc,
           s, c, gp, t1, t2, tb, dq, part16, rs, xs, zs, ssem, rsem, lsem, ring):
    loads = [pltpu.make_async_copy(a, b, lsem.at[i]) for i, (a, b) in enumerate(
        ((vol_hbm, vol), (cot_hbm, cot), (w_hbm, wbuf), (b_hbm, bbuf)))]
    for load in loads:
        load.start()

    if comm:
        gx = lax.axis_index("gx")
        gy = lax.axis_index("gy")
        ngx = lax.axis_size("gx")
        ngy = lax.axis_size("gy")
        xi = lax.rem(gy, X_CHIPS)
        zi = lax.div(gy, X_CHIPS)

        def at(ax, ay):
            return {"gx": lax.rem(ax + ngx, ngx), "gy": lax.rem(ay + ngy, ngy)}

        around = [(a, b) for a in (-1, 0, 1) for b in (-1, 0, 1) if a or b]
        gx_peers = [at(gx + k, gy) for k in range(1, 8)]
        x_peers = [at(gx, zi * X_CHIPS + lax.rem(xi + k, X_CHIPS)) for k in range(1, X_CHIPS)]
        z_peers = [at(gx, lax.rem(zi + k, Z_CHIPS) * X_CHIPS + xi) for k in range(1, Z_CHIPS)]
        z_near = [z_peers[0], z_peers[Z_CHIPS - 2]]
        z_next = [z_peers[1], z_peers[Z_CHIPS - 3]]
        peers = [at(gx + a, gy + b) for a, b in around if b] + gx_peers + x_peers + z_near
        barrier = pltpu.get_barrier_semaphore()
        for peer in peers:
            pl.semaphore_signal(barrier, inc=1, device_id=peer, device_id_type=MESH)


    lane = lax.broadcasted_iota(jnp.int32, (1, 128), 1)
    low = lane < 64
    z_first = (lane % 64) != 0
    z_last = (lane % 64) != 63
    perm = one_hot(256, 256, lambda r, q: q == (r % 16) * 16 + r // 16).astype(BF)

    def turn(src, dst, first, offset):
        for x in range(0, 8, 2):
            parts = [
                jnp.concatenate([src[x + e, :, g * 128:(g + 1) * 128] for g in range(16)], axis=0)
                for e in range(2)
            ]
            out = jnp.dot(perm, jnp.concatenate(parts, axis=1), preferred_element_type=F32).astype(BF)
            dst[first + x, offset:offset + 256] = out[:, :128]
            dst[first + x + 1, offset:offset + 256] = out[:, 128:]

    used = []

    def send(src, dst, peer):
        index = len(used)
        used.append(index)
        copy = pltpu.make_async_remote_copy(
            src_ref=src, dst_ref=dst, send_sem=ssem.at[index], recv_sem=rsem.at[index],
            device_id=peer, device_id_type=MESH)
        copy.start()
        return copy

    def wipe(ref, *shape):
        ref[...] = jnp.zeros(shape, BF)

    loads[0].wait()
    turn(vol, nv, 2, 32)
    if comm:
        pl.semaphore_wait(barrier, len(peers))
        for peer in z_near:
            pl.semaphore_signal(ring.at[0], inc=1, device_id=peer, device_id_type=MESH)
        wave1 = [
            send(nv.at[2, 32:288], nv.at[10, 32:288], at(gx - 1, gy)),
            send(nv.at[9, 32:288], nv.at[1, 32:288], at(gx + 1, gy)),
            send(nv.at[2:10, 32:48], nv.at[2:10, 288:304], at(gx, gy - 1)),
            send(nv.at[2:10, 272:288], nv.at[2:10, 16:32], at(gx, gy + 1)),
        ]
        inner_x = {-1: (2, 10), 1: (9, 1)}
        inner_y = {-1: (slice(32, 48), slice(288, 304)), 1: (slice(272, 288), slice(16, 32))}
        for a in (-1, 1):
            for b in (-1, 1):
                wave1.append(send(nv.at[inner_x[a][0], inner_y[b][0]],
                                  nv.at[inner_x[a][1], inner_y[b][1]], at(gx + a, gy + b)))
    loads[1].wait()
    turn(cot, nc, 1, 16)

    def paired(buf, j, r0, r1):
        rows = (r1 - r0) // 16
        a = buf[j, r0:r1]
        b = buf[j + 4, r0:r1]
        even = jnp.where(low, a, pltpu.roll(b, 64, axis=1))
        odd = jnp.where(low, pltpu.roll(a, 64, axis=1), b)
        both = jnp.concatenate(
            [even.reshape(rows, 1, 16, 128), odd.reshape(rows, 1, 16, 128)], axis=1)
        return both.reshape(rows * 32, 128)

    def fill_s(j, y0, y1):
        block = paired(nv, j, y0 * 16, y1 * 16)
        s[1, j, y0 * 32:y1 * 32] = block
        s[0, j, y0 * 32:y1 * 32] = shifted(block, 1, z_first)
        s[2, j, y0 * 32:y1 * 32] = shifted(block, 127, z_last)

    def fill_c(j, y0, y1):
        c[j, y0 * 32:y1 * 32] = paired(nc, j, y0 * 16, y1 * 16)

    @pl.loop(2, 6)
    def _(j):
        fill_s(j, 2, 18)

    @pl.loop(1, 5)
    def _(j):
        fill_c(j, 1, 17)

    def spread(t, kk, base):
        turned = [base] + [pltpu.roll(base, 32 * i, axis=1) for i in (1, 2, 3)]
        zero = jnp.zeros_like(base)
        rows = [(base, zero), (turned[1], zero),
                (jnp.where(lane >= 64, turned[2], zero), jnp.where(lane < 64, turned[2], zero)),
                (jnp.where(lane >= 96, turned[3], zero), jnp.where(lane < 96, turned[3], zero)),
                (zero, base), (zero, turned[1])]
        for yo in range(6):
            for half in range(2):
                t[2 * kk + half, yo * 32:(yo + 1) * 32] = rows[yo][half]

    loads[2].wait()
    loads[3].wait()
    rows4 = one_hot(128, 128, lambda r, q: (r // 32 == q // 32) & (q % 32 == natural(r))).astype(BF)
    lanes1 = one_hot(32, 32, lambda r, q: q == natural(r)).astype(BF)
    stacked = []
    for kk in range(9):
        raw = jnp.concatenate([wbuf[(kk // 3) * 9 + ky * 3 + kk % 3] for ky in range(3)]
                              + [jnp.zeros((32, 32), BF)], axis=0)
        stacked.append(jnp.dot(rows4, raw, preferred_element_type=F32).astype(BF))
        spread(t1, kk, lax.dot_general(lanes1, stacked[kk], NT, preferred_element_type=F32).astype(BF))
    tb[...] = lax.dot_general(
        one_hot(192, 32, lambda r, q: q == natural(r)),
        jnp.broadcast_to(bbuf[...], (128, 32)), NT,
        preferred_element_type=F32, precision=lax.Precision.HIGHEST)

    if comm:
        pl.semaphore_wait(ring.at[0], 2)
        for peer in z_next:
            pl.semaphore_signal(ring.at[1], inc=1, device_id=peer, device_id_type=MESH)
        for copy in wave1:
            copy.wait()

        wave2 = [
            send(nv.at[3, 32:288], nv.at[11, 32:288], at(gx - 1, gy)),
            send(nv.at[8, 32:288], nv.at[0, 32:288], at(gx + 1, gy)),
            send(nv.at[2:10, 48:64], nv.at[2:10, 304:320], at(gx, gy - 1)),
            send(nv.at[2:10, 256:272], nv.at[2:10, 0:16], at(gx, gy + 1)),
        ]
        outer_x = {-1: (3, 11), 1: (8, 0)}
        outer_y = {-1: (slice(48, 64), slice(304, 320)), 1: (slice(256, 272), slice(0, 16))}
        both_y = {-1: (slice(32, 64), slice(288, 320)), 1: (slice(256, 288), slice(0, 32))}
        for a in (-1, 1):
            for b in (-1, 1):
                peer = at(gx + a, gy + b)
                wave2.append(send(nv.at[outer_x[a][0], both_y[b][0]],
                                  nv.at[outer_x[a][1], both_y[b][1]], peer))
                wave2.append(send(nv.at[inner_x[a][0], outer_y[b][0]],
                                  nv.at[inner_x[a][1], outer_y[b][1]], peer))
        side_x = {-1: (slice(1, 2), slice(9, 10)), 0: (slice(1, 9), slice(1, 9)),
                  1: (slice(8, 9), slice(0, 1))}
        side_y = {-1: (slice(16, 32), slice(272, 288)), 0: (slice(16, 272), slice(16, 272)),
                  1: (slice(256, 272), slice(0, 16))}
        for a, b in around:
            wave2.append(send(nc.at[side_x[a][0], side_y[b][0]],
                              nc.at[side_x[a][1], side_y[b][1]], at(gx + a, gy + b)))

        @pl.when(gx == 0)
        def _():
            wipe(nv.at[1, 16:304], 288, 128)

        @pl.when(gx == ngx - 1)
        def _():
            wipe(nv.at[10, 16:304], 288, 128)

        @pl.when(gy == 0)
        def _():
            wipe(nv.at[1:11, 16:32], 10, 16, 128)

        @pl.when(gy == ngy - 1)
        def _():
            wipe(nv.at[1:11, 288:304], 10, 16, 128)
    else:
        wipe(nv.at[0:2], 2, 320, 128)
        wipe(nv.at[10:12], 2, 320, 128)
        wipe(nv.at[:, 0:32], 12, 32, 128)
        wipe(nv.at[:, 288:320], 12, 32, 128)
        wipe(nc.at[0], 288, 128)
        wipe(nc.at[9], 288, 128)
        wipe(nc.at[:, 0:16], 10, 16, 128)
        wipe(nc.at[:, 272:288], 10, 16, 128)

    fill_s(1, 1, 19)
    fill_s(6, 1, 19)
    for j in range(2, 6):
        fill_s(j, 1, 2)
        fill_s(j, 18, 19)

    def tiles(buf, kz, cells, r0, r1):
        return jnp.concatenate([buf[kz, cell, r0:r1] for cell in cells], axis=1)

    def filter_rows(t, r0, r1, halves=(0, 1)):
        return jnp.concatenate([t[2 * kk + h, r0:r1] for kk in range(9) for h in halves], axis=1)

    def activate(acc, r0, r1, cells, y):
        for e, cell in enumerate(cells):
            pre = acc[:, e * 128:(e + 1) * 128] + tb[r0:r1]
            sig = 0.5 * jnp.tanh(0.5 * pre) + 0.5
            grad = c[cell, y:y + r1 - r0].astype(F32)
            gp[1, cell, y:y + r1 - r0] = (grad * sig * (1.0 + pre * (1.0 - sig))).astype(BF)

    def forward(r0, r1, y_in, y_out, cells):
        rhs = jnp.concatenate(
            [tiles(s, kz, [cell + kx for cell in cells], y_in * 32, y_in * 32 + 256)
             for kx in range(3) for kz in range(3)], axis=0)
        acc = jnp.dot(filter_rows(t1, r0, r1), rhs, preferred_element_type=F32)
        activate(acc, r0, r1, cells, y_out * 32)

    for n in range(2):
        cells = (2 * n + 1, 2 * n + 2)
        forward(0, 192, 1, 1, cells)
        forward(0, 192, 7, 7, cells)
        forward(64, 192, 11, 13, cells)

    group = lane // 32

    def gathered(wide, rows, step):
        cells = [wide[step * q:step * q + rows, :128] + wide[step * (q + 4):step * (q + 4) + rows, 128:]
                 for q in range(4)]
        total = jnp.where(group == 0, cells[0], jnp.where(group == 1, cells[1],
                          jnp.where(group == 2, cells[2], cells[3])))
        total = total + pltpu.roll(total, 64, axis=1)
        return total + pltpu.roll(total, 32, axis=1)

    lower = lax.broadcasted_iota(jnp.int32, (32, 128), 0) >= 16

    def split(value, index):
        rounded = value.astype(BF)
        rest = (value - rounded.astype(F32)).astype(BF)
        return jnp.where((index == 6) & (group == 3) & lower, rest, rounded)

    def joined(value, index):
        both = value + jnp.concatenate([value[16:], value[:16]], axis=0)
        return jnp.where((index == 6) & (group == 3), both, value)

    done = []

    def put(four):
        value = jnp.where(group == 0, four[0], jnp.where(group == 1, four[1],
                          jnp.where(group == 2, four[2], four[3])))
        part16[len(done)] = split(value, len(done)) if len(done) == 6 else value.astype(BF)
        done.append(0)

    own = range(1, 5)
    right = jnp.concatenate([tiles(gp, 1, own, 32, 288), tiles(gp, 1, own, 288, 544)], axis=1)
    sums = gathered(lax.dot_general(jnp.ones((16, 1024), BF), right, NT, preferred_element_type=F32), 16, 0)
    blocks = []
    for kx in range(3):
        for kz in range(3):
            cells = [kx + cell for cell in own]
            left = jnp.concatenate([tiles(s, kz, cells, 32, 352), tiles(s, kz, cells, 288, 608)], axis=1)
            wide = lax.dot_general(left, right, NT, preferred_element_type=F32)
            total = gathered(wide, 96, 32)
            blocks += [total[ky * 32:(ky + 1) * 32] for ky in range(3)]
            while len(blocks) >= 4:
                put(blocks[:4])
                blocks = blocks[4:]
    put(blocks + [jnp.concatenate([sums, sums], axis=0)])
    part16[7] = jnp.zeros((32, 128), BF)

    def later_halo():
        @pl.loop(1, 5)
        def _(j):
            turn_gp(j, 1, 17)

        base = sum(jnp.dot(jnp.concatenate([stacked_rows(kk, 2 - d) for kk in range(9)], axis=0),
                           one_hot(32, 128, lambda r, q: (q // 32 == d) & (r == natural(q))).astype(BF),
                           preferred_element_type=F32) for d in range(3)).astype(BF)
        for kk in range(9):
            spread(t2, kk, base[kk * 32:(kk + 1) * 32])

        if comm:
            for copy in wave2:
                copy.wait()

            @pl.when(gx == 0)
            def _():
                wipe(nv.at[0], 320, 128)
                wipe(nv.at[1, 0:16], 16, 128)
                wipe(nv.at[1, 304:320], 16, 128)
                wipe(nc.at[0], 288, 128)

            @pl.when(gx == ngx - 1)
            def _():
                wipe(nv.at[11], 320, 128)
                wipe(nv.at[10, 0:16], 16, 128)
                wipe(nv.at[10, 304:320], 16, 128)
                wipe(nc.at[9], 288, 128)

            @pl.when(gy == 0)
            def _():
                wipe(nv.at[:, 0:16], 12, 16, 128)
                wipe(nv.at[0, 16:32], 16, 128)
                wipe(nv.at[11, 16:32], 16, 128)
                wipe(nc.at[:, 0:16], 10, 16, 128)

            @pl.when(gy == ngy - 1)
            def _():
                wipe(nv.at[:, 304:320], 12, 16, 128)
                wipe(nv.at[0, 288:304], 16, 128)
                wipe(nv.at[11, 288:304], 16, 128)
                wipe(nc.at[:, 272:288], 10, 16, 128)

        for j in (0, 7):
            fill_s(j, 0, 20)
        for j in range(1, 7):
            fill_s(j, 0, 1)
            fill_s(j, 19, 20)
        for j in (0, 5):
            fill_c(j, 0, 18)
        for j in own:
            fill_c(j, 0, 1)
            fill_c(j, 17, 18)
        for b in range(3):
            forward(0, 192, 6 * b, 6 * b, (0, 5))
        for cells in ((1, 2), (3, 4)):
            for half, y_in, r0, y_out in ((0, 0, 0, 0), (1, 16, 160, 17)):
                rhs = jnp.concatenate(
                    [tiles(s, kz, [cell + kx for cell in cells], y_in * 32, y_in * 32 + 128)
                     for kx in range(3) for kz in range(3)], axis=0)
                acc = jnp.dot(filter_rows(t1, r0, r0 + 32, (half,)), rhs, preferred_element_type=F32)
                activate(acc, r0, r0 + 32, cells, y_out * 32)
        for j in (0, 5):
            turn_gp(j, 0, 18)
        for j in own:
            turn_gp(j, 0, 1)
            turn_gp(j, 17, 18)

    def stacked_rows(kk, ky):
        return stacked[kk][ky * 32:(ky + 1) * 32]

    def turn_gp(j, y0, y1):
        block = gp[1, j, y0 * 32:y1 * 32]
        gp[0, j, y0 * 32:y1 * 32] = shifted(block, 127, z_last)
        gp[2, j, y0 * 32:y1 * 32] = shifted(block, 1, z_first)

    def backward(b):
        start, r0 = ((0, 0), (6, 0), (10, 64))[b]
        left = filter_rows(t2, r0, 192)
        out = start * 32 + r0
        for n in range(2):
            rhs = jnp.concatenate(
                [tiles(gp, kz, (2 * n + 2 - kx, 2 * n + 3 - kx), start * 32, start * 32 + 256)
                 for kx in range(3) for kz in range(3)], axis=0)
            acc = jnp.dot(left, rhs, preferred_element_type=F32).astype(BF)
            dq[2 * n, out:out + 192 - r0] = acc[:, :128]
            dq[2 * n + 1, out:out + 192 - r0] = acc[:, 128:]

    def emit():
        for j in range(4):
            block = dq[j].reshape(16, 2, 16, 128)
            even = block[:, 0].reshape(256, 128)
            odd = block[:, 1].reshape(256, 128)
            first = jnp.where(low, even, pltpu.roll(odd, 64, axis=1))
            second = jnp.where(low, pltpu.roll(even, 64, axis=1), odd)
            out = jnp.dot(perm, jnp.concatenate([first, second], axis=1),
                          preferred_element_type=F32).astype(BF)
            for g in range(16):
                dx[j, :, g * 128:(g + 1) * 128] = out[g * 16:(g + 1) * 16, :128]
                dx[j + 4, :, g * 128:(g + 1) * 128] = out[g * 16:(g + 1) * 16, 128:]

    def summed(buf, count, index):
        total = buf[0].astype(F32)
        for k in range(1, count):
            total = total + buf[k].astype(F32)
        return joined(total, index)

    if comm:
        round1 = [send(part16.at[lax.rem(gx + k + 1, 8)], rs.at[k], gx_peers[k]) for k in range(7)]
        rs[7] = part16[gx]
        later_halo()
        for copy in round1:
            copy.wait()
        xs[xi] = split(summed(rs, 8, gx), gx)
        round2 = [send(xs.at[xi], xs.at[xi], x_peers[k]) for k in range(X_CHIPS - 1)]
        backward(0)
        backward(1)
        for copy in round2:
            copy.wait()
        pl.semaphore_wait(ring.at[1], 2)
        zs[zi] = split(summed(xs, X_CHIPS, gx), gx)
        round3 = [send(zs.at[zi], zs.at[zi], z_peers[k]) for k in range(Z_CHIPS - 1)]
        backward(2)
        emit()
        for copy in round3:
            copy.wait()
        fin[gx] = split(summed(zs, Z_CHIPS, gx), gx)
        round4 = [send(fin.at[gx], fin.at[gx], gx_peers[k]) for k in range(7)]
        for copy in round4:
            copy.wait()
    else:
        later_halo()
        backward(0)
        backward(1)
        backward(2)
        emit()
        for i in range(8):
            fin[i] = part16[i]


def finish(scale, dx, fin, dx_hbm, df_hbm, db_hbm, df, db, sem):
    out = pltpu.make_async_copy(dx, dx_hbm, sem.at[0])
    out.start()
    swap = one_hot(128, 128, lambda r, q: r == (q // 32) * 32 + (q % 2) * 16 + (q % 32) // 2).astype(BF)
    final = jnp.dot(fin[...].reshape(256, 128), swap, preferred_element_type=F32) * scale
    for t in range(27):
        block = final[(t // 4) * 32:(t // 4) * 32 + 32]
        if t % 4:
            block = pltpu.roll(block, 128 - 32 * (t % 4), axis=1)
        k = (t // 9) * 9 + (t % 3) * 3 + (t // 3) % 3
        df[k, pl.ds(0, 16, stride=2), :] = block[0:16, 0:32]
        df[k, pl.ds(1, 16, stride=2), :] = block[16:32, 0:32]
    db[...] = pltpu.roll(final[192:200] + final[208:216], 32, axis=1)[0:1, 0:32]
    others = [pltpu.make_async_copy(df, df_hbm, sem.at[1]), pltpu.make_async_copy(db, db_hbm, sem.at[2])]
    for copy in others:
        copy.start()
    for copy in [out] + others:
        copy.wait()


def shards(comm, cells, volume, cotangent, weight, bias):
    vm = pl.BlockSpec(memory_space=pltpu.VMEM)
    hbm = pl.BlockSpec(memory_space=pltpu.MemorySpace.HBM)
    inputs = (volume, cotangent, weight.reshape(27, C, C), bias.reshape(1, C))
    if comm:
        inputs = [pltpu.with_memory_space_constraint(a, pltpu.MemorySpace.HBM) for a in inputs]
    dx, fin = pl.pallas_call(
        functools.partial(kernel, comm),
        out_shape=(jax.ShapeDtypeStruct(volume.shape, BF), jax.ShapeDtypeStruct((8, 32, 128), BF)),
        in_specs=[hbm] * 4,
        out_specs=(vm, vm),
        scratch_shapes=[
            pltpu.VMEM((8, 16, 2048), BF),
            pltpu.VMEM((8, 16, 2048), BF),
            pltpu.VMEM((27, C, C), BF),
            pltpu.VMEM((1, C), F32),
            pltpu.VMEM((12, 320, 128), BF),
            pltpu.VMEM((10, 288, 128), BF),
            pltpu.VMEM((3, 8, 640, 128), BF),
            pltpu.VMEM((6, 576, 128), BF),
            pltpu.VMEM((3, 6, 576, 128), BF),
            pltpu.VMEM((18, 192, 128), BF),
            pltpu.VMEM((18, 192, 128), BF),
            pltpu.VMEM((192, 128), F32),
            pltpu.VMEM((4, 512, 128), BF),
            pltpu.VMEM((8, 32, 128), BF),
            pltpu.VMEM((8, 32, 128), BF),
            pltpu.VMEM((X_CHIPS, 32, 128), BF),
            pltpu.VMEM((Z_CHIPS, 32, 128), BF),
            pltpu.SemaphoreType.DMA((52,)),
            pltpu.SemaphoreType.DMA((52,)),
            pltpu.SemaphoreType.DMA((4,)),
            pltpu.SemaphoreType.REGULAR((2,)),
        ],
        compiler_params=pltpu.CompilerParams(
            collective_id=0 if comm else None, has_side_effects=comm, vmem_limit_bytes=48 << 20),
    )(*inputs)
    dg, df, db = pl.pallas_call(
        functools.partial(finish, 1.0 / math.sqrt(cells)),
        out_shape=(jax.ShapeDtypeStruct(volume.shape, BF),
                   jax.ShapeDtypeStruct((27, C, C), F32),
                   jax.ShapeDtypeStruct((1, C), F32)),
        in_specs=[vm, vm],
        out_specs=[pl.BlockSpec(memory_space=pl.ANY)] * 3,
        scratch_shapes=[pltpu.VMEM((27, C, C), F32), pltpu.VMEM((1, C), F32),
                        pltpu.SemaphoreType.DMA((3,))],
        compiler_params=pltpu.CompilerParams(vmem_limit_bytes=4 << 20),
    )(dx, fin)
    return dg, df.reshape(3, 3, 3, C, C), db.reshape(C)


def solution(mesh):
    cells = 8 * mesh.shape["gx"] * 16 * mesh.shape["gy"] * 64
    in_specs = (P("gx", "gy", None), P("gx", "gy", None), P(), P())
    out_specs = (P("gx", "gy", None), P(), P())
    return jax.shard_map(functools.partial(shards, True, cells), mesh=mesh, in_specs=in_specs,
                         out_specs=out_specs, check_vma=False)
```

```python
import functools
import math

import jax
import jax.numpy as jnp
from jax import lax
from jax.experimental import pallas as pl
from jax.experimental.pallas import tpu as pltpu
from jax.sharding import PartitionSpec as P

C = 32
MESH = pl.DeviceIdType.MESH
BF = jnp.bfloat16
F32 = jnp.float32
X_CHIPS = 4
Z_CHIPS = 8
NT = (((1,), (1,)), ((), ()))


def shifted(block, amount, keep):
    return jnp.where(keep, pltpu.roll(block, amount, axis=1), jnp.zeros_like(block))


def natural(index):
    return 2 * (index % 16) + (index % 32) // 16


def one_hot(rows, cols, test):
    row = lax.broadcasted_iota(jnp.int32, (rows, cols), 0)
    col = lax.broadcasted_iota(jnp.int32, (rows, cols), 1)
    return jnp.where(test(row, col), 1.0, 0.0)


def kernel(comm, vol_hbm, cot_hbm, w_hbm, b_hbm, dx, fin, vol, cot, wbuf, bbuf, nv, nc,
           s, c, gp, t1, t2, tb, dq, part16, rs, xs, zs, ssem, rsem, lsem, ring):
    loads = [pltpu.make_async_copy(a, b, lsem.at[i]) for i, (a, b) in enumerate(
        ((vol_hbm, vol), (cot_hbm, cot), (w_hbm, wbuf), (b_hbm, bbuf)))]
    for load in loads:
        load.start()

    if comm:
        gx = lax.axis_index("gx")
        gy = lax.axis_index("gy")
        ngx = lax.axis_size("gx")
        ngy = lax.axis_size("gy")
        xi = lax.rem(gy, X_CHIPS)
        zi = lax.div(gy, X_CHIPS)

        def at(ax, ay):
            return {"gx": lax.rem(ax + ngx, ngx), "gy": lax.rem(ay + ngy, ngy)}

        around = [(a, b) for a in (-1, 0, 1) for b in (-1, 0, 1) if a or b]
        gx_peers = [at(gx + k, gy) for k in range(1, 8)]
        x_peers = [at(gx, zi * X_CHIPS + lax.rem(xi + k, X_CHIPS)) for k in range(1, X_CHIPS)]
        z_peers = [at(gx, lax.rem(zi + k, Z_CHIPS) * X_CHIPS + xi) for k in range(1, Z_CHIPS)]
        z_near = [z_peers[0], z_peers[Z_CHIPS - 2]]
        z_next = [z_peers[1], z_peers[Z_CHIPS - 3]]
        peers = [at(gx + a, gy + b) for a, b in around if b] + gx_peers + x_peers + z_near
        barrier = pltpu.get_barrier_semaphore()
        for peer in peers:
            pl.semaphore_signal(barrier, inc=1, device_id=peer, device_id_type=MESH)


    lane = lax.broadcasted_iota(jnp.int32, (1, 128), 1)
    low = lane < 64
    z_first = (lane % 64) != 0
    z_last = (lane % 64) != 63
    perm = one_hot(256, 256, lambda r, q: q == (r % 16) * 16 + r // 16).astype(BF)

    def turn(src, dst, first, offset):
        for x in range(0, 8, 2):
            parts = [
                jnp.concatenate([src[x + e, :, g * 128:(g + 1) * 128] for g in range(16)], axis=0)
                for e in range(2)
            ]
            out = jnp.dot(perm, jnp.concatenate(parts, axis=1), preferred_element_type=F32).astype(BF)
            dst[first + x, offset:offset + 256] = out[:, :128]
            dst[first + x + 1, offset:offset + 256] = out[:, 128:]

    used = []

    def send(src, dst, peer):
        index = len(used)
        used.append(index)
        copy = pltpu.make_async_remote_copy(
            src_ref=src, dst_ref=dst, send_sem=ssem.at[index], recv_sem=rsem.at[index],
            device_id=peer, device_id_type=MESH)
        copy.start()
        return copy

    def wipe(ref, *shape):
        ref[...] = jnp.zeros(shape, BF)

    loads[0].wait()
    turn(vol, nv, 2, 32)
    if comm:
        pl.semaphore_wait(barrier, len(peers))
        for peer in z_near:
            pl.semaphore_signal(ring.at[0], inc=1, device_id=peer, device_id_type=MESH)
        wave1 = [
            send(nv.at[2, 32:288], nv.at[10, 32:288], at(gx - 1, gy)),
            send(nv.at[9, 32:288], nv.at[1, 32:288], at(gx + 1, gy)),
            send(nv.at[2:10, 32:48], nv.at[2:10, 288:304], at(gx, gy - 1)),
            send(nv.at[2:10, 272:288], nv.at[2:10, 16:32], at(gx, gy + 1)),
        ]
        inner_x = {-1: (2, 10), 1: (9, 1)}
        inner_y = {-1: (slice(32, 48), slice(288, 304)), 1: (slice(272, 288), slice(16, 32))}
        for a in (-1, 1):
            for b in (-1, 1):
                wave1.append(send(nv.at[inner_x[a][0], inner_y[b][0]],
                                  nv.at[inner_x[a][1], inner_y[b][1]], at(gx + a, gy + b)))
    loads[1].wait()
    turn(cot, nc, 1, 16)

    def paired(buf, j, r0, r1):
        rows = (r1 - r0) // 16
        a = buf[j, r0:r1]
        b = buf[j + 4, r0:r1]
        even = jnp.where(low, a, pltpu.roll(b, 64, axis=1))
        odd = jnp.where(low, pltpu.roll(a, 64, axis=1), b)
        both = jnp.concatenate(
            [even.reshape(rows, 1, 16, 128), odd.reshape(rows, 1, 16, 128)], axis=1)
        return both.reshape(rows * 32, 128)

    def fill_s(j, y0, y1):
        block = paired(nv, j, y0 * 16, y1 * 16)
        s[1, j, y0 * 32:y1 * 32] = block
        s[0, j, y0 * 32:y1 * 32] = shifted(block, 1, z_first)
        s[2, j, y0 * 32:y1 * 32] = shifted(block, 127, z_last)

    def fill_c(j, y0, y1):
        c[j, y0 * 32:y1 * 32] = paired(nc, j, y0 * 16, y1 * 16)

    @pl.loop(2, 6)
    def _(j):
        fill_s(j, 2, 18)

    @pl.loop(1, 5)
    def _(j):
        fill_c(j, 1, 17)

    def spread(t, kk, base):
        turned = [base] + [pltpu.roll(base, 32 * i, axis=1) for i in (1, 2, 3)]
        zero = jnp.zeros_like(base)
        rows = [(base, zero), (turned[1], zero),
                (jnp.where(lane >= 64, turned[2], zero), jnp.where(lane < 64, turned[2], zero)),
                (jnp.where(lane >= 96, turned[3], zero), jnp.where(lane < 96, turned[3], zero)),
                (zero, base), (zero, turned[1])]
        for yo in range(6):
            for half in range(2):
                t[2 * kk + half, yo * 32:(yo + 1) * 32] = rows[yo][half]

    loads[2].wait()
    loads[3].wait()
    rows4 = one_hot(128, 128, lambda r, q: (r // 32 == q // 32) & (q % 32 == natural(r))).astype(BF)
    lanes1 = one_hot(32, 32, lambda r, q: q == natural(r)).astype(BF)
    stacked = []
    for kk in range(9):
        raw = jnp.concatenate([wbuf[(kk // 3) * 9 + ky * 3 + kk % 3] for ky in range(3)]
                              + [jnp.zeros((32, 32), BF)], axis=0)
        stacked.append(jnp.dot(rows4, raw, preferred_element_type=F32).astype(BF))
        spread(t1, kk, lax.dot_general(lanes1, stacked[kk], NT, preferred_element_type=F32).astype(BF))
    tb[...] = lax.dot_general(
        one_hot(192, 32, lambda r, q: q == natural(r)),
        jnp.broadcast_to(bbuf[...], (128, 32)), NT,
        preferred_element_type=F32, precision=lax.Precision.HIGHEST)

    if comm:
        pl.semaphore_wait(ring.at[0], 2)
        for peer in z_next:
            pl.semaphore_signal(ring.at[1], inc=1, device_id=peer, device_id_type=MESH)
        for copy in wave1:
            copy.wait()

        wave2 = [
            send(nv.at[3, 32:288], nv.at[11, 32:288], at(gx - 1, gy)),
            send(nv.at[8, 32:288], nv.at[0, 32:288], at(gx + 1, gy)),
            send(nv.at[2:10, 48:64], nv.at[2:10, 304:320], at(gx, gy - 1)),
            send(nv.at[2:10, 256:272], nv.at[2:10, 0:16], at(gx, gy + 1)),
        ]
        outer_x = {-1: (3, 11), 1: (8, 0)}
        outer_y = {-1: (slice(48, 64), slice(304, 320)), 1: (slice(256, 272), slice(0, 16))}
        both_y = {-1: (slice(32, 64), slice(288, 320)), 1: (slice(256, 288), slice(0, 32))}
        for a in (-1, 1):
            for b in (-1, 1):
                peer = at(gx + a, gy + b)
                wave2.append(send(nv.at[outer_x[a][0], both_y[b][0]],
                                  nv.at[outer_x[a][1], both_y[b][1]], peer))
                wave2.append(send(nv.at[inner_x[a][0], outer_y[b][0]],
                                  nv.at[inner_x[a][1], outer_y[b][1]], peer))
        side_x = {-1: (slice(1, 2), slice(9, 10)), 0: (slice(1, 9), slice(1, 9)),
                  1: (slice(8, 9), slice(0, 1))}
        side_y = {-1: (slice(16, 32), slice(272, 288)), 0: (slice(16, 272), slice(16, 272)),
                  1: (slice(256, 272), slice(0, 16))}
        for a, b in around:
            wave2.append(send(nc.at[side_x[a][0], side_y[b][0]],
                              nc.at[side_x[a][1], side_y[b][1]], at(gx + a, gy + b)))

        @pl.when(gx == 0)
        def _():
            wipe(nv.at[1, 16:304], 288, 128)

        @pl.when(gx == ngx - 1)
        def _():
            wipe(nv.at[10, 16:304], 288, 128)

        @pl.when(gy == 0)
        def _():
            wipe(nv.at[1:11, 16:32], 10, 16, 128)

        @pl.when(gy == ngy - 1)
        def _():
            wipe(nv.at[1:11, 288:304], 10, 16, 128)
    else:
        wipe(nv.at[0:2], 2, 320, 128)
        wipe(nv.at[10:12], 2, 320, 128)
        wipe(nv.at[:, 0:32], 12, 32, 128)
        wipe(nv.at[:, 288:320], 12, 32, 128)
        wipe(nc.at[0], 288, 128)
        wipe(nc.at[9], 288, 128)
        wipe(nc.at[:, 0:16], 10, 16, 128)
        wipe(nc.at[:, 272:288], 10, 16, 128)

    fill_s(1, 1, 19)
    fill_s(6, 1, 19)
    for j in range(2, 6):
        fill_s(j, 1, 2)
        fill_s(j, 18, 19)

    def tiles(buf, kz, cells, r0, r1):
        return jnp.concatenate([buf[kz, cell, r0:r1] for cell in cells], axis=1)

    def filter_rows(t, r0, r1, halves=(0, 1)):
        return jnp.concatenate([t[2 * kk + h, r0:r1] for kk in range(9) for h in halves], axis=1)

    def activate(acc, r0, r1, cells, y):
        for e, cell in enumerate(cells):
            pre = acc[:, e * 128:(e + 1) * 128] + tb[r0:r1]
            sig = 0.5 * jnp.tanh(0.5 * pre) + 0.5
            grad = c[cell, y:y + r1 - r0].astype(F32)
            block = (grad * sig * (1.0 + pre * (1.0 - sig))).astype(BF)
            gp[1, cell, y:y + r1 - r0] = block
            gp[0, cell, y:y + r1 - r0] = shifted(block, 127, z_last)
            gp[2, cell, y:y + r1 - r0] = shifted(block, 1, z_first)

    def forward(r0, r1, y_in, y_out, cells):
        rhs = jnp.concatenate(
            [tiles(s, kz, [cell + kx for cell in cells], y_in * 32, y_in * 32 + 256)
             for kx in range(3) for kz in range(3)], axis=0)
        acc = jnp.dot(filter_rows(t1, r0, r1), rhs, preferred_element_type=F32)
        activate(acc, r0, r1, cells, y_out * 32)

    for b in range(8):
        for cells in ((1, 2), (3, 4)):
            rhs = jnp.concatenate(
                [tiles(s, kz, [cell + kx for cell in cells], (2 * b + 1) * 32, (2 * b + 5) * 32)
                 for kx in range(3) for kz in range(3)], axis=0)
            acc = jnp.dot(filter_rows(t1, 0, 64, (0,)), rhs, preferred_element_type=F32)
            activate(acc, 0, 64, cells, (2 * b + 1) * 32)

    group = lane // 32

    lower = lax.broadcasted_iota(jnp.int32, (32, 128), 0) >= 16

    def split(value, index):
        rounded = value.astype(BF)
        rest = (value - rounded.astype(F32)).astype(BF)
        return jnp.where((index == 6) & (group == 3) & lower, rest, rounded)

    def joined(value, index):
        both = value + jnp.concatenate([value[16:], value[:16]], axis=0)
        return jnp.where((index == 6) & (group == 3), both, value)

    done = []

    def put(four):
        value = jnp.where(group == 0, four[0], jnp.where(group == 1, four[1],
                          jnp.where(group == 2, four[2], four[3])))
        part16[len(done)] = split(value, len(done)) if len(done) == 6 else value.astype(BF)
        done.append(0)

    own = range(1, 5)
    right = jnp.concatenate(
        [jnp.concatenate([tiles(gp, kz, own, (2 * b + 1) * 32, (2 * b + 3) * 32) for kz in range(3)], axis=0)
         for b in range(8)], axis=1)
    even = group % 2 == 0
    blocks = []

    def placed(value, source):
        turns = (len(done) * 4 + len(blocks) - source) % 4
        blocks.append(pltpu.roll(value, 32 * turns, axis=1) if turns else value)
        if len(blocks) == 4:
            put(blocks)
            blocks.clear()

    for kx in range(3):
        left = jnp.concatenate(
            [tiles(s, 1, [kx + cell for cell in own], (2 * b + 1) * 32, (2 * b + 5) * 32)
             for b in range(8)], axis=1)
        if kx == 0:
            left = jnp.concatenate([left, jnp.ones((16, 4096), BF)], axis=0)
        wide = lax.dot_general(left, right, NT, preferred_element_type=F32)
        wide = [wide[:, :128], jnp.concatenate([wide[:, 128:], jnp.zeros_like(wide[:, 128:])], axis=1)]
        if kx == 0:
            sums = wide[0][128:144] + pltpu.roll(wide[0][128:144], 96, axis=1)
        for kz in range(3):
            for ky in range(3):
                half = wide[kz // 2]
                both = jnp.where(even, half[ky * 32:ky * 32 + 32], half[ky * 32 + 32:ky * 32 + 64])
                placed(both + pltpu.roll(both, 96, axis=1), 2 * (kz % 2))
    placed(jnp.concatenate([sums, sums], axis=0), 2)
    part16[7] = jnp.zeros((32, 128), BF)

    def later_halo():
        if comm:
            for copy in wave2:
                copy.wait()

            @pl.when(gx == 0)
            def _():
                wipe(nv.at[0], 320, 128)
                wipe(nv.at[1, 0:16], 16, 128)
                wipe(nv.at[1, 304:320], 16, 128)
                wipe(nc.at[0], 288, 128)

            @pl.when(gx == ngx - 1)
            def _():
                wipe(nv.at[11], 320, 128)
                wipe(nv.at[10, 0:16], 16, 128)
                wipe(nv.at[10, 304:320], 16, 128)
                wipe(nc.at[9], 288, 128)

            @pl.when(gy == 0)
            def _():
                wipe(nv.at[:, 0:16], 12, 16, 128)
                wipe(nv.at[0, 16:32], 16, 128)
                wipe(nv.at[11, 16:32], 16, 128)
                wipe(nc.at[:, 0:16], 10, 16, 128)

            @pl.when(gy == ngy - 1)
            def _():
                wipe(nv.at[:, 304:320], 12, 16, 128)
                wipe(nv.at[0, 288:304], 16, 128)
                wipe(nv.at[11, 288:304], 16, 128)
                wipe(nc.at[:, 272:288], 10, 16, 128)

        base = sum(jnp.dot(jnp.concatenate([stacked_rows(kk, 2 - d) for kk in range(9)], axis=0),
                           one_hot(32, 128, lambda r, q: (q // 32 == d) & (r == natural(q))).astype(BF),
                           preferred_element_type=F32) for d in range(3)).astype(BF)
        for kk in range(9):
            spread(t2, kk, base[kk * 32:(kk + 1) * 32])
        for j in (0, 7):
            fill_s(j, 0, 20)
        for j in range(1, 7):
            fill_s(j, 0, 1)
            fill_s(j, 19, 20)
        for j in (0, 5):
            fill_c(j, 0, 18)
        for j in own:
            fill_c(j, 0, 1)
            fill_c(j, 17, 18)
        for b in range(3):
            forward(0, 192, 6 * b, 6 * b, (0, 5))
        for cells in ((1, 2), (3, 4)):
            for half, y_in, r0, y_out in ((0, 0, 0, 0), (1, 16, 160, 17)):
                rhs = jnp.concatenate(
                    [tiles(s, kz, [cell + kx for cell in cells], y_in * 32, y_in * 32 + 128)
                     for kx in range(3) for kz in range(3)], axis=0)
                acc = jnp.dot(filter_rows(t1, r0, r0 + 32, (half,)), rhs, preferred_element_type=F32)
                activate(acc, r0, r0 + 32, cells, y_out * 32)

    def stacked_rows(kk, ky):
        return stacked[kk][ky * 32:(ky + 1) * 32]

    def backward(b):
        start, r0 = ((0, 0), (6, 0), (10, 64))[b]
        left = filter_rows(t2, r0, 192)
        out = start * 32 + r0
        for n in range(2):
            rhs = jnp.concatenate(
                [tiles(gp, kz, (2 * n + 2 - kx, 2 * n + 3 - kx), start * 32, start * 32 + 256)
                 for kx in range(3) for kz in range(3)], axis=0)
            acc = jnp.dot(left, rhs, preferred_element_type=F32).astype(BF)
            dq[2 * n, out:out + 192 - r0] = acc[:, :128]
            dq[2 * n + 1, out:out + 192 - r0] = acc[:, 128:]

    def emit():
        for j in range(4):
            block = dq[j].reshape(16, 2, 16, 128)
            even = block[:, 0].reshape(256, 128)
            odd = block[:, 1].reshape(256, 128)
            first = jnp.where(low, even, pltpu.roll(odd, 64, axis=1))
            second = jnp.where(low, pltpu.roll(even, 64, axis=1), odd)
            out = jnp.dot(perm, jnp.concatenate([first, second], axis=1),
                          preferred_element_type=F32).astype(BF)
            for g in range(16):
                dx[j, :, g * 128:(g + 1) * 128] = out[g * 16:(g + 1) * 16, :128]
                dx[j + 4, :, g * 128:(g + 1) * 128] = out[g * 16:(g + 1) * 16, 128:]

    def summed(buf, count, index):
        total = buf[0].astype(F32)
        for k in range(1, count):
            total = total + buf[k].astype(F32)
        return joined(total, index)

    if comm:
        round1 = [send(part16.at[lax.rem(gx + k + 1, 8)], rs.at[k], gx_peers[k]) for k in range(7)]
        rs[7] = part16[gx]
        later_halo()
        for copy in round1:
            copy.wait()
        xs[xi] = split(summed(rs, 8, gx), gx)
        round2 = [send(xs.at[xi], xs.at[xi], x_peers[k]) for k in range(X_CHIPS - 1)]
        backward(0)
        backward(1)
        for copy in round2:
            copy.wait()
        pl.semaphore_wait(ring.at[1], 2)
        zs[zi] = split(summed(xs, X_CHIPS, gx), gx)
        round3 = [send(zs.at[zi], zs.at[zi], z_peers[k]) for k in range(Z_CHIPS - 1)]
        backward(2)
        emit()
        for copy in round3:
            copy.wait()
        fin[gx] = split(summed(zs, Z_CHIPS, gx), gx)
        round4 = [send(fin.at[gx], fin.at[gx], gx_peers[k]) for k in range(7)]
        for copy in round4:
            copy.wait()
    else:
        later_halo()
        backward(0)
        backward(1)
        backward(2)
        emit()
        for i in range(8):
            fin[i] = part16[i]


def finish(scale, dx, fin, dx_hbm, df_hbm, db_hbm, df, db, sem):
    out = pltpu.make_async_copy(dx, dx_hbm, sem.at[0])
    out.start()
    swap = one_hot(128, 128, lambda r, q: r == (q // 32) * 32 + (q % 2) * 16 + (q % 32) // 2).astype(BF)
    final = jnp.dot(fin[...].reshape(256, 128), swap, preferred_element_type=F32) * scale
    for t in range(27):
        block = final[(t // 4) * 32:(t // 4) * 32 + 32]
        if t % 4:
            block = pltpu.roll(block, 128 - 32 * (t % 4), axis=1)
        k = (t // 9) * 9 + (t % 3) * 3 + (t // 3) % 3
        df[k, pl.ds(0, 16, stride=2), :] = block[0:16, 0:32]
        df[k, pl.ds(1, 16, stride=2), :] = block[16:32, 0:32]
    db[...] = pltpu.roll(final[192:200] + final[208:216], 32, axis=1)[0:1, 0:32]
    others = [pltpu.make_async_copy(df, df_hbm, sem.at[1]), pltpu.make_async_copy(db, db_hbm, sem.at[2])]
    for copy in others:
        copy.start()
    for copy in [out] + others:
        copy.wait()


def shards(comm, cells, volume, cotangent, weight, bias):
    vm = pl.BlockSpec(memory_space=pltpu.VMEM)
    hbm = pl.BlockSpec(memory_space=pltpu.MemorySpace.HBM)
    inputs = (volume, cotangent, weight.reshape(27, C, C), bias.reshape(1, C))
    if comm:
        inputs = [pltpu.with_memory_space_constraint(a, pltpu.MemorySpace.HBM) for a in inputs]
    dx, fin = pl.pallas_call(
        functools.partial(kernel, comm),
        out_shape=(jax.ShapeDtypeStruct(volume.shape, BF), jax.ShapeDtypeStruct((8, 32, 128), BF)),
        in_specs=[hbm] * 4,
        out_specs=(vm, vm),
        scratch_shapes=[
            pltpu.VMEM((8, 16, 2048), BF),
            pltpu.VMEM((8, 16, 2048), BF),
            pltpu.VMEM((27, C, C), BF),
            pltpu.VMEM((1, C), F32),
            pltpu.VMEM((12, 320, 128), BF),
            pltpu.VMEM((10, 288, 128), BF),
            pltpu.VMEM((3, 8, 640, 128), BF),
            pltpu.VMEM((6, 576, 128), BF),
            pltpu.VMEM((3, 6, 576, 128), BF),
            pltpu.VMEM((18, 192, 128), BF),
            pltpu.VMEM((18, 192, 128), BF),
            pltpu.VMEM((192, 128), F32),
            pltpu.VMEM((4, 512, 128), BF),
            pltpu.VMEM((8, 32, 128), BF),
            pltpu.VMEM((8, 32, 128), BF),
            pltpu.VMEM((X_CHIPS, 32, 128), BF),
            pltpu.VMEM((Z_CHIPS, 32, 128), BF),
            pltpu.SemaphoreType.DMA((52,)),
            pltpu.SemaphoreType.DMA((52,)),
            pltpu.SemaphoreType.DMA((4,)),
            pltpu.SemaphoreType.REGULAR((2,)),
        ],
        compiler_params=pltpu.CompilerParams(
            collective_id=0 if comm else None, has_side_effects=comm, vmem_limit_bytes=48 << 20),
    )(*inputs)
    dg, df, db = pl.pallas_call(
        functools.partial(finish, 1.0 / math.sqrt(cells)),
        out_shape=(jax.ShapeDtypeStruct(volume.shape, BF),
                   jax.ShapeDtypeStruct((27, C, C), F32),
                   jax.ShapeDtypeStruct((1, C), F32)),
        in_specs=[vm, vm],
        out_specs=[pl.BlockSpec(memory_space=pl.ANY)] * 3,
        scratch_shapes=[pltpu.VMEM((27, C, C), F32), pltpu.VMEM((1, C), F32),
                        pltpu.SemaphoreType.DMA((3,))],
        compiler_params=pltpu.CompilerParams(vmem_limit_bytes=4 << 20),
    )(dx, fin)
    return dg, df.reshape(3, 3, 3, C, C), db.reshape(C)


def solution(mesh):
    cells = 8 * mesh.shape["gx"] * 16 * mesh.shape["gy"] * 64
    in_specs = (P("gx", "gy", None), P("gx", "gy", None), P(), P())
    out_specs = (P("gx", "gy", None), P(), P())
    return jax.shard_map(functools.partial(shards, True, cells), mesh=mesh, in_specs=in_specs,
                         out_specs=out_specs, check_vma=False)
```

```python
import functools
import math

import jax
import jax.numpy as jnp
from jax import lax
from jax.experimental import pallas as pl
from jax.experimental.pallas import tpu as pltpu
from jax.sharding import PartitionSpec as P

C = 32
MESH = pl.DeviceIdType.MESH
BF = jnp.bfloat16
F32 = jnp.float32
X_CHIPS = 4
Z_CHIPS = 8
NT = (((1,), (1,)), ((), ()))


def shifted(block, amount, keep):
    return jnp.where(keep, pltpu.roll(block, amount, axis=1), jnp.zeros_like(block))


def natural(index):
    return 2 * (index % 16) + (index % 32) // 16


def one_hot(rows, cols, test):
    row = lax.broadcasted_iota(jnp.int32, (rows, cols), 0)
    col = lax.broadcasted_iota(jnp.int32, (rows, cols), 1)
    return jnp.where(test(row, col), 1.0, 0.0)


def kernel(comm, vol_hbm, cot_hbm, w_hbm, b_hbm, dx, fin, vol, cot, wbuf, bbuf, nv, nc,
           s, c, gp, t1, t2, tb, dq, part16, rs, xs, zs, ssem, rsem, lsem, ring):
    loads = [pltpu.make_async_copy(a, b, lsem.at[i]) for i, (a, b) in enumerate(
        ((vol_hbm, vol), (cot_hbm, cot), (w_hbm, wbuf), (b_hbm, bbuf)))]
    for load in loads:
        load.start()

    if comm:
        gx = lax.axis_index("gx")
        gy = lax.axis_index("gy")
        ngx = lax.axis_size("gx")
        ngy = lax.axis_size("gy")
        xi = lax.rem(gy, X_CHIPS)
        zi = lax.div(gy, X_CHIPS)

        def at(ax, ay):
            return {"gx": lax.rem(ax + ngx, ngx), "gy": lax.rem(ay + ngy, ngy)}

        around = [(a, b) for a in (-1, 0, 1) for b in (-1, 0, 1) if a or b]
        gx_peers = [at(gx + k, gy) for k in range(1, 8)]
        x_peers = [at(gx, zi * X_CHIPS + lax.rem(xi + k, X_CHIPS)) for k in range(1, X_CHIPS)]
        z_peers = [at(gx, lax.rem(zi + k, Z_CHIPS) * X_CHIPS + xi) for k in range(1, Z_CHIPS)]
        z_near = [z_peers[0], z_peers[Z_CHIPS - 2]]
        z_next = [z_peers[1], z_peers[Z_CHIPS - 3]]
        peers = [at(gx + a, gy + b) for a, b in around if b] + gx_peers + x_peers + z_near
        barrier = pltpu.get_barrier_semaphore()
        for peer in peers:
            pl.semaphore_signal(barrier, inc=1, device_id=peer, device_id_type=MESH)


    lane = lax.broadcasted_iota(jnp.int32, (1, 128), 1)
    low = lane < 64
    z_first = (lane % 64) != 0
    z_last = (lane % 64) != 63
    perm = one_hot(256, 256, lambda r, q: q == (r % 16) * 16 + r // 16).astype(BF)

    def turn(src, dst, first, offset):
        for x in range(0, 8, 2):
            parts = [
                jnp.concatenate([src[x + e, :, g * 128:(g + 1) * 128] for g in range(16)], axis=0)
                for e in range(2)
            ]
            out = jnp.dot(perm, jnp.concatenate(parts, axis=1), preferred_element_type=F32).astype(BF)
            dst[first + x, offset:offset + 256] = out[:, :128]
            dst[first + x + 1, offset:offset + 256] = out[:, 128:]

    used = []

    def send(src, dst, peer):
        index = len(used)
        used.append(index)
        copy = pltpu.make_async_remote_copy(
            src_ref=src, dst_ref=dst, send_sem=ssem.at[index], recv_sem=rsem.at[index],
            device_id=peer, device_id_type=MESH)
        copy.start()
        return copy

    def wipe(ref, *shape):
        ref[...] = jnp.zeros(shape, BF)

    loads[0].wait()
    turn(vol, nv, 2, 32)
    if comm:
        pl.semaphore_wait(barrier, len(peers))
        for peer in z_near:
            pl.semaphore_signal(ring.at[0], inc=1, device_id=peer, device_id_type=MESH)
        wave1 = [
            send(nv.at[2, 32:288], nv.at[10, 32:288], at(gx - 1, gy)),
            send(nv.at[9, 32:288], nv.at[1, 32:288], at(gx + 1, gy)),
            send(nv.at[2:10, 32:48], nv.at[2:10, 288:304], at(gx, gy - 1)),
            send(nv.at[2:10, 272:288], nv.at[2:10, 16:32], at(gx, gy + 1)),
        ]
        inner_x = {-1: (2, 10), 1: (9, 1)}
        inner_y = {-1: (slice(32, 48), slice(288, 304)), 1: (slice(272, 288), slice(16, 32))}
        for a in (-1, 1):
            for b in (-1, 1):
                wave1.append(send(nv.at[inner_x[a][0], inner_y[b][0]],
                                  nv.at[inner_x[a][1], inner_y[b][1]], at(gx + a, gy + b)))
    loads[1].wait()
    turn(cot, nc, 1, 16)
    if comm:
        wave2 = [
            send(nv.at[3, 32:288], nv.at[11, 32:288], at(gx - 1, gy)),
            send(nv.at[8, 32:288], nv.at[0, 32:288], at(gx + 1, gy)),
            send(nv.at[2:10, 48:64], nv.at[2:10, 304:320], at(gx, gy - 1)),
            send(nv.at[2:10, 256:272], nv.at[2:10, 0:16], at(gx, gy + 1)),
        ]
        outer_x = {-1: (3, 11), 1: (8, 0)}
        outer_y = {-1: (slice(48, 64), slice(304, 320)), 1: (slice(256, 272), slice(0, 16))}
        both_y = {-1: (slice(32, 64), slice(288, 320)), 1: (slice(256, 288), slice(0, 32))}
        for a in (-1, 1):
            for b in (-1, 1):
                peer = at(gx + a, gy + b)
                wave2.append(send(nv.at[outer_x[a][0], both_y[b][0]],
                                  nv.at[outer_x[a][1], both_y[b][1]], peer))
                wave2.append(send(nv.at[inner_x[a][0], outer_y[b][0]],
                                  nv.at[inner_x[a][1], outer_y[b][1]], peer))
        side_x = {-1: (slice(1, 2), slice(9, 10)), 0: (slice(1, 9), slice(1, 9)),
                  1: (slice(8, 9), slice(0, 1))}
        side_y = {-1: (slice(16, 32), slice(272, 288)), 0: (slice(16, 272), slice(16, 272)),
                  1: (slice(256, 272), slice(0, 16))}
        for a, b in around:
            wave2.append(send(nc.at[side_x[a][0], side_y[b][0]],
                              nc.at[side_x[a][1], side_y[b][1]], at(gx + a, gy + b)))

    def paired(buf, j, r0, r1):
        rows = (r1 - r0) // 16
        a = buf[j, r0:r1]
        b = buf[j + 4, r0:r1]
        even = jnp.where(low, a, pltpu.roll(b, 64, axis=1))
        odd = jnp.where(low, pltpu.roll(a, 64, axis=1), b)
        both = jnp.concatenate(
            [even.reshape(rows, 1, 16, 128), odd.reshape(rows, 1, 16, 128)], axis=1)
        return both.reshape(rows * 32, 128)

    def fill_s(j, y0, y1):
        block = paired(nv, j, y0 * 16, y1 * 16)
        s[1, j, y0 * 32:y1 * 32] = block
        s[0, j, y0 * 32:y1 * 32] = shifted(block, 1, z_first)
        s[2, j, y0 * 32:y1 * 32] = shifted(block, 127, z_last)

    def fill_c(j, y0, y1):
        c[j, y0 * 32:y1 * 32] = paired(nc, j, y0 * 16, y1 * 16)

    @pl.loop(2, 6)
    def _(j):
        fill_s(j, 2, 18)

    @pl.loop(1, 5)
    def _(j):
        fill_c(j, 1, 17)

    def spread(t, kk, base):
        turned = [base] + [pltpu.roll(base, 32 * i, axis=1) for i in (1, 2, 3)]
        zero = jnp.zeros_like(base)
        rows = [(base, zero), (turned[1], zero),
                (jnp.where(lane >= 64, turned[2], zero), jnp.where(lane < 64, turned[2], zero)),
                (jnp.where(lane >= 96, turned[3], zero), jnp.where(lane < 96, turned[3], zero)),
                (zero, base), (zero, turned[1])]
        for yo in range(6):
            for half in range(2):
                t[2 * kk + half, yo * 32:(yo + 1) * 32] = rows[yo][half]

    loads[2].wait()
    loads[3].wait()
    rows4 = one_hot(128, 128, lambda r, q: (r // 32 == q // 32) & (q % 32 == natural(r))).astype(BF)
    lanes1 = one_hot(32, 32, lambda r, q: q == natural(r)).astype(BF)
    stacked = []
    for kk in range(9):
        raw = jnp.concatenate([wbuf[(kk // 3) * 9 + ky * 3 + kk % 3] for ky in range(3)]
                              + [jnp.zeros((32, 32), BF)], axis=0)
        stacked.append(jnp.dot(rows4, raw, preferred_element_type=F32).astype(BF))
        spread(t1, kk, lax.dot_general(lanes1, stacked[kk], NT, preferred_element_type=F32).astype(BF))
    base = sum(jnp.dot(jnp.concatenate([stacked[kk][(2 - d) * 32:(3 - d) * 32] for kk in range(9)], axis=0),
                       one_hot(32, 128, lambda r, q: (q // 32 == d) & (r == natural(q))).astype(BF),
                       preferred_element_type=F32) for d in range(3)).astype(BF)
    for kk in range(9):
        spread(t2, kk, base[kk * 32:(kk + 1) * 32])
    tb[...] = lax.dot_general(
        one_hot(192, 32, lambda r, q: q == natural(r)),
        jnp.broadcast_to(bbuf[...], (128, 32)), NT,
        preferred_element_type=F32, precision=lax.Precision.HIGHEST)

    if comm:
        pl.semaphore_wait(ring.at[0], 2)
        for peer in z_next:
            pl.semaphore_signal(ring.at[1], inc=1, device_id=peer, device_id_type=MESH)
        for copy in wave1:
            copy.wait()

        @pl.when(gx == 0)
        def _():
            wipe(nv.at[1, 16:304], 288, 128)

        @pl.when(gx == ngx - 1)
        def _():
            wipe(nv.at[10, 16:304], 288, 128)

        @pl.when(gy == 0)
        def _():
            wipe(nv.at[1:11, 16:32], 10, 16, 128)

        @pl.when(gy == ngy - 1)
        def _():
            wipe(nv.at[1:11, 288:304], 10, 16, 128)
    else:
        wipe(nv.at[0:2], 2, 320, 128)
        wipe(nv.at[10:12], 2, 320, 128)
        wipe(nv.at[:, 0:32], 12, 32, 128)
        wipe(nv.at[:, 288:320], 12, 32, 128)
        wipe(nc.at[0], 288, 128)
        wipe(nc.at[9], 288, 128)
        wipe(nc.at[:, 0:16], 10, 16, 128)
        wipe(nc.at[:, 272:288], 10, 16, 128)

    fill_s(1, 1, 19)
    fill_s(6, 1, 19)
    for j in range(2, 6):
        fill_s(j, 1, 2)
        fill_s(j, 18, 19)

    def tiles(buf, kz, cells, r0, r1):
        return jnp.concatenate([buf[kz, cell, r0:r1] for cell in cells], axis=1)

    def filter_rows(t, r0, r1, halves=(0, 1)):
        return jnp.concatenate([t[2 * kk + h, r0:r1] for kk in range(9) for h in halves], axis=1)

    def activate(acc, r0, r1, cells, y):
        for e, cell in enumerate(cells):
            pre = acc[:, e * 128:(e + 1) * 128] + tb[r0:r1]
            sig = 0.5 * jnp.tanh(0.5 * pre) + 0.5
            grad = c[cell, y:y + r1 - r0].astype(F32)
            block = (grad * sig * (1.0 + pre * (1.0 - sig))).astype(BF)
            gp[1, cell, y:y + r1 - r0] = block
            gp[0, cell, y:y + r1 - r0] = shifted(block, 127, z_last)
            gp[2, cell, y:y + r1 - r0] = shifted(block, 1, z_first)

    def forward(r0, r1, y_in, y_out, cells):
        rhs = jnp.concatenate(
            [tiles(s, kz, [cell + kx for cell in cells], y_in * 32, y_in * 32 + 256)
             for kx in range(3) for kz in range(3)], axis=0)
        acc = jnp.dot(filter_rows(t1, r0, r1), rhs, preferred_element_type=F32)
        activate(acc, r0, r1, cells, y_out * 32)

    for b in range(8):
        for cells in ((1, 2), (3, 4)):
            rhs = jnp.concatenate(
                [tiles(s, kz, [cell + kx for cell in cells], (2 * b + 1) * 32, (2 * b + 5) * 32)
                 for kx in range(3) for kz in range(3)], axis=0)
            acc = jnp.dot(filter_rows(t1, 0, 64, (0,)), rhs, preferred_element_type=F32)
            activate(acc, 0, 64, cells, (2 * b + 1) * 32)

    group = lane // 32

    lower = lax.broadcasted_iota(jnp.int32, (32, 128), 0) >= 16

    def split(value, index):
        rounded = value.astype(BF)
        rest = (value - rounded.astype(F32)).astype(BF)
        return jnp.where((index == 6) & (group == 3) & lower, rest, rounded)

    def joined(value, index):
        both = value + jnp.concatenate([value[16:], value[:16]], axis=0)
        return jnp.where((index == 6) & (group == 3), both, value)

    done = []

    def put(four):
        value = jnp.where(group == 0, four[0], jnp.where(group == 1, four[1],
                          jnp.where(group == 2, four[2], four[3])))
        part16[len(done)] = split(value, len(done)) if len(done) == 6 else value.astype(BF)
        done.append(0)

    own = range(1, 5)
    right = jnp.concatenate(
        [jnp.concatenate([tiles(gp, kz, own, (2 * b + 1) * 32, (2 * b + 3) * 32) for kz in range(3)], axis=0)
         for b in range(8)], axis=1)
    even = group % 2 == 0
    blocks = []

    def placed(value, source):
        turns = (len(done) * 4 + len(blocks) - source) % 4
        blocks.append(pltpu.roll(value, 32 * turns, axis=1) if turns else value)
        if len(blocks) == 4:
            put(blocks)
            blocks.clear()

    for kx in range(3):
        left = jnp.concatenate(
            [tiles(s, 1, [kx + cell for cell in own], (2 * b + 1) * 32, (2 * b + 5) * 32)
             for b in range(8)], axis=1)
        if kx == 0:
            left = jnp.concatenate([left, jnp.ones((16, 4096), BF)], axis=0)
        wide = lax.dot_general(left, right, NT, preferred_element_type=F32)
        wide = [wide[:, :128], jnp.concatenate([wide[:, 128:], jnp.zeros_like(wide[:, 128:])], axis=1)]
        if kx == 0:
            sums = wide[0][128:144] + pltpu.roll(wide[0][128:144], 96, axis=1)
        for kz in range(3):
            for ky in range(3):
                half = wide[kz // 2]
                both = jnp.where(even, half[ky * 32:ky * 32 + 32], half[ky * 32 + 32:ky * 32 + 64])
                placed(both + pltpu.roll(both, 96, axis=1), 2 * (kz % 2))
    placed(jnp.concatenate([sums, sums], axis=0), 2)
    part16[7] = jnp.zeros((32, 128), BF)

    def later_halo():
        if comm:
            for copy in wave2:
                copy.wait()

            @pl.when(gx == 0)
            def _():
                wipe(nv.at[0], 320, 128)
                wipe(nv.at[1, 0:16], 16, 128)
                wipe(nv.at[1, 304:320], 16, 128)
                wipe(nc.at[0], 288, 128)

            @pl.when(gx == ngx - 1)
            def _():
                wipe(nv.at[11], 320, 128)
                wipe(nv.at[10, 0:16], 16, 128)
                wipe(nv.at[10, 304:320], 16, 128)
                wipe(nc.at[9], 288, 128)

            @pl.when(gy == 0)
            def _():
                wipe(nv.at[:, 0:16], 12, 16, 128)
                wipe(nv.at[0, 16:32], 16, 128)
                wipe(nv.at[11, 16:32], 16, 128)
                wipe(nc.at[:, 0:16], 10, 16, 128)

            @pl.when(gy == ngy - 1)
            def _():
                wipe(nv.at[:, 304:320], 12, 16, 128)
                wipe(nv.at[0, 288:304], 16, 128)
                wipe(nv.at[11, 288:304], 16, 128)
                wipe(nc.at[:, 272:288], 10, 16, 128)

        for j in (0, 7):
            fill_s(j, 0, 20)
        for j in range(1, 7):
            fill_s(j, 0, 1)
            fill_s(j, 19, 20)
        for j in (0, 5):
            fill_c(j, 0, 18)
        for j in own:
            fill_c(j, 0, 1)
            fill_c(j, 17, 18)
        for b in range(3):
            forward(0, 192, 6 * b, 6 * b, (0, 5))
        for cells in ((1, 2), (3, 4)):
            for half, y_in, r0, y_out in ((0, 0, 0, 0), (1, 16, 160, 17)):
                rhs = jnp.concatenate(
                    [tiles(s, kz, [cell + kx for cell in cells], y_in * 32, y_in * 32 + 128)
                     for kx in range(3) for kz in range(3)], axis=0)
                acc = jnp.dot(filter_rows(t1, r0, r0 + 32, (half,)), rhs, preferred_element_type=F32)
                activate(acc, r0, r0 + 32, cells, y_out * 32)

    def backward(b):
        start, r0 = ((0, 0), (6, 0), (10, 64))[b]
        left = filter_rows(t2, r0, 192)
        out = start * 32 + r0
        for n in range(2):
            rhs = jnp.concatenate(
                [tiles(gp, kz, (2 * n + 2 - kx, 2 * n + 3 - kx), start * 32, start * 32 + 256)
                 for kx in range(3) for kz in range(3)], axis=0)
            acc = jnp.dot(left, rhs, preferred_element_type=F32).astype(BF)
            dq[2 * n, out:out + 192 - r0] = acc[:, :128]
            dq[2 * n + 1, out:out + 192 - r0] = acc[:, 128:]

    def emit():
        for j in range(4):
            block = dq[j].reshape(16, 2, 16, 128)
            even = block[:, 0].reshape(256, 128)
            odd = block[:, 1].reshape(256, 128)
            first = jnp.where(low, even, pltpu.roll(odd, 64, axis=1))
            second = jnp.where(low, pltpu.roll(even, 64, axis=1), odd)
            out = jnp.dot(perm, jnp.concatenate([first, second], axis=1),
                          preferred_element_type=F32).astype(BF)
            for g in range(16):
                dx[j, :, g * 128:(g + 1) * 128] = out[g * 16:(g + 1) * 16, :128]
                dx[j + 4, :, g * 128:(g + 1) * 128] = out[g * 16:(g + 1) * 16, 128:]

    def summed(buf, count, index):
        total = buf[0].astype(F32)
        for k in range(1, count):
            total = total + buf[k].astype(F32)
        return joined(total, index)

    if comm:
        round1 = [send(part16.at[lax.rem(gx + k + 1, 8)], rs.at[k], gx_peers[k]) for k in range(7)]
        rs[7] = part16[gx]
        later_halo()
        for copy in round1:
            copy.wait()
        xs[xi] = split(summed(rs, 8, gx), gx)
        round2 = [send(xs.at[xi], xs.at[xi], x_peers[k]) for k in range(X_CHIPS - 1)]
        backward(0)
        backward(1)
        for copy in round2:
            copy.wait()
        pl.semaphore_wait(ring.at[1], 2)
        zs[zi] = split(summed(xs, X_CHIPS, gx), gx)
        round3 = [send(zs.at[zi], zs.at[zi], z_peers[k]) for k in range(Z_CHIPS - 1)]
        backward(2)
        emit()
        for copy in round3:
            copy.wait()
        fin[gx] = split(summed(zs, Z_CHIPS, gx), gx)
        round4 = [send(fin.at[gx], fin.at[gx], gx_peers[k]) for k in range(7)]
        for copy in round4:
            copy.wait()
    else:
        later_halo()
        backward(0)
        backward(1)
        backward(2)
        emit()
        for i in range(8):
            fin[i] = part16[i]


def finish(scale, dx, fin, dx_hbm, df_hbm, db_hbm, df, db, sem):
    out = pltpu.make_async_copy(dx, dx_hbm, sem.at[0])
    out.start()
    swap = one_hot(128, 128, lambda r, q: r == (q // 32) * 32 + (q % 2) * 16 + (q % 32) // 2).astype(BF)
    final = jnp.dot(fin[...].reshape(256, 128), swap, preferred_element_type=F32) * scale
    others = []
    for t in range(27):
        block = final[(t // 4) * 32:(t // 4) * 32 + 32]
        if t % 4:
            block = pltpu.roll(block, 128 - 32 * (t % 4), axis=1)
        k = (t // 9) * 9 + (t % 3) * 3 + (t // 3) % 3
        df[k, pl.ds(0, 16, stride=2), :] = block[0:16, 0:32]
        df[k, pl.ds(1, 16, stride=2), :] = block[16:32, 0:32]
        if t % 9 == 8:
            planes = slice(t - 8, t + 1)
            others.append(pltpu.make_async_copy(df.at[planes], df_hbm.at[planes], sem.at[1 + t // 9]))
            others[-1].start()
    db[...] = pltpu.roll(final[192:200] + final[208:216], 32, axis=1)[0:1, 0:32]
    others.append(pltpu.make_async_copy(db, db_hbm, sem.at[4]))
    others[-1].start()
    for copy in [out] + others:
        copy.wait()


def shards(comm, cells, volume, cotangent, weight, bias):
    vm = pl.BlockSpec(memory_space=pltpu.VMEM)
    hbm = pl.BlockSpec(memory_space=pltpu.MemorySpace.HBM)
    inputs = (volume, cotangent, weight.reshape(27, C, C), bias.reshape(1, C))
    if comm:
        inputs = [pltpu.with_memory_space_constraint(a, pltpu.MemorySpace.HBM) for a in inputs]
    dx, fin = pl.pallas_call(
        functools.partial(kernel, comm),
        out_shape=(jax.ShapeDtypeStruct(volume.shape, BF), jax.ShapeDtypeStruct((8, 32, 128), BF)),
        in_specs=[hbm] * 4,
        out_specs=(vm, vm),
        scratch_shapes=[
            pltpu.VMEM((8, 16, 2048), BF),
            pltpu.VMEM((8, 16, 2048), BF),
            pltpu.VMEM((27, C, C), BF),
            pltpu.VMEM((1, C), F32),
            pltpu.VMEM((12, 320, 128), BF),
            pltpu.VMEM((10, 288, 128), BF),
            pltpu.VMEM((3, 8, 640, 128), BF),
            pltpu.VMEM((6, 576, 128), BF),
            pltpu.VMEM((3, 6, 576, 128), BF),
            pltpu.VMEM((18, 192, 128), BF),
            pltpu.VMEM((18, 192, 128), BF),
            pltpu.VMEM((192, 128), F32),
            pltpu.VMEM((4, 512, 128), BF),
            pltpu.VMEM((8, 32, 128), BF),
            pltpu.VMEM((8, 32, 128), BF),
            pltpu.VMEM((X_CHIPS, 32, 128), BF),
            pltpu.VMEM((Z_CHIPS, 32, 128), BF),
            pltpu.SemaphoreType.DMA((52,)),
            pltpu.SemaphoreType.DMA((52,)),
            pltpu.SemaphoreType.DMA((4,)),
            pltpu.SemaphoreType.REGULAR((2,)),
        ],
        compiler_params=pltpu.CompilerParams(
            collective_id=0 if comm else None, has_side_effects=comm, vmem_limit_bytes=48 << 20),
    )(*inputs)
    dg, df, db = pl.pallas_call(
        functools.partial(finish, 1.0 / math.sqrt(cells)),
        out_shape=(jax.ShapeDtypeStruct(volume.shape, BF),
                   jax.ShapeDtypeStruct((27, C, C), F32),
                   jax.ShapeDtypeStruct((1, C), F32)),
        in_specs=[vm, vm],
        out_specs=[pl.BlockSpec(memory_space=pl.ANY)] * 3,
        scratch_shapes=[pltpu.VMEM((27, C, C), F32), pltpu.VMEM((1, C), F32),
                        pltpu.SemaphoreType.DMA((5,))],
        compiler_params=pltpu.CompilerParams(vmem_limit_bytes=4 << 20),
    )(dx, fin)
    return dg, df.reshape(3, 3, 3, C, C), db.reshape(C)


def solution(mesh):
    cells = 8 * mesh.shape["gx"] * 16 * mesh.shape["gy"] * 64
    in_specs = (P("gx", "gy", None), P("gx", "gy", None), P(), P())
    out_specs = (P("gx", "gy", None), P(), P())
    return jax.shard_map(functools.partial(shards, True, cells), mesh=mesh, in_specs=in_specs,
                         out_specs=out_specs, check_vma=False)
```

```python
import functools
import math

import jax
import jax.numpy as jnp
from jax import lax
from jax.experimental import pallas as pl
from jax.experimental.pallas import tpu as pltpu
from jax.sharding import PartitionSpec as P

C = 32
MESH = pl.DeviceIdType.MESH
BF = jnp.bfloat16
F32 = jnp.float32
X_CHIPS = 4
Z_CHIPS = 8
NT = (((1,), (1,)), ((), ()))


def shifted(block, amount, keep):
    return jnp.where(keep, pltpu.roll(block, amount, axis=1), jnp.zeros_like(block))


def natural(index):
    return 2 * (index % 16) + (index % 32) // 16


def one_hot(rows, cols, test):
    row = lax.broadcasted_iota(jnp.int32, (rows, cols), 0)
    col = lax.broadcasted_iota(jnp.int32, (rows, cols), 1)
    return jnp.where(test(row, col), 1.0, 0.0)


def kernel(comm, vol_hbm, cot_hbm, w_hbm, b_hbm, dx, fin, vol, cot, wbuf, bbuf, nv, nc,
           s, c, gp, t1, t2, tb, dq, part16, rs, xs, zs, ssem, rsem, lsem, ring):
    loads = [pltpu.make_async_copy(a, b, lsem.at[i]) for i, (a, b) in enumerate(
        ((vol_hbm, vol), (cot_hbm, cot), (w_hbm, wbuf), (b_hbm, bbuf)))]
    for load in loads:
        load.start()

    if comm:
        gx = lax.axis_index("gx")
        gy = lax.axis_index("gy")
        ngx = lax.axis_size("gx")
        ngy = lax.axis_size("gy")
        xi = lax.rem(gy, X_CHIPS)
        zi = lax.div(gy, X_CHIPS)

        def at(ax, ay):
            return {"gx": lax.rem(ax + ngx, ngx), "gy": lax.rem(ay + ngy, ngy)}

        around = [(a, b) for a in (-1, 0, 1) for b in (-1, 0, 1) if a or b]
        gx_peers = [at(gx + k, gy) for k in range(1, 8)]
        x_peers = [at(gx, zi * X_CHIPS + lax.rem(xi + k, X_CHIPS)) for k in range(1, X_CHIPS)]
        z_peers = [at(gx, lax.rem(zi + k, Z_CHIPS) * X_CHIPS + xi) for k in range(1, Z_CHIPS)]
        z_near = [z_peers[0], z_peers[Z_CHIPS - 2]]
        z_next = [z_peers[1], z_peers[Z_CHIPS - 3]]
        peers = [at(gx + a, gy + b) for a, b in around if b] + gx_peers + x_peers + z_near
        barrier = pltpu.get_barrier_semaphore()
        for peer in peers:
            pl.semaphore_signal(barrier, inc=1, device_id=peer, device_id_type=MESH)


    lane = lax.broadcasted_iota(jnp.int32, (1, 128), 1)
    low = lane < 64
    z_first = (lane % 64) != 0
    z_last = (lane % 64) != 63
    perm = one_hot(256, 256, lambda r, q: q == (r % 16) * 16 + r // 16).astype(BF)

    def turn(src, dst, first, offset):
        for x in range(0, 8, 2):
            parts = [
                jnp.concatenate([src[x + e, :, g * 128:(g + 1) * 128] for g in range(16)], axis=0)
                for e in range(2)
            ]
            out = jnp.dot(perm, jnp.concatenate(parts, axis=1), preferred_element_type=F32).astype(BF)
            dst[first + x, offset:offset + 256] = out[:, :128]
            dst[first + x + 1, offset:offset + 256] = out[:, 128:]

    used = []

    def send(src, dst, peer):
        index = len(used)
        used.append(index)
        copy = pltpu.make_async_remote_copy(
            src_ref=src, dst_ref=dst, send_sem=ssem.at[index], recv_sem=rsem.at[index],
            device_id=peer, device_id_type=MESH)
        copy.start()
        return copy

    def wipe(ref, *shape):
        ref[...] = jnp.zeros(shape, BF)

    loads[0].wait()
    turn(vol, nv, 2, 32)
    if comm:
        pl.semaphore_wait(barrier, len(peers))
        for peer in z_near:
            pl.semaphore_signal(ring.at[0], inc=1, device_id=peer, device_id_type=MESH)
        wave1 = [
            send(nv.at[2, 32:288], nv.at[10, 32:288], at(gx - 1, gy)),
            send(nv.at[9, 32:288], nv.at[1, 32:288], at(gx + 1, gy)),
            send(nv.at[2:10, 32:48], nv.at[2:10, 288:304], at(gx, gy - 1)),
            send(nv.at[2:10, 272:288], nv.at[2:10, 16:32], at(gx, gy + 1)),
        ]
        inner_x = {-1: (2, 10), 1: (9, 1)}
        inner_y = {-1: (slice(32, 48), slice(288, 304)), 1: (slice(272, 288), slice(16, 32))}
        for a in (-1, 1):
            for b in (-1, 1):
                wave1.append(send(nv.at[inner_x[a][0], inner_y[b][0]],
                                  nv.at[inner_x[a][1], inner_y[b][1]], at(gx + a, gy + b)))
    loads[1].wait()
    turn(cot, nc, 1, 16)
    if comm:
        wave2 = [
            send(nv.at[3, 32:288], nv.at[11, 32:288], at(gx - 1, gy)),
            send(nv.at[8, 32:288], nv.at[0, 32:288], at(gx + 1, gy)),
            send(nv.at[2:10, 48:64], nv.at[2:10, 304:320], at(gx, gy - 1)),
            send(nv.at[2:10, 256:272], nv.at[2:10, 0:16], at(gx, gy + 1)),
        ]
        outer_x = {-1: (3, 11), 1: (8, 0)}
        outer_y = {-1: (slice(48, 64), slice(304, 320)), 1: (slice(256, 272), slice(0, 16))}
        both_y = {-1: (slice(32, 64), slice(288, 320)), 1: (slice(256, 288), slice(0, 32))}
        for a in (-1, 1):
            for b in (-1, 1):
                peer = at(gx + a, gy + b)
                wave2.append(send(nv.at[outer_x[a][0], both_y[b][0]],
                                  nv.at[outer_x[a][1], both_y[b][1]], peer))
                wave2.append(send(nv.at[inner_x[a][0], outer_y[b][0]],
                                  nv.at[inner_x[a][1], outer_y[b][1]], peer))
        side_x = {-1: (slice(1, 2), slice(9, 10)), 0: (slice(1, 9), slice(1, 9)),
                  1: (slice(8, 9), slice(0, 1))}
        side_y = {-1: (slice(16, 32), slice(272, 288)), 0: (slice(16, 272), slice(16, 272)),
                  1: (slice(256, 272), slice(0, 16))}
        for a, b in around:
            wave2.append(send(nc.at[side_x[a][0], side_y[b][0]],
                              nc.at[side_x[a][1], side_y[b][1]], at(gx + a, gy + b)))

    def paired(buf, j, r0, r1):
        rows = (r1 - r0) // 16
        a = buf[j, r0:r1]
        b = buf[j + 4, r0:r1]
        even = jnp.where(low, a, pltpu.roll(b, 64, axis=1))
        odd = jnp.where(low, pltpu.roll(a, 64, axis=1), b)
        both = jnp.concatenate(
            [even.reshape(rows, 1, 16, 128), odd.reshape(rows, 1, 16, 128)], axis=1)
        return both.reshape(rows * 32, 128)

    def fill_s(j, y0, y1):
        block = paired(nv, j, y0 * 16, y1 * 16)
        s[1, j, y0 * 32:y1 * 32] = block
        s[0, j, y0 * 32:y1 * 32] = shifted(block, 1, z_first)
        s[2, j, y0 * 32:y1 * 32] = shifted(block, 127, z_last)

    def fill_c(j, y0, y1):
        c[j, y0 * 32:y1 * 32] = paired(nc, j, y0 * 16, y1 * 16)

    @pl.loop(2, 6)
    def _(j):
        fill_s(j, 2, 18)

    @pl.loop(1, 5)
    def _(j):
        fill_c(j, 1, 17)

    def spread(t, kk, base):
        turned = [base] + [pltpu.roll(base, 32 * i, axis=1) for i in (1, 2, 3)]
        zero = jnp.zeros_like(base)
        rows = [(base, zero), (turned[1], zero),
                (jnp.where(lane >= 64, turned[2], zero), jnp.where(lane < 64, turned[2], zero)),
                (jnp.where(lane >= 96, turned[3], zero), jnp.where(lane < 96, turned[3], zero)),
                (zero, base), (zero, turned[1])]
        for yo in range(6):
            for half in range(2):
                t[2 * kk + half, yo * 32:(yo + 1) * 32] = rows[yo][half]

    loads[2].wait()
    loads[3].wait()
    rows4 = one_hot(128, 128, lambda r, q: (r // 32 == q // 32) & (q % 32 == natural(r))).astype(BF)
    lanes1 = one_hot(32, 32, lambda r, q: q == natural(r)).astype(BF)
    stacked = []
    for kk in range(9):
        raw = jnp.concatenate([wbuf[(kk // 3) * 9 + ky * 3 + kk % 3] for ky in range(3)]
                              + [jnp.zeros((32, 32), BF)], axis=0)
        stacked.append(jnp.dot(rows4, raw, preferred_element_type=F32).astype(BF))
        spread(t1, kk, lax.dot_general(lanes1, stacked[kk], NT, preferred_element_type=F32).astype(BF))
    base = sum(jnp.dot(jnp.concatenate([stacked[kk][(2 - d) * 32:(3 - d) * 32] for kk in range(9)], axis=0),
                       one_hot(32, 128, lambda r, q: (q // 32 == d) & (r == natural(q))).astype(BF),
                       preferred_element_type=F32) for d in range(3)).astype(BF)
    for kk in range(9):
        spread(t2, kk, base[kk * 32:(kk + 1) * 32])
    tb[...] = lax.dot_general(
        one_hot(192, 32, lambda r, q: q == natural(r)),
        jnp.broadcast_to(bbuf[...], (128, 32)), NT,
        preferred_element_type=F32, precision=lax.Precision.HIGHEST)

    if comm:
        pl.semaphore_wait(ring.at[0], 2)
        for peer in z_next:
            pl.semaphore_signal(ring.at[1], inc=1, device_id=peer, device_id_type=MESH)
        for copy in wave1:
            copy.wait()

        @pl.when(gx == 0)
        def _():
            wipe(nv.at[1, 16:304], 288, 128)

        @pl.when(gx == ngx - 1)
        def _():
            wipe(nv.at[10, 16:304], 288, 128)

        @pl.when(gy == 0)
        def _():
            wipe(nv.at[1:11, 16:32], 10, 16, 128)

        @pl.when(gy == ngy - 1)
        def _():
            wipe(nv.at[1:11, 288:304], 10, 16, 128)
    else:
        wipe(nv.at[0:2], 2, 320, 128)
        wipe(nv.at[10:12], 2, 320, 128)
        wipe(nv.at[:, 0:32], 12, 32, 128)
        wipe(nv.at[:, 288:320], 12, 32, 128)
        wipe(nc.at[0], 288, 128)
        wipe(nc.at[9], 288, 128)
        wipe(nc.at[:, 0:16], 10, 16, 128)
        wipe(nc.at[:, 272:288], 10, 16, 128)

    fill_s(1, 1, 19)
    fill_s(6, 1, 19)
    for j in range(2, 6):
        fill_s(j, 1, 2)
        fill_s(j, 18, 19)

    def tiles(buf, kz, cells, r0, r1):
        return jnp.concatenate([buf[kz, cell, r0:r1] for cell in cells], axis=1)

    def filter_rows(t, r0, r1, halves=(0, 1)):
        return jnp.concatenate([t[2 * kk + h, r0:r1] for kk in range(9) for h in halves], axis=1)

    def activate(acc, r0, r1, cells, y):
        for e, cell in enumerate(cells):
            pre = acc[:, e * 128:(e + 1) * 128] + tb[r0:r1]
            sig = 0.5 * jnp.tanh(0.5 * pre) + 0.5
            grad = c[cell, y:y + r1 - r0].astype(F32)
            block = (grad * sig * (1.0 + pre * (1.0 - sig))).astype(BF)
            gp[1, cell, y:y + r1 - r0] = block
            gp[0, cell, y:y + r1 - r0] = shifted(block, 127, z_last)
            gp[2, cell, y:y + r1 - r0] = shifted(block, 1, z_first)

    def forward(r0, r1, y_in, y_out, cells):
        rhs = jnp.concatenate(
            [tiles(s, kz, [cell + kx for cell in cells], y_in * 32, y_in * 32 + 256)
             for kx in range(3) for kz in range(3)], axis=0)
        acc = jnp.dot(filter_rows(t1, r0, r1), rhs, preferred_element_type=F32)
        activate(acc, r0, r1, cells, y_out * 32)

    for b in range(8):
        for cells in ((1, 2), (3, 4)):
            rhs = jnp.concatenate(
                [tiles(s, kz, [cell + kx for cell in cells], (2 * b + 1) * 32, (2 * b + 5) * 32)
                 for kx in range(3) for kz in range(3)], axis=0)
            acc = jnp.dot(filter_rows(t1, 0, 64, (0,)), rhs, preferred_element_type=F32)
            activate(acc, 0, 64, cells, (2 * b + 1) * 32)

    group = lane // 32

    lower = lax.broadcasted_iota(jnp.int32, (32, 128), 0) >= 16

    def split(value, index):
        rounded = value.astype(BF)
        rest = (value - rounded.astype(F32)).astype(BF)
        return jnp.where((index == 6) & (group == 3) & lower, rest, rounded)

    def joined(value, index):
        both = value + jnp.concatenate([value[16:], value[:16]], axis=0)
        return jnp.where((index == 6) & (group == 3), both, value)

    done = []

    def put(four):
        value = jnp.where(group == 0, four[0], jnp.where(group == 1, four[1],
                          jnp.where(group == 2, four[2], four[3])))
        part16[len(done)] = split(value, len(done)) if len(done) == 6 else value.astype(BF)
        done.append(0)

    own = range(1, 5)
    right = jnp.concatenate(
        [jnp.concatenate([tiles(gp, kz, own, (2 * b + 1) * 32, (2 * b + 3) * 32) for kz in range(3)], axis=0)
         for b in range(8)], axis=1)
    even = group % 2 == 0
    blocks = []

    def placed(value, source):
        turns = (len(done) * 4 + len(blocks) - source) % 4
        blocks.append(pltpu.roll(value, 32 * turns, axis=1) if turns else value)
        if len(blocks) == 4:
            put(blocks)
            blocks.clear()

    for kx in range(3):
        left = jnp.concatenate(
            [tiles(s, 1, [kx + cell for cell in own], (2 * b + 1) * 32, (2 * b + 5) * 32)
             for b in range(8)], axis=1)
        if kx == 0:
            left = jnp.concatenate([left, jnp.ones((16, 4096), BF)], axis=0)
        wide = lax.dot_general(left, right, NT, preferred_element_type=F32)
        wide = [wide[:, :128], jnp.concatenate([wide[:, 128:], jnp.zeros_like(wide[:, 128:])], axis=1)]
        if kx == 0:
            sums = wide[0][128:144] + pltpu.roll(wide[0][128:144], 96, axis=1)
        for kz in range(3):
            for ky in range(3):
                half = wide[kz // 2]
                both = jnp.where(even, half[ky * 32:ky * 32 + 32], half[ky * 32 + 32:ky * 32 + 64])
                placed(both + pltpu.roll(both, 96, axis=1), 2 * (kz % 2))
    placed(jnp.concatenate([sums, sums], axis=0), 2)
    part16[7] = jnp.zeros((32, 128), BF)

    def later_halo():
        if comm:
            for copy in wave2:
                copy.wait()

            @pl.when(gx == 0)
            def _():
                wipe(nv.at[0], 320, 128)
                wipe(nv.at[1, 0:16], 16, 128)
                wipe(nv.at[1, 304:320], 16, 128)
                wipe(nc.at[0], 288, 128)

            @pl.when(gx == ngx - 1)
            def _():
                wipe(nv.at[11], 320, 128)
                wipe(nv.at[10, 0:16], 16, 128)
                wipe(nv.at[10, 304:320], 16, 128)
                wipe(nc.at[9], 288, 128)

            @pl.when(gy == 0)
            def _():
                wipe(nv.at[:, 0:16], 12, 16, 128)
                wipe(nv.at[0, 16:32], 16, 128)
                wipe(nv.at[11, 16:32], 16, 128)
                wipe(nc.at[:, 0:16], 10, 16, 128)

            @pl.when(gy == ngy - 1)
            def _():
                wipe(nv.at[:, 304:320], 12, 16, 128)
                wipe(nv.at[0, 288:304], 16, 128)
                wipe(nv.at[11, 288:304], 16, 128)
                wipe(nc.at[:, 272:288], 10, 16, 128)

        for j in (0, 7):
            fill_s(j, 0, 20)
        for j in range(1, 7):
            fill_s(j, 0, 1)
            fill_s(j, 19, 20)
        for j in (0, 5):
            fill_c(j, 0, 18)
        for j in own:
            fill_c(j, 0, 1)
            fill_c(j, 17, 18)
        for b in range(3):
            forward(0, 192, 6 * b, 6 * b, (0, 5))
        for cells in ((1, 2), (3, 4)):
            for half, y_in, r0, y_out in ((0, 0, 0, 0), (1, 16, 160, 17)):
                rhs = jnp.concatenate(
                    [tiles(s, kz, [cell + kx for cell in cells], y_in * 32, y_in * 32 + 128)
                     for kx in range(3) for kz in range(3)], axis=0)
                acc = jnp.dot(filter_rows(t1, r0, r0 + 32, (half,)), rhs, preferred_element_type=F32)
                activate(acc, r0, r0 + 32, cells, y_out * 32)

    def backward(b):
        start, r0 = ((0, 0), (6, 0), (10, 64))[b]
        left = filter_rows(t2, r0, 192)
        out = start * 32 + r0
        for n in range(2):
            rhs = jnp.concatenate(
                [tiles(gp, kz, (2 * n + 2 - kx, 2 * n + 3 - kx), start * 32, start * 32 + 256)
                 for kx in range(3) for kz in range(3)], axis=0)
            acc = jnp.dot(left, rhs, preferred_element_type=F32).astype(BF)
            dq[2 * n, out:out + 192 - r0] = acc[:, :128]
            dq[2 * n + 1, out:out + 192 - r0] = acc[:, 128:]

    def emit():
        for j in range(4):
            block = dq[j].reshape(16, 2, 16, 128)
            even = block[:, 0].reshape(256, 128)
            odd = block[:, 1].reshape(256, 128)
            first = jnp.where(low, even, pltpu.roll(odd, 64, axis=1))
            second = jnp.where(low, pltpu.roll(even, 64, axis=1), odd)
            out = jnp.dot(perm, jnp.concatenate([first, second], axis=1),
                          preferred_element_type=F32).astype(BF)
            for g in range(16):
                dx[j, :, g * 128:(g + 1) * 128] = out[g * 16:(g + 1) * 16, :128]
                dx[j + 4, :, g * 128:(g + 1) * 128] = out[g * 16:(g + 1) * 16, 128:]

    def summed(buf, count, index):
        total = buf[0].astype(F32)
        for k in range(1, count):
            total = total + buf[k].astype(F32)
        return joined(total, index)

    if comm:
        round1 = [send(part16.at[lax.rem(gx + k + 1, 8)], rs.at[k], gx_peers[k]) for k in range(7)]
        rs[7] = part16[gx]
        for copy in round1:
            copy.wait()
        xs[xi] = split(summed(rs, 8, gx), gx)
        round2 = [send(xs.at[xi], xs.at[xi], x_peers[k]) for k in range(X_CHIPS - 1)]
        later_halo()
        for copy in round2:
            copy.wait()
        pl.semaphore_wait(ring.at[1], 2)
        zs[zi] = split(summed(xs, X_CHIPS, gx), gx)
        round3 = [send(zs.at[zi], zs.at[zi], z_peers[k]) for k in range(Z_CHIPS - 1)]
        backward(0)
        backward(1)
        backward(2)
        emit()
        for copy in round3:
            copy.wait()
        fin[gx] = split(summed(zs, Z_CHIPS, gx), gx)
        round4 = [send(fin.at[gx], fin.at[gx], gx_peers[k]) for k in range(7)]
        for copy in round4:
            copy.wait()
    else:
        later_halo()
        backward(0)
        backward(1)
        backward(2)
        emit()
        for i in range(8):
            fin[i] = part16[i]


def finish(scale, dx, fin, dx_hbm, df_hbm, db_hbm, df, db, sem):
    out = pltpu.make_async_copy(dx, dx_hbm, sem.at[0])
    out.start()
    swap = one_hot(128, 128, lambda r, q: r == (q // 32) * 32 + (q % 2) * 16 + (q % 32) // 2).astype(BF)
    final = jnp.dot(fin[...].reshape(256, 128), swap, preferred_element_type=F32) * scale
    others = []
    for t in range(27):
        block = final[(t // 4) * 32:(t // 4) * 32 + 32]
        if t % 4:
            block = pltpu.roll(block, 128 - 32 * (t % 4), axis=1)
        k = (t // 9) * 9 + (t % 3) * 3 + (t // 3) % 3
        df[k, pl.ds(0, 16, stride=2), :] = block[0:16, 0:32]
        df[k, pl.ds(1, 16, stride=2), :] = block[16:32, 0:32]
        if t % 9 == 8:
            planes = slice(t - 8, t + 1)
            others.append(pltpu.make_async_copy(df.at[planes], df_hbm.at[planes], sem.at[1 + t // 9]))
            others[-1].start()
    db[...] = pltpu.roll(final[192:200] + final[208:216], 32, axis=1)[0:1, 0:32]
    others.append(pltpu.make_async_copy(db, db_hbm, sem.at[4]))
    others[-1].start()
    for copy in [out] + others:
        copy.wait()


def shards(comm, cells, volume, cotangent, weight, bias):
    vm = pl.BlockSpec(memory_space=pltpu.VMEM)
    hbm = pl.BlockSpec(memory_space=pltpu.MemorySpace.HBM)
    inputs = (volume, cotangent, weight.reshape(27, C, C), bias.reshape(1, C))
    if comm:
        inputs = [pltpu.with_memory_space_constraint(a, pltpu.MemorySpace.HBM) for a in inputs]
    dx, fin = pl.pallas_call(
        functools.partial(kernel, comm),
        out_shape=(jax.ShapeDtypeStruct(volume.shape, BF), jax.ShapeDtypeStruct((8, 32, 128), BF)),
        in_specs=[hbm] * 4,
        out_specs=(vm, vm),
        scratch_shapes=[
            pltpu.VMEM((8, 16, 2048), BF),
            pltpu.VMEM((8, 16, 2048), BF),
            pltpu.VMEM((27, C, C), BF),
            pltpu.VMEM((1, C), F32),
            pltpu.VMEM((12, 320, 128), BF),
            pltpu.VMEM((10, 288, 128), BF),
            pltpu.VMEM((3, 8, 640, 128), BF),
            pltpu.VMEM((6, 576, 128), BF),
            pltpu.VMEM((3, 6, 576, 128), BF),
            pltpu.VMEM((18, 192, 128), BF),
            pltpu.VMEM((18, 192, 128), BF),
            pltpu.VMEM((192, 128), F32),
            pltpu.VMEM((4, 512, 128), BF),
            pltpu.VMEM((8, 32, 128), BF),
            pltpu.VMEM((8, 32, 128), BF),
            pltpu.VMEM((X_CHIPS, 32, 128), BF),
            pltpu.VMEM((Z_CHIPS, 32, 128), BF),
            pltpu.SemaphoreType.DMA((52,)),
            pltpu.SemaphoreType.DMA((52,)),
            pltpu.SemaphoreType.DMA((4,)),
            pltpu.SemaphoreType.REGULAR((2,)),
        ],
        compiler_params=pltpu.CompilerParams(
            collective_id=0 if comm else None, has_side_effects=comm, vmem_limit_bytes=48 << 20),
    )(*inputs)
    dg, df, db = pl.pallas_call(
        functools.partial(finish, 1.0 / math.sqrt(cells)),
        out_shape=(jax.ShapeDtypeStruct(volume.shape, BF),
                   jax.ShapeDtypeStruct((27, C, C), F32),
                   jax.ShapeDtypeStruct((1, C), F32)),
        in_specs=[vm, vm],
        out_specs=[pl.BlockSpec(memory_space=pl.ANY)] * 3,
        scratch_shapes=[pltpu.VMEM((27, C, C), F32), pltpu.VMEM((1, C), F32),
                        pltpu.SemaphoreType.DMA((5,))],
        compiler_params=pltpu.CompilerParams(vmem_limit_bytes=4 << 20),
    )(dx, fin)
    return dg, df.reshape(3, 3, 3, C, C), db.reshape(C)


def solution(mesh):
    cells = 8 * mesh.shape["gx"] * 16 * mesh.shape["gy"] * 64
    in_specs = (P("gx", "gy", None), P("gx", "gy", None), P(), P())
    out_specs = (P("gx", "gy", None), P(), P())
    return jax.shard_map(functools.partial(shards, True, cells), mesh=mesh, in_specs=in_specs,
                         out_specs=out_specs, check_vma=False)
```
